32 devices in a mesh: hyd: 4 (over y, x), src: 8 (over z, core).
Axes of the slice: x: 2, y: 2, z: 4, core: 2. Of those that a mesh axis runs over, the one named last changes fastest.
Arguments:
- record: float32 [2, 4096, 128], P(None, 'hyd'), may hold values from -6 to 6
- tile_data: bfloat16 [4, 8, 24, 2, 128, 128], P('hyd', 'src'), may hold values from -0.125 to 0.125
- tile_rows: int32 [4, 8, 24], P('hyd', 'src'), may hold values from 0 to 7, as said below
- tile_cols: int32 [4, 8, 24], P('hyd', 'src'), may hold values from 0 to 7, as said below
- tile_counts: int32 [4, 8], P('hyd', 'src'), may hold values from 3 to 24, as said below
Outputs:
- solution: float32 [2, 8192, 128], P(None, 'src')
- residual: float32 [2, 4096, 128], P(None, 'hyd')
The draws below stay inside these ranges and needn't reach their ends.
Inputs may be any that keep to these rules, and one draw needn't show every extreme that they name: `tile_rows`: together with tile_cols, the 24 slots of one device name different tile pairs. `tile_cols`: column tiles below 4 belong to the upper layer. `tile_counts`: slots at and beyond a device's count hold no tiles of A.
All inputs are finite; a program needn't handle non-finite values.
Results may differ from the reference program's by a relative error of at most 0.014.
Values may be sent and summed in bfloat16 or wider, within the bound.
No kernel may reach another device: no remote copies, remote signals or barrier semaphores. Data moves between devices by JAX's collectives and lax.ppermute only.
A program may use at most 64 MiB of HBM per device.

```python
import jax
import jax.numpy as jnp
from jax import lax

HYD_DEV = 512
SRC_DEV = 512
NSHOT = 128
TB = 128
TCAP = 24
ITERS = 3
HROWS = 4096
NCOLS = 8192
N_HYD = 4
N_SRC = 8


def tile_places(key):
    row_tiles = 2 * HYD_DEV // TB
    col_tiles = 2 * SRC_DEV // TB
    keys = jax.random.split(jax.random.fold_in(key, 11), N_HYD * N_SRC)
    orders = jax.vmap(lambda one_key: jax.random.permutation(one_key, row_tiles * col_tiles))(keys)
    return (orders[:, :TCAP].reshape(N_HYD, N_SRC, TCAP).astype(jnp.int32), col_tiles)


def draw_tile_rows(key, part):
    places, col_tiles = tile_places(key)
    return (places // col_tiles).astype(jnp.int32)


def draw_tile_cols(key, part):
    places, col_tiles = tile_places(key)
    return (places % col_tiles).astype(jnp.int32)


def draw_tile_counts(key, part):
    devices = N_HYD * N_SRC
    base_key = jax.random.fold_in(key, 23)
    first_key, second_key, third_key = jax.random.split(base_key, 3)
    base_load = jax.random.randint(first_key, (devices,), TCAP // 4, 3 * TCAP // 4 + 1)
    busiest = jax.random.randint(second_key, (), 0, devices)
    lightest = (busiest + 1 + jax.random.randint(third_key, (), 0, devices - 1)) % devices
    base_load = base_load.at[busiest].set(TCAP).at[lightest].set(TCAP // 8)
    return base_load.reshape(N_HYD, N_SRC).astype(jnp.int32)


def shard_levels(rng, shape, shards, least, high):
    def one(axis_at, parts):
        draws = jax.random.uniform(jax.random.fold_in(jax.random.fold_in(rng, 6), axis_at), (parts,), jnp.float32, least / len(shards), high / len(shards))
        return jnp.repeat(jnp.exp(draws), shape[axis_at] // parts).reshape((-1,) + (1,) * (len(shape) - axis_at - 1))

    factor_of = one(*shards[0])
    for cut in shards[1:]:
        factor_of = factor_of * one(*cut)
    return factor_of


def centred(stream_key, shape, deviation, most, pieces=(), dtype=jnp.bfloat16):
    gain = shard_levels(stream_key, shape, pieces, -0.22, 0.18) if pieces else 1.0
    values = jax.random.normal(stream_key, shape, jnp.float32) * deviation * gain
    return jnp.minimum(jnp.maximum(values, -most), most).astype(dtype)


def setup_inputs(seed: int = 0) -> dict:
    streams_of = jax.random.split(jax.random.key(seed), 6)
    return {
        "record": centred(streams_of[0], (2, HROWS, NSHOT), 1.0, 6.0, ((1, 4),), jnp.float32),
        "tile_data": centred(streams_of[1], (N_HYD, N_SRC, TCAP, 2, TB, TB), (TB * N_SRC * 2) ** -0.5, 0.125, ((0, 4), (1, 8))),
        "tile_rows": draw_tile_rows(jax.random.fold_in(streams_of[5], 71), 0),
        "tile_cols": draw_tile_cols(jax.random.fold_in(streams_of[5], 71), 0),
        "tile_counts": draw_tile_counts(jax.random.fold_in(streams_of[5], 71), 0),
    }


EPSILON = 1e-6


def forward_all(tile_data, tile_rows, tile_cols, tile_counts, vector_b):
    row_tiles = 2 * HYD_DEV // TB
    col_tiles = 2 * SRC_DEV // TB
    blocks = vector_b.astype(jnp.float32).reshape(2, N_SRC, col_tiles, TB, NSHOT)

    def one_row(hrow):
        def over_src(scol, total):
            def over_slot(slot, total):
                tile = tile_data[hrow, scol, slot].astype(jnp.float32)
                piece = blocks[:, scol, tile_cols[hrow, scol, slot]]
                real_part = jnp.dot(tile[0], piece[0], preferred_element_type=jnp.float32) - jnp.dot(tile[1], piece[1], preferred_element_type=jnp.float32)
                imag_part = jnp.dot(tile[0], piece[1], preferred_element_type=jnp.float32) + jnp.dot(tile[1], piece[0], preferred_element_type=jnp.float32)
                return total.at[:, tile_rows[hrow, scol, slot]].add(jnp.stack([real_part, imag_part]))
            return lax.fori_loop(0, tile_counts[hrow, scol], over_slot, total)
        return lax.fori_loop(0, N_SRC, over_src, jnp.zeros((2, row_tiles, TB, NSHOT), jnp.float32))

    stacked = lax.map(one_row, jnp.arange(N_HYD))
    return jnp.transpose(stacked, (1, 0, 2, 3, 4)).reshape(2, HROWS, NSHOT)


def adjoint_all(tile_data, tile_rows, tile_cols, tile_counts, residual_b):
    row_tiles = 2 * HYD_DEV // TB
    col_tiles = 2 * SRC_DEV // TB
    blocks = residual_b.astype(jnp.float32).reshape(2, N_HYD, row_tiles, TB, NSHOT)

    def one_column(scol):
        def over_hyd(hrow, total):
            def over_slot(slot, total):
                tile = tile_data[hrow, scol, slot].astype(jnp.float32)
                piece = blocks[:, hrow, tile_rows[hrow, scol, slot]]
                real_part = jnp.dot(tile[0].T, piece[0], preferred_element_type=jnp.float32) + jnp.dot(tile[1].T, piece[1], preferred_element_type=jnp.float32)
                imag_part = jnp.dot(tile[0].T, piece[1], preferred_element_type=jnp.float32) - jnp.dot(tile[1].T, piece[0], preferred_element_type=jnp.float32)
                return total.at[:, tile_cols[hrow, scol, slot]].add(jnp.stack([real_part, imag_part]))
            return lax.fori_loop(0, tile_counts[hrow, scol], over_slot, total)
        return lax.fori_loop(0, N_HYD, over_hyd, jnp.zeros((2, col_tiles, TB, NSHOT), jnp.float32))

    stacked = lax.map(one_column, jnp.arange(N_SRC))
    return jnp.transpose(stacked, (1, 0, 2, 3, 4)).reshape(2, NCOLS, NSHOT)


def reference(record, tile_data, tile_rows, tile_cols, tile_counts):
    residual = record
    gradient = adjoint_all(tile_data, tile_rows, tile_cols, tile_counts, residual.astype(jnp.bfloat16))
    direction = gradient
    solution = jnp.zeros_like(gradient)
    gamma_now = jnp.sum(gradient * gradient, axis=(0, 1))
    for step_index in range(ITERS):
        image = forward_all(tile_data, tile_rows, tile_cols, tile_counts, direction.astype(jnp.bfloat16))
        alpha_step = gamma_now / (jnp.sum(image * image, axis=(0, 1)) + EPSILON)
        solution = solution + alpha_step * direction
        residual = residual - alpha_step * image
        if step_index + 1 < ITERS:
            gradient = adjoint_all(tile_data, tile_rows, tile_cols, tile_counts, residual.astype(jnp.bfloat16))
            gamma_next = jnp.sum(gradient * gradient, axis=(0, 1))
            direction = gradient + (gamma_next / (gamma_now + EPSILON)) * direction
            gamma_now = gamma_next
    return solution, residual
```

```python
import functools

import jax
import jax.numpy as jnp
from jax import lax
from jax.experimental import pallas as pl
from jax.experimental.pallas import tpu as pltpu
from jax.sharding import PartitionSpec as P

SRC_DEV = 512
ITERS = 3
EPSILON = 1e-06
GROUP = 8
TAIL = 16

F32 = jnp.float32
BF16 = jnp.bfloat16


def call(kernel, name, outs, scratch, *ins):
    def space(dtype):
        return pltpu.SMEM if dtype == jnp.int32 else pltpu.VMEM

    return pl.pallas_call(
        kernel,
        name=name,
        out_shape=[jax.ShapeDtypeStruct(s, d) for s, d in outs],
        in_specs=[pl.BlockSpec(memory_space=space(a.dtype)) for a in ins],
        out_specs=[pl.BlockSpec(memory_space=pltpu.VMEM) for _ in outs],
        scratch_shapes=[pltpu.VMEM(s, d) for s, d in scratch],
    )(*ins)


def low_half(shape):
    return lax.broadcasted_iota(jnp.int32, shape, len(shape) - 1) < shape[-1] // 2


def turn(value):
    return pltpu.roll(value, value.shape[-1] // 2, value.ndim - 1)


def times_i(value, sign):
    rolled = turn(value)
    return jnp.where(low_half(value.shape), -sign * rolled, sign * rolled)


def both_parts(row):
    return row + turn(row)


def fold_squares(value):
    return jnp.sum((value * value).reshape(-1, 8, value.shape[-1]), axis=0)


def rows_of_norm(folded):
    row = both_parts(jnp.sum(folded, axis=0, keepdims=True))
    return jnp.broadcast_to(row, (8, folded.shape[-1]))


def norm_tail(norm):
    row = jnp.broadcast_to(norm[:1], (TAIL, norm.shape[-1]))
    high = row.astype(BF16).astype(F32)
    at = lax.broadcasted_iota(jnp.int32, row.shape, 0)
    return jnp.where(at == 0, high, jnp.where(at == 1, row - high, 0.0)).astype(BF16)


def norm_from(tail):
    tail = tail.astype(F32)
    return jnp.broadcast_to(tail[:1] + tail[1:2], (8, tail.shape[-1]))


def spans(size, count):
    return pl.ds(pl.multiple_of(count * size, size), size)


def slots(index_ref, step):
    used = index_ref[2, 0]

    def turn_of(group, carry):
        for lane in range(GROUP):
            slot = group * GROUP + lane
            step(slot, slot < used, index_ref[0, slot], index_ref[1, slot])
        return carry

    lax.fori_loop(0, (used + GROUP - 1) // GROUP, turn_of, 0)


def add_tile(acc_ref, weights, plain_ref, turned_ref, source, target):
    size = weights.shape[0]
    right = jnp.concatenate([plain_ref[spans(size, source), :], turned_ref[spans(size, source), :]], axis=0)
    at = spans(size, target)
    acc_ref[at, :] = acc_ref[at, :] + jnp.dot(weights, right, preferred_element_type=F32)


def put_chunk(chunk, plain_ref, turned_ref, at, sign):
    wide = chunk.astype(F32)
    plain_ref[at, :] = chunk
    turned_ref[at, :] = times_i(wide, sign).astype(BF16)
    return fold_squares(wide)


def pack_kernel(core_axis, tiles, record_ref, tile_ref, index_ref, turned_tile_ref, total_ref, plain_ref, turned_ref):
    core = lax.rem(lax.axis_index(core_axis), 2)
    rows = plain_ref.shape[0]
    for at in range(0, rows, 128):
        real = record_ref[0, pl.ds(at, 128), :]
        imag = record_ref[1, pl.ds(at, 128), :]
        first = jnp.where(core == 0, real, turn(real))
        second = jnp.where(core == 0, turn(imag), imag)
        packed = jnp.where(low_half(real.shape), first, second).astype(BF16)
        put_chunk(packed, plain_ref, turned_ref, pl.ds(at, 128), -1.0)
    total_ref[...] = jnp.zeros_like(total_ref)
    turn_tiles(tiles, tile_ref, index_ref, turned_tile_ref, total_ref, plain_ref, turned_ref)


def turn_tiles(tiles, tile_ref, index_ref, turned_tile_ref, total_ref, plain_ref, turned_ref):
    def step(slot, valid, row, col):
        weights = jnp.concatenate([tile_ref[slot, 0].T, tile_ref[slot, 1].T], axis=1)
        turned_tile_ref[slot] = weights
        add_tile(total_ref, weights, plain_ref, turned_ref, row, jnp.where(valid, col, tiles))

    slots(index_ref, step)


def first_adjoint_kernel(hyd_axis, hyds, tiles, tile_ref, index_ref, own_total_ref, plain_ref, turned_ref, *refs):
    turned_tile_ref, own_ref, sends, total_ref = refs[0], refs[1], refs[2:-1], refs[-1]
    total_ref[...] = jnp.zeros_like(total_ref)
    turn_tiles(tiles, tile_ref, index_ref, turned_tile_ref, total_ref, plain_ref, turned_ref)
    give_columns(hyd_axis, hyds, own_total_ref, total_ref, own_ref, sends, None)


def give_columns(hyd_axis, hyds, first_ref, second_ref, own_ref, sends, tail):
    here = lax.axis_index(hyd_axis)
    part = own_ref.shape[0] // 2
    own_ref[:part, :] = first_ref[spans(part, here), :]
    own_ref[part:, :] = second_ref[spans(part, here), :]
    for offset in range(1, hyds):
        there = here ^ offset
        send = sends[offset - 1]
        send[:part, :] = first_ref[spans(part, there), :].astype(BF16)
        send[part : 2 * part, :] = second_ref[spans(part, there), :].astype(BF16)
        if tail is not None:
            send[2 * part :, :] = tail


def adjoint_kernel(hyd_axis, core_axis, hyds, zs, tiles, *refs):
    tile_a, tile_b, index_a, index_b = refs[:4]
    chunks = refs[4 : 4 + zs]
    plain_ref, own_ref, norm_ref = refs[4 + zs : 7 + zs]
    sends = refs[7 + zs : 6 + zs + hyds]
    turned_ref, first_ref, second_ref = refs[6 + zs + hyds :]
    here = lax.axis_index(core_axis) // 2
    rows = chunks[0].shape[0]
    folded = jnp.zeros((8, plain_ref.shape[-1]), F32)
    for offset in range(zs):
        folded += put_chunk(chunks[offset][...], plain_ref, turned_ref, spans(rows, here ^ offset), -1.0)
    norm = rows_of_norm(folded)
    norm_ref[...] = norm
    for index_ref, tile_ref, total_ref in ((index_a, tile_a, first_ref), (index_b, tile_b, second_ref)):
        total_ref[...] = jnp.zeros_like(total_ref)

        def step(slot, valid, row, col):
            add_tile(total_ref, tile_ref[slot], plain_ref, turned_ref, row, jnp.where(valid, col, tiles))

        slots(index_ref, step)
    give_columns(hyd_axis, hyds, first_ref, second_ref, own_ref, sends, norm_tail(norm))


def forward_kernel(hyd_axis, core_axis, hyds, zs, tiles, *refs):
    tile_a, tile_b, index_a, index_b = refs[:4]
    chunks = refs[4 : 4 + hyds]
    plain_a, plain_b, own_ref, norm_ref = refs[4 + hyds : 8 + hyds]
    sends = refs[8 + hyds : 7 + hyds + zs]
    turned_a, turned_b, total_ref = refs[7 + hyds + zs :]
    here = lax.axis_index(hyd_axis)
    part = chunks[0].shape[0] // 2
    folded = jnp.zeros((8, plain_a.shape[-1]), F32)
    for offset in range(hyds):
        at = spans(part, here ^ offset)
        folded += put_chunk(chunks[offset][:part, :], plain_a, turned_a, at, 1.0)
        folded += put_chunk(chunks[offset][part:, :], plain_b, turned_b, at, 1.0)
    norm = rows_of_norm(folded)
    norm_ref[...] = norm
    total_ref[...] = jnp.zeros_like(total_ref)
    for index_ref, tile_ref, plain_ref, turned_ref in (
        (index_a, tile_a, plain_a, turned_a),
        (index_b, tile_b, plain_b, turned_b),
    ):

        def step(slot, valid, row, col):
            weights = jnp.concatenate([tile_ref[slot, 0], tile_ref[slot, 1]], axis=1)
            add_tile(total_ref, weights, plain_ref, turned_ref, col, jnp.where(valid, row, tiles))

        slots(index_ref, step)
    here = lax.axis_index(core_axis) // 2
    rows = own_ref.shape[0]
    own_ref[...] = total_ref[spans(rows, here), :]
    tail = norm_tail(norm)
    for offset in range(1, zs):
        sends[offset - 1][:rows, :] = total_ref[spans(rows, here ^ offset), :].astype(BF16)
        sends[offset - 1][rows:, :] = tail


def summed(own_ref, others):
    value = own_ref[...]
    for other in others:
        value = value + other[: own_ref.shape[0], :].astype(F32)
    return value


def norm_sum(own_norm, others, size):
    norm = own_norm
    for other in others:
        norm = norm + norm_from(other[size:, :])
    return norm


def start_kernel(others, own_ref, *refs):
    gradient = summed(own_ref, refs[:others])
    refs[-2][...] = gradient
    refs[-1][...] = gradient.astype(BF16)


def image_kernel(others, later, own_ref, norm_ref, *refs):
    ins, refs = refs[:others], refs[others:]
    image = summed(own_ref, ins)
    gamma = norm_sum(norm_ref[...], ins, own_ref.shape[0])
    if later:
        before_ref, gamma_ref = refs[:2]
        beta = gamma / (gamma_ref[...] + EPSILON)
        image = image + beta[:1] * before_ref[...]
        refs = refs[2:]
        refs[3][...] = beta
    refs[0][...] = image
    refs[1][...] = image.astype(BF16)
    refs[2][...] = gamma


def gradient_kernel(others, own_ref, norm_ref, *refs):
    ins, (before_ref, gamma_ref, wide_ref, narrow_ref, alpha_ref) = refs[:others], refs[others:]
    change = summed(own_ref, ins)
    alpha = gamma_ref[...] / (norm_sum(norm_ref[...], ins, own_ref.shape[0]) + EPSILON)
    gradient = before_ref[...] - alpha[:1] * change
    wide_ref[...] = gradient
    narrow_ref[...] = gradient.astype(BF16)
    alpha_ref[...] = alpha


def gather_kernel(core_axis, zs, *refs):
    chunks, (plain_ref, norm_ref) = refs[:zs], refs[zs:]
    here = lax.axis_index(core_axis) // 2
    rows = chunks[0].shape[0]
    folded = jnp.zeros((8, plain_ref.shape[-1]), F32)
    for offset in range(zs):
        chunk = chunks[offset][...]
        plain_ref[spans(rows, here ^ offset), :] = chunk
        folded += fold_squares(chunk.astype(F32))
    norm_ref[...] = rows_of_norm(folded)


def answer_kernel(core_axis, norms, record_ref, gamma_ref, *refs):
    norm = refs[0][...]
    for other in refs[1:norms]:
        norm = norm + other[...]
    refs = refs[norms:]
    alphas = [ref[...] for ref in refs[: ITERS - 1]] + [gamma_ref[...] / (norm + EPSILON)]
    refs = refs[ITERS - 1 :]
    betas = [ref[...] for ref in refs[: ITERS - 1]]
    refs = refs[ITERS - 1 :]
    own_g, pair_g, images = refs[:ITERS], refs[ITERS : 2 * ITERS], refs[2 * ITERS : 3 * ITERS]
    own_x, pair_x, wide_r, narrow_r = refs[3 * ITERS :]
    weights = [None] * ITERS
    weights[-1] = alphas[-1]
    for k in range(ITERS - 2, -1, -1):
        weights[k] = alphas[k] + betas[k] * weights[k + 1]
    core = lax.rem(lax.axis_index(core_axis), 2)
    for at in range(0, own_x.shape[0], 128):
        span = pl.ds(at, 128)
        own_x[span, :] = sum(w[:1] * g[span, :].astype(F32) for w, g in zip(weights, own_g))
        pair_x[span, :] = sum(w[:1] * g[span, :].astype(F32) for w, g in zip(weights, pair_g)).astype(BF16)
    for at in range(0, wide_r.shape[0], 128):
        span = pl.ds(at, 128)
        real, imag = record_ref[0, span, :], record_ref[1, span, :]
        first = jnp.where(core == 0, real, turn(real))
        second = jnp.where(core == 0, turn(imag), imag)
        residual = jnp.where(low_half(real.shape), first, second)
        for alpha, image in zip(alphas, images):
            residual = residual - alpha[:1] * image[span, :].astype(F32)
        wide_r[span, :] = residual
        narrow_r[span, :] = residual.astype(BF16)


def unpack_kernel(core_axis, own_x, own_r, pair_x, pair_r, x_ref, r_ref):
    core = lax.rem(lax.axis_index(core_axis), 2)
    for own, pair, out in ((own_x, pair_x, x_ref), (own_r, pair_r, r_ref)):
        for at in range(0, own.shape[0], 128):
            span = pl.ds(at, 128)
            mine, theirs = own[span, :], pair[span, :].astype(F32)
            first = jnp.where(core == 0, mine, theirs)
            second = jnp.where(core == 0, theirs, mine)
            low = low_half(mine.shape)
            out[0, span, :] = jnp.where(low, first, turn(second))
            out[1, span, :] = jnp.where(low, turn(first), second)


def solution(mesh):
    hyds, srcs = mesh.shape["hyd"], mesh.shape["src"]
    zs = srcs // 2

    def swap(value, axis, size, offset):
        return lax.ppermute(value, axis, [(i, i ^ offset) for i in range(size)])

    def over_hyd(values):
        return [swap(v, "hyd", hyds, o + 1) for o, v in enumerate(values)]

    def over_z(values):
        return [swap(v, "src", srcs, 2 * (o + 1)) for o, v in enumerate(values)]

    def body(record, tile_data, tile_rows, tile_cols, tile_counts):
        own_tiles = tile_data[0, 0]
        slot_count, _, size, _ = own_tiles.shape
        rows, shots = record.shape[1:]
        cols = 2 * SRC_DEV
        row_tiles, col_tiles = rows // size, cols // size
        row_part, col_part = rows // zs, cols // hyds
        norm = ((8, shots), F32)
        row_sends = [((row_part + TAIL, shots), BF16)] * (zs - 1)
        col_sends = [((2 * col_part + TAIL, shots), BF16)] * (hyds - 1)
        row_total, col_total = ((rows + size, shots), F32), ((cols + size, shots), F32)
        vector = lambda n, dtype: ((n, shots), dtype)

        index = jnp.stack([tile_rows[0, 0], tile_cols[0, 0], jnp.broadcast_to(tile_counts[0, 0], (slot_count,))])
        pair_index = swap(index, "src", srcs, 1)
        pair_tiles = swap(own_tiles, "src", srcs, 1)

        turned_shape = ((slot_count, size, 2 * size), BF16)
        turned_own, total, plain, turned = call(
            functools.partial(pack_kernel, "src", col_tiles), "pack",
            [turned_shape, col_total, vector(rows, BF16), vector(rows, BF16)], [],
            record, own_tiles, index,
        )
        turned_pair, own, *sends = call(
            functools.partial(first_adjoint_kernel, "hyd", hyds, col_tiles), "first_adjoint",
            [turned_shape, vector(2 * col_part, F32)] + [vector(2 * col_part, BF16)] * (hyds - 1), [col_total],
            pair_tiles, pair_index, total, plain, turned,
        )
        gradient, narrow = call(
            functools.partial(start_kernel, hyds - 1), "start",
            [vector(2 * col_part, F32), vector(2 * col_part, BF16)], [],
            own, *over_hyd(sends),
        )

        alphas, betas, own_g, pair_g, images = [], [], [], [], []
        image = gamma = None
        for step in range(ITERS):
            plain_a, plain_b, own, own_norm, *sends = call(
                functools.partial(forward_kernel, "hyd", "src", hyds, zs, row_tiles), "forward",
                [vector(cols, BF16), vector(cols, BF16), vector(row_part, F32), norm] + row_sends,
                [vector(cols, BF16), vector(cols, BF16), row_total],
                own_tiles, pair_tiles, index, pair_index, narrow, *over_hyd([narrow] * (hyds - 1)),
            )
            own_g.append(plain_a)
            pair_g.append(plain_b)
            outs = [vector(row_part, F32), vector(row_part, BF16), norm]
            before = [image, gamma] if step else []
            image, narrow, gamma, *beta = call(
                functools.partial(image_kernel, zs - 1, step > 0), "image",
                outs + [norm] * (step > 0), [],
                own, own_norm, *over_z(sends), *before,
            )
            betas += beta
            chunks = [narrow] + over_z([narrow] * (zs - 1))
            if step + 1 == ITERS:
                break
            plain, own, own_norm, *sends = call(
                functools.partial(adjoint_kernel, "hyd", "src", hyds, zs, col_tiles), "adjoint",
                [vector(rows, BF16), vector(2 * col_part, F32), norm] + col_sends,
                [vector(rows, BF16), col_total, col_total],
                turned_own, turned_pair, index, pair_index, *chunks,
            )
            images.append(plain)
            gradient, narrow, alpha = call(
                functools.partial(gradient_kernel, hyds - 1), "gradient",
                [vector(2 * col_part, F32), vector(2 * col_part, BF16), norm], [],
                own, own_norm, *over_hyd(sends), gradient, gamma,
            )
            alphas.append(alpha)

        plain, own_norm = call(functools.partial(gather_kernel, "src", zs), "gather", [vector(rows, BF16), norm], [], *chunks)
        images.append(plain)
        norms = [own_norm] + over_hyd([own_norm] * (hyds - 1))
        own_x, pair_x, wide_r, narrow_r = call(
            functools.partial(answer_kernel, "src", hyds), "answer",
            [vector(cols, F32), vector(cols, BF16), vector(rows, F32), vector(rows, BF16)], [],
            record, gamma, *norms, *alphas, *betas, *own_g, *pair_g, *images,
        )
        return call(
            functools.partial(unpack_kernel, "src"), "unpack",
            [((2, cols, shots), F32), ((2, rows, shots), F32)], [],
            own_x, wide_r, swap(pair_x, "src", srcs, 1), swap(narrow_r, "src", srcs, 1),
        )

    in_specs = (
        P(None, "hyd", None),
        P("hyd", "src", None, None, None, None),
        P("hyd", "src", None),
        P("hyd", "src", None),
        P("hyd", "src"),
    )
    out_specs = (P(None, "src", None), P(None, "hyd", None))
    return jax.shard_map(body, mesh=mesh, in_specs=in_specs, out_specs=out_specs, check_vma=False)
```

```python
import functools

import jax
import jax.numpy as jnp
from jax import lax
from jax.experimental import pallas as pl
from jax.experimental.pallas import tpu as pltpu
from jax.sharding import PartitionSpec as P

SRC_DEV = 512
ITERS = 3
EPSILON = 1e-06
GROUP = 8
TAIL = 16
VMEM_BYTES = 16 << 20

F32 = jnp.float32
BF16 = jnp.bfloat16


def call(kernel, name, outs, scratch, *ins):
    def space(dtype):
        return pltpu.SMEM if dtype == jnp.int32 else pltpu.VMEM

    return pl.pallas_call(
        kernel,
        name=name,
        out_shape=[jax.ShapeDtypeStruct(s, d) for s, d in outs],
        in_specs=[pl.BlockSpec(memory_space=space(a.dtype)) for a in ins],
        out_specs=[pl.BlockSpec(memory_space=pltpu.VMEM) for _ in outs],
        scratch_shapes=[pltpu.VMEM(s, d) for s, d in scratch],
        compiler_params=pltpu.CompilerParams(vmem_limit_bytes=VMEM_BYTES),
    )(*ins)


def low_half(shape):
    return lax.broadcasted_iota(jnp.int32, shape, len(shape) - 1) < shape[-1] // 2


def turn(value):
    return pltpu.roll(value, value.shape[-1] // 2, value.ndim - 1)


def times_i(value, sign):
    rolled = turn(value)
    return jnp.where(low_half(value.shape), -sign * rolled, sign * rolled)


def both_parts(row):
    return row + turn(row)


def fold_squares(value):
    return jnp.sum((value * value).reshape(-1, 8, value.shape[-1]), axis=0)


def rows_of_norm(folded):
    row = both_parts(jnp.sum(folded, axis=0, keepdims=True))
    return jnp.broadcast_to(row, (8, folded.shape[-1]))


def norm_tail(norm):
    row = jnp.broadcast_to(norm[:1], (TAIL, norm.shape[-1]))
    high = row.astype(BF16).astype(F32)
    at = lax.broadcasted_iota(jnp.int32, row.shape, 0)
    return jnp.where(at == 0, high, jnp.where(at == 1, row - high, 0.0)).astype(BF16)


def norm_from(tail):
    tail = tail.astype(F32)
    return jnp.broadcast_to(tail[:1] + tail[1:2], (8, tail.shape[-1]))


def spans(size, count):
    return pl.ds(pl.multiple_of(count * size, size), size)


def slots(index_ref, step):
    used = index_ref[2, 0]

    def turn_of(group, carry):
        for lane in range(GROUP):
            slot = group * GROUP + lane
            step(slot, slot < used, index_ref[0, slot], index_ref[1, slot])
        return carry

    lax.fori_loop(0, (used + GROUP - 1) // GROUP, turn_of, 0)


def add_tile(acc_ref, weights, plain_ref, turned_ref, source, target):
    size = weights.shape[0]
    right = jnp.concatenate([plain_ref[spans(size, source), :], turned_ref[spans(size, source), :]], axis=0)
    at = spans(size, target)
    acc_ref[at, :] = acc_ref[at, :] + jnp.dot(weights, right, preferred_element_type=F32)


def put_chunk(chunk, plain_ref, turned_ref, at, sign):
    wide = chunk.astype(F32)
    plain_ref[at, :] = chunk
    turned_ref[at, :] = times_i(wide, sign).astype(BF16)
    return fold_squares(wide)


def pack_kernel(core_axis, tiles, record_ref, tile_ref, index_ref, turned_tile_ref, total_ref, plain_ref, turned_ref):
    core = lax.rem(lax.axis_index(core_axis), 2)
    rows = plain_ref.shape[0]
    for at in range(0, rows, 128):
        real = record_ref[0, pl.ds(at, 128), :]
        imag = record_ref[1, pl.ds(at, 128), :]
        first = jnp.where(core == 0, real, turn(real))
        second = jnp.where(core == 0, turn(imag), imag)
        packed = jnp.where(low_half(real.shape), first, second).astype(BF16)
        put_chunk(packed, plain_ref, turned_ref, pl.ds(at, 128), -1.0)
    total_ref[...] = jnp.zeros_like(total_ref)
    turn_tiles(tiles, tile_ref, index_ref, turned_tile_ref, total_ref, plain_ref, turned_ref)


def turn_tiles(tiles, tile_ref, index_ref, turned_tile_ref, total_ref, plain_ref, turned_ref):
    def step(slot, valid, row, col):
        weights = jnp.concatenate([tile_ref[slot, 0].T, tile_ref[slot, 1].T], axis=1)
        turned_tile_ref[slot] = weights
        add_tile(total_ref, weights, plain_ref, turned_ref, row, jnp.where(valid, col, tiles))

    slots(index_ref, step)


def first_adjoint_kernel(hyd_axis, hyds, tiles, tile_ref, index_ref, own_total_ref, plain_ref, turned_ref, *refs):
    turned_tile_ref, own_ref, sends, total_ref = refs[0], refs[1], refs[2:-1], refs[-1]
    total_ref[...] = jnp.zeros_like(total_ref)
    turn_tiles(tiles, tile_ref, index_ref, turned_tile_ref, total_ref, plain_ref, turned_ref)
    give_columns(hyd_axis, hyds, own_total_ref, total_ref, own_ref, sends, None)


def give_columns(hyd_axis, hyds, first_ref, second_ref, own_ref, sends, tail):
    here = lax.axis_index(hyd_axis)
    part = own_ref.shape[0] // 2
    own_ref[:part, :] = first_ref[spans(part, here), :]
    own_ref[part:, :] = second_ref[spans(part, here), :]
    for offset in range(1, hyds):
        there = here ^ offset
        send = sends[offset - 1]
        send[:part, :] = first_ref[spans(part, there), :].astype(BF16)
        send[part : 2 * part, :] = second_ref[spans(part, there), :].astype(BF16)
        if tail is not None:
            send[2 * part :, :] = tail


def adjoint_kernel(hyd_axis, core_axis, hyds, zs, tiles, *refs):
    tile_a, tile_b, index_a, index_b = refs[:4]
    chunks = refs[4 : 4 + zs]
    plain_ref, own_ref, norm_ref = refs[4 + zs : 7 + zs]
    sends = refs[7 + zs : 6 + zs + hyds]
    turned_ref, first_ref, second_ref = refs[6 + zs + hyds :]
    here = lax.axis_index(core_axis) // 2
    rows = chunks[0].shape[0]
    folded = jnp.zeros((8, plain_ref.shape[-1]), F32)
    for offset in range(zs):
        folded += put_chunk(chunks[offset][...], plain_ref, turned_ref, spans(rows, here ^ offset), -1.0)
    norm = rows_of_norm(folded)
    norm_ref[...] = norm
    for index_ref, tile_ref, total_ref in ((index_a, tile_a, first_ref), (index_b, tile_b, second_ref)):
        total_ref[...] = jnp.zeros_like(total_ref)

        def step(slot, valid, row, col):
            add_tile(total_ref, tile_ref[slot], plain_ref, turned_ref, row, jnp.where(valid, col, tiles))

        slots(index_ref, step)
    give_columns(hyd_axis, hyds, first_ref, second_ref, own_ref, sends, norm_tail(norm))


def forward_kernel(hyd_axis, core_axis, hyds, zs, tiles, *refs):
    tile_a, tile_b, index_a, index_b = refs[:4]
    chunks = refs[4 : 4 + hyds]
    plain_a, plain_b, own_ref, norm_ref = refs[4 + hyds : 8 + hyds]
    sends = refs[8 + hyds : 7 + hyds + zs]
    turned_a, turned_b, total_ref = refs[7 + hyds + zs :]
    here = lax.axis_index(hyd_axis)
    part = chunks[0].shape[0] // 2
    folded = jnp.zeros((8, plain_a.shape[-1]), F32)
    for offset in range(hyds):
        at = spans(part, here ^ offset)
        folded += put_chunk(chunks[offset][:part, :], plain_a, turned_a, at, 1.0)
        folded += put_chunk(chunks[offset][part:, :], plain_b, turned_b, at, 1.0)
    norm = rows_of_norm(folded)
    norm_ref[...] = norm
    total_ref[...] = jnp.zeros_like(total_ref)
    for index_ref, tile_ref, plain_ref, turned_ref in (
        (index_a, tile_a, plain_a, turned_a),
        (index_b, tile_b, plain_b, turned_b),
    ):

        def step(slot, valid, row, col):
            weights = jnp.concatenate([tile_ref[slot, 0], tile_ref[slot, 1]], axis=1)
            add_tile(total_ref, weights, plain_ref, turned_ref, col, jnp.where(valid, row, tiles))

        slots(index_ref, step)
    here = lax.axis_index(core_axis) // 2
    rows = own_ref.shape[0]
    own_ref[...] = total_ref[spans(rows, here), :]
    tail = norm_tail(norm)
    for offset in range(1, zs):
        sends[offset - 1][:rows, :] = total_ref[spans(rows, here ^ offset), :].astype(BF16)
        sends[offset - 1][rows:, :] = tail


def summed(own_ref, others):
    value = own_ref[...]
    for other in others:
        value = value + other[: own_ref.shape[0], :].astype(F32)
    return value


def norm_sum(own_norm, others, size):
    norm = own_norm
    for other in others:
        norm = norm + norm_from(other[size:, :])
    return norm


def start_kernel(others, own_ref, *refs):
    gradient = summed(own_ref, refs[:others])
    refs[-2][...] = gradient
    refs[-1][...] = gradient.astype(BF16)


def image_kernel(others, later, own_ref, norm_ref, *refs):
    ins, refs = refs[:others], refs[others:]
    image = summed(own_ref, ins)
    gamma = norm_sum(norm_ref[...], ins, own_ref.shape[0])
    if later:
        before_ref, gamma_ref = refs[:2]
        beta = gamma / (gamma_ref[...] + EPSILON)
        image = image + beta[:1] * before_ref[...]
        refs = refs[2:]
        refs[3][...] = beta
    refs[0][...] = image
    refs[1][...] = image.astype(BF16)
    refs[2][...] = gamma


def gradient_kernel(others, own_ref, norm_ref, *refs):
    ins, (before_ref, gamma_ref, wide_ref, narrow_ref, alpha_ref) = refs[:others], refs[others:]
    change = summed(own_ref, ins)
    alpha = gamma_ref[...] / (norm_sum(norm_ref[...], ins, own_ref.shape[0]) + EPSILON)
    gradient = before_ref[...] - alpha[:1] * change
    wide_ref[...] = gradient
    narrow_ref[...] = gradient.astype(BF16)
    alpha_ref[...] = alpha


def gather_kernel(core_axis, zs, *refs):
    chunks, (plain_ref, norm_ref) = refs[:zs], refs[zs:]
    here = lax.axis_index(core_axis) // 2
    rows = chunks[0].shape[0]
    folded = jnp.zeros((8, plain_ref.shape[-1]), F32)
    for offset in range(zs):
        chunk = chunks[offset][...]
        plain_ref[spans(rows, here ^ offset), :] = chunk
        folded += fold_squares(chunk.astype(F32))
    norm_ref[...] = rows_of_norm(folded)


def answer_kernel(core_axis, norms, record_ref, gamma_ref, *refs):
    norm = refs[0][...]
    for other in refs[1:norms]:
        norm = norm + other[...]
    refs = refs[norms:]
    alphas = [ref[...] for ref in refs[: ITERS - 1]] + [gamma_ref[...] / (norm + EPSILON)]
    refs = refs[ITERS - 1 :]
    betas = [ref[...] for ref in refs[: ITERS - 1]]
    refs = refs[ITERS - 1 :]
    own_g, pair_g, images = refs[:ITERS], refs[ITERS : 2 * ITERS], refs[2 * ITERS : 3 * ITERS]
    own_x, pair_x, wide_r, narrow_r = refs[3 * ITERS :]
    weights = [None] * ITERS
    weights[-1] = alphas[-1]
    for k in range(ITERS - 2, -1, -1):
        weights[k] = alphas[k] + betas[k] * weights[k + 1]
    core = lax.rem(lax.axis_index(core_axis), 2)
    for at in range(0, own_x.shape[0], 128):
        span = pl.ds(at, 128)
        own_x[span, :] = sum(w[:1] * g[span, :].astype(F32) for w, g in zip(weights, own_g))
        pair_x[span, :] = sum(w[:1] * g[span, :].astype(F32) for w, g in zip(weights, pair_g)).astype(BF16)
    for at in range(0, wide_r.shape[0], 128):
        span = pl.ds(at, 128)
        real, imag = record_ref[0, span, :], record_ref[1, span, :]
        first = jnp.where(core == 0, real, turn(real))
        second = jnp.where(core == 0, turn(imag), imag)
        residual = jnp.where(low_half(real.shape), first, second)
        for alpha, image in zip(alphas, images):
            residual = residual - alpha[:1] * image[span, :].astype(F32)
        wide_r[span, :] = residual
        narrow_r[span, :] = residual.astype(BF16)


def unpack_kernel(core_axis, own_x, own_r, pair_x, pair_r, x_ref, r_ref):
    core = lax.rem(lax.axis_index(core_axis), 2)
    for own, pair, out in ((own_x, pair_x, x_ref), (own_r, pair_r, r_ref)):
        for at in range(0, own.shape[0], 128):
            span = pl.ds(at, 128)
            mine, theirs = own[span, :], pair[span, :].astype(F32)
            first = jnp.where(core == 0, mine, theirs)
            second = jnp.where(core == 0, theirs, mine)
            low = low_half(mine.shape)
            out[0, span, :] = jnp.where(low, first, turn(second))
            out[1, span, :] = jnp.where(low, turn(first), second)


def solution(mesh):
    hyds, srcs = mesh.shape["hyd"], mesh.shape["src"]
    zs = srcs // 2

    def swap(value, axis, size, offset):
        return lax.ppermute(value, axis, [(i, i ^ offset) for i in range(size)])

    def over_hyd(values):
        return [swap(v, "hyd", hyds, o + 1) for o, v in enumerate(values)]

    def over_z(values):
        return [swap(v, "src", srcs, 2 * (o + 1)) for o, v in enumerate(values)]

    def body(record, tile_data, tile_rows, tile_cols, tile_counts):
        own_tiles = tile_data[0, 0]
        slot_count, _, size, _ = own_tiles.shape
        rows, shots = record.shape[1:]
        cols = 2 * SRC_DEV
        row_tiles, col_tiles = rows // size, cols // size
        row_part, col_part = rows // zs, cols // hyds
        norm = ((8, shots), F32)
        row_sends = [((row_part + TAIL, shots), BF16)] * (zs - 1)
        col_sends = [((2 * col_part + TAIL, shots), BF16)] * (hyds - 1)
        row_total, col_total = ((rows + size, shots), F32), ((cols + size, shots), F32)
        vector = lambda n, dtype: ((n, shots), dtype)

        index = jnp.stack([tile_rows[0, 0], tile_cols[0, 0], jnp.broadcast_to(tile_counts[0, 0], (slot_count,))])
        pair_index = swap(index, "src", srcs, 1)
        pair_tiles = swap(own_tiles, "src", srcs, 1)

        turned_shape = ((slot_count, size, 2 * size), BF16)
        turned_own, total, plain, turned = call(
            functools.partial(pack_kernel, "src", col_tiles), "pack",
            [turned_shape, col_total, vector(rows, BF16), vector(rows, BF16)], [],
            record, own_tiles, index,
        )
        turned_pair, own, *sends = call(
            functools.partial(first_adjoint_kernel, "hyd", hyds, col_tiles), "first_adjoint",
            [turned_shape, vector(2 * col_part, F32)] + [vector(2 * col_part, BF16)] * (hyds - 1), [col_total],
            pair_tiles, pair_index, total, plain, turned,
        )
        gradient, narrow = call(
            functools.partial(start_kernel, hyds - 1), "start",
            [vector(2 * col_part, F32), vector(2 * col_part, BF16)], [],
            own, *over_hyd(sends),
        )

        alphas, betas, own_g, pair_g, images = [], [], [], [], []
        image = gamma = None
        for step in range(ITERS):
            plain_a, plain_b, own, own_norm, *sends = call(
                functools.partial(forward_kernel, "hyd", "src", hyds, zs, row_tiles), "forward",
                [vector(cols, BF16), vector(cols, BF16), vector(row_part, F32), norm] + row_sends,
                [vector(cols, BF16), vector(cols, BF16), row_total],
                own_tiles, pair_tiles, index, pair_index, narrow, *over_hyd([narrow] * (hyds - 1)),
            )
            own_g.append(plain_a)
            pair_g.append(plain_b)
            outs = [vector(row_part, F32), vector(row_part, BF16), norm]
            before = [image, gamma] if step else []
            image, narrow, gamma, *beta = call(
                functools.partial(image_kernel, zs - 1, step > 0), "image",
                outs + [norm] * (step > 0), [],
                own, own_norm, *over_z(sends), *before,
            )
            betas += beta
            chunks = [narrow] + over_z([narrow] * (zs - 1))
            if step + 1 == ITERS:
                break
            plain, own, own_norm, *sends = call(
                functools.partial(adjoint_kernel, "hyd", "src", hyds, zs, col_tiles), "adjoint",
                [vector(rows, BF16), vector(2 * col_part, F32), norm] + col_sends,
                [vector(rows, BF16), col_total, col_total],
                turned_own, turned_pair, index, pair_index, *chunks,
            )
            images.append(plain)
            gradient, narrow, alpha = call(
                functools.partial(gradient_kernel, hyds - 1), "gradient",
                [vector(2 * col_part, F32), vector(2 * col_part, BF16), norm], [],
                own, own_norm, *over_hyd(sends), gradient, gamma,
            )
            alphas.append(alpha)

        plain, own_norm = call(functools.partial(gather_kernel, "src", zs), "gather", [vector(rows, BF16), norm], [], *chunks)
        images.append(plain)
        norms = [own_norm] + over_hyd([own_norm] * (hyds - 1))
        own_x, pair_x, wide_r, narrow_r = call(
            functools.partial(answer_kernel, "src", hyds), "answer",
            [vector(cols, F32), vector(cols, BF16), vector(rows, F32), vector(rows, BF16)], [],
            record, gamma, *norms, *alphas, *betas, *own_g, *pair_g, *images,
        )
        return call(
            functools.partial(unpack_kernel, "src"), "unpack",
            [((2, cols, shots), F32), ((2, rows, shots), F32)], [],
            own_x, wide_r, swap(pair_x, "src", srcs, 1), swap(narrow_r, "src", srcs, 1),
        )

    in_specs = (
        P(None, "hyd", None),
        P("hyd", "src", None, None, None, None),
        P("hyd", "src", None),
        P("hyd", "src", None),
        P("hyd", "src"),
    )
    out_specs = (P(None, "src", None), P(None, "hyd", None))
    return jax.shard_map(body, mesh=mesh, in_specs=in_specs, out_specs=out_specs, check_vma=False)
```

```python
import functools

import jax
import jax.numpy as jnp
from jax import lax
from jax.experimental import pallas as pl
from jax.experimental.pallas import tpu as pltpu
from jax.sharding import PartitionSpec as P

SRC_DEV = 512
ITERS = 3
EPSILON = 1e-06
GROUP = 8
TAIL = 16
VMEM_BYTES = 16 << 20

F32 = jnp.float32
BF16 = jnp.bfloat16


def call(kernel, name, outs, scratch, *ins, away=0):
    def space(place, dtype):
        if place < away:
            return pltpu.HBM
        return pltpu.SMEM if dtype == jnp.int32 else pltpu.VMEM

    def room(shape, dtype):
        if dtype is pltpu.SemaphoreType.DMA:
            return dtype((shape,))
        return (pltpu.SMEM if dtype == jnp.int32 else pltpu.VMEM)(shape, dtype)

    return pl.pallas_call(
        kernel,
        name=name,
        out_shape=[jax.ShapeDtypeStruct(s, d) for s, d in outs],
        in_specs=[pl.BlockSpec(memory_space=space(i, a.dtype)) for i, a in enumerate(ins)],
        out_specs=[pl.BlockSpec(memory_space=pltpu.VMEM) for _ in outs],
        scratch_shapes=[room(s, d) for s, d in scratch],
        compiler_params=pltpu.CompilerParams(vmem_limit_bytes=VMEM_BYTES),
    )(*ins)


def low_half(shape):
    return lax.broadcasted_iota(jnp.int32, shape, len(shape) - 1) < shape[-1] // 2


def turn(value):
    return pltpu.roll(value, value.shape[-1] // 2, value.ndim - 1)


def times_i(value, sign):
    rolled = turn(value)
    return jnp.where(low_half(value.shape), -sign * rolled, sign * rolled)


def both_parts(row):
    return row + turn(row)


def fold_squares(value):
    return jnp.sum((value * value).reshape(-1, 8, value.shape[-1]), axis=0)


def rows_of_norm(folded):
    row = both_parts(jnp.sum(folded, axis=0, keepdims=True))
    return jnp.broadcast_to(row, (8, folded.shape[-1]))


def norm_tail(norm):
    row = jnp.broadcast_to(norm[:1], (TAIL, norm.shape[-1]))
    high = row.astype(BF16).astype(F32)
    at = lax.broadcasted_iota(jnp.int32, row.shape, 0)
    return jnp.where(at == 0, high, jnp.where(at == 1, row - high, 0.0)).astype(BF16)


def norm_from(tail):
    tail = tail.astype(F32)
    return jnp.broadcast_to(tail[:1] + tail[1:2], (8, tail.shape[-1]))


def spans(size, count):
    return pl.ds(pl.multiple_of(count * size, size), size)


def slots(index_ref, step):
    used = index_ref[2, 0]

    def turn_of(group, carry):
        for lane in range(GROUP):
            slot = group * GROUP + lane
            step(slot, slot < used, index_ref[0, slot], index_ref[1, slot])
        return carry

    lax.fori_loop(0, (used + GROUP - 1) // GROUP, turn_of, 0)


def add_tile(acc_ref, weights, plain_ref, turned_ref, source, target):
    size = weights.shape[0]
    right = jnp.concatenate([plain_ref[spans(size, source), :], turned_ref[spans(size, source), :]], axis=0)
    at = spans(size, target)
    acc_ref[at, :] = acc_ref[at, :] + jnp.dot(weights, right, preferred_element_type=F32)


def put_chunk(chunk, plain_ref, turned_ref, at, sign):
    wide = chunk.astype(F32)
    plain_ref[at, :] = chunk
    turned_ref[at, :] = times_i(wide, sign).astype(BF16)
    return fold_squares(wide)


def packed_record(core, real, imag):
    first = jnp.where(core == 0, real, turn(real))
    second = jnp.where(core == 0, turn(imag), imag)
    return jnp.where(low_half(real.shape), first, second)


def pack_kernel(core_axis, tiles, record_ref, tile_ref, index_ref, turned_tile_ref, total_ref, plain_ref, turned_ref):
    core = lax.rem(lax.axis_index(core_axis), 2)
    for at in range(0, plain_ref.shape[0], 128):
        span = pl.ds(at, 128)
        packed = packed_record(core, record_ref[0, span, :], record_ref[1, span, :])
        put_chunk(packed.astype(BF16), plain_ref, turned_ref, span, -1.0)
    total_ref[...] = jnp.zeros_like(total_ref)
    slots(index_ref, turn_step(tiles, tile_ref, turned_tile_ref, total_ref, plain_ref, turned_ref))


def turn_step(tiles, tile_ref, turned_tile_ref, total_ref, plain_ref, turned_ref):
    def step(slot, valid, row, col):
        weights = jnp.concatenate([tile_ref[slot, 0].T, tile_ref[slot, 1].T], axis=1)
        turned_tile_ref[slot] = weights
        add_tile(total_ref, weights, plain_ref, turned_ref, row, jnp.where(valid, col, tiles))

    return step


def first_adjoint_kernel(hyd_axis, order, tiles, tile_ref, index_ref, own_total_ref, plain_ref, turned_ref, *refs):
    turned_tile_ref, own_ref, sends, total_ref = refs[0], refs[1], refs[2:-1], refs[-1]
    total_ref[...] = jnp.zeros_like(total_ref)
    slots(index_ref, turn_step(tiles, tile_ref, turned_tile_ref, total_ref, plain_ref, turned_ref))
    give_columns(hyd_axis, order, own_total_ref, total_ref, own_ref, sends, None)


def give_columns(hyd_axis, order, first_ref, second_ref, own_ref, sends, tail):
    here = lax.axis_index(hyd_axis)
    part = own_ref.shape[0] // 2
    own_ref[:part, :] = first_ref[spans(part, here), :]
    own_ref[part:, :] = second_ref[spans(part, here), :]
    for send, offset in zip(sends, order):
        there = here ^ offset
        send[:part, :] = first_ref[spans(part, there), :].astype(BF16)
        send[part : 2 * part, :] = second_ref[spans(part, there), :].astype(BF16)
        if tail is not None:
            send[2 * part :, :] = tail


def adjoint_kernel(hyd_axis, core_axis, order, z_order, tiles, *refs):
    tile_a, tile_b, index_a, index_b = refs[:4]
    zs, hyds, refs = len(z_order) + 1, len(order) + 1, refs[4:]
    chunks = refs[:zs]
    plain_ref, own_ref, norm_ref = refs[zs : 3 + zs]
    sends = refs[3 + zs : 2 + zs + hyds]
    turned_ref, first_ref, second_ref = refs[2 + zs + hyds :]
    here = lax.axis_index(core_axis) // 2
    rows = chunks[0].shape[0]
    folded = jnp.zeros((8, plain_ref.shape[-1]), F32)
    for chunk, offset in zip(chunks, (0, *z_order)):
        folded += put_chunk(chunk[...], plain_ref, turned_ref, spans(rows, here ^ offset), -1.0)
    norm = rows_of_norm(folded)
    norm_ref[...] = norm
    for index, tile_ref, total_ref in ((index_a, tile_a, first_ref), (index_b, tile_b, second_ref)):
        total_ref[...] = jnp.zeros_like(total_ref)

        def step(slot, valid, row, col):
            add_tile(total_ref, tile_ref[slot], plain_ref, turned_ref, row, jnp.where(valid, col, tiles))

        slots(index, step)
    give_columns(hyd_axis, order, first_ref, second_ref, own_ref, sends, norm_tail(norm))


def forward_kernel(hyd_axis, core_axis, order, z_order, tiles, *refs):
    tile_a, tile_b, index_a, index_b = refs[:4]
    zs, hyds, refs = len(z_order) + 1, len(order) + 1, refs[4:]
    chunks = refs[:hyds]
    plain_a, plain_b, own_ref, norm_ref = refs[hyds : 4 + hyds]
    sends = refs[4 + hyds : 3 + hyds + zs]
    turned_a, turned_b, total_ref = refs[3 + hyds + zs :]
    here = lax.axis_index(hyd_axis)
    part = chunks[0].shape[0] // 2
    folded = jnp.zeros((8, plain_a.shape[-1]), F32)
    for chunk, offset in zip(chunks, (0, *order)):
        at = spans(part, here ^ offset)
        folded += put_chunk(chunk[:part, :], plain_a, turned_a, at, 1.0)
        folded += put_chunk(chunk[part:, :], plain_b, turned_b, at, 1.0)
    norm = rows_of_norm(folded)
    norm_ref[...] = norm
    total_ref[...] = jnp.zeros_like(total_ref)
    for index, tile_ref, plain_ref, turned_ref in (
        (index_a, tile_a, plain_a, turned_a),
        (index_b, tile_b, plain_b, turned_b),
    ):

        def step(slot, valid, row, col):
            weights = jnp.concatenate([tile_ref[slot, 0], tile_ref[slot, 1]], axis=1)
            add_tile(total_ref, weights, plain_ref, turned_ref, col, jnp.where(valid, row, tiles))

        slots(index, step)
    here = lax.axis_index(core_axis) // 2
    rows = own_ref.shape[0]
    own_ref[...] = total_ref[spans(rows, here), :]
    tail = norm_tail(norm)
    for send, offset in zip(sends, z_order):
        send[:rows, :] = total_ref[spans(rows, here ^ offset), :].astype(BF16)
        send[rows:, :] = tail


def summed(own_ref, others):
    value = own_ref[...]
    for other in others:
        value = value + other[: own_ref.shape[0], :].astype(F32)
    return value


def norm_sum(own_norm, others, size):
    norm = own_norm
    for other in others:
        norm = norm + norm_from(other[size:, :])
    return norm


def start_kernel(others, own_ref, *refs):
    gradient = summed(own_ref, refs[:others])
    refs[-2][...] = gradient
    refs[-1][...] = gradient.astype(BF16)


def image_kernel(others, later, last, own_ref, norm_ref, *refs):
    ins, refs = refs[:others], refs[others:]
    image = summed(own_ref, ins)
    gamma = norm_sum(norm_ref[...], ins, own_ref.shape[0])
    if later:
        before_ref, gamma_ref = refs[:2]
        beta = gamma / (gamma_ref[...] + EPSILON)
        image = image + beta[:1] * before_ref[...]
        refs = refs[2:]
        refs[2][...] = beta
    refs[0][...] = image.astype(BF16)
    refs[1][...] = gamma
    if not last:
        refs[-1][...] = image


def gradient_kernel(others, own_ref, norm_ref, *refs):
    ins, (before_ref, gamma_ref, narrow_ref, alpha_ref, *wide) = refs[:others], refs[others:]
    change = summed(own_ref, ins)
    alpha = gamma_ref[...] / (norm_sum(norm_ref[...], ins, own_ref.shape[0]) + EPSILON)
    gradient = before_ref[...] - alpha[:1] * change
    narrow_ref[...] = gradient.astype(BF16)
    alpha_ref[...] = alpha
    for wide_ref in wide:
        wide_ref[...] = gradient


def gather_kernel(core_axis, z_order, *refs):
    chunks, (plain_ref, norm_ref) = refs[:-2], refs[-2:]
    here = lax.axis_index(core_axis) // 2
    rows = chunks[0].shape[0]
    folded = jnp.zeros((8, plain_ref.shape[-1]), F32)
    for chunk, offset in zip(chunks, (0, *z_order)):
        chunk = chunk[...]
        plain_ref[spans(rows, here ^ offset), :] = chunk
        folded += fold_squares(chunk.astype(F32))
    norm_ref[...] = rows_of_norm(folded)


def answer_kernel(core_axis, norms, record_ref, gamma_ref, *refs):
    norm = refs[0][...]
    for other in refs[1:norms]:
        norm = norm + other[...]
    refs = refs[norms:]
    alphas = [ref[...] for ref in refs[: ITERS - 1]] + [gamma_ref[...] / (norm + EPSILON)]
    refs = refs[ITERS - 1 :]
    betas = [ref[...] for ref in refs[: ITERS - 1]]
    refs = refs[ITERS - 1 :]
    own_g, pair_g, images = refs[:ITERS], refs[ITERS : 2 * ITERS], refs[2 * ITERS : 3 * ITERS]
    own_x, pair_x, wide_r, narrow_r = refs[3 * ITERS :]
    weights = [None] * ITERS
    weights[-1] = alphas[-1]
    for k in range(ITERS - 2, -1, -1):
        weights[k] = alphas[k] + betas[k] * weights[k + 1]
    core = lax.rem(lax.axis_index(core_axis), 2)
    for at in range(0, own_x.shape[0], 128):
        span = pl.ds(at, 128)
        own_x[span, :] = sum(w[:1] * g[span, :].astype(F32) for w, g in zip(weights, own_g))
        pair_x[span, :] = sum(w[:1] * g[span, :].astype(F32) for w, g in zip(weights, pair_g)).astype(BF16)
    for at in range(0, wide_r.shape[0], 128):
        span = pl.ds(at, 128)
        residual = packed_record(core, record_ref[0, span, :], record_ref[1, span, :])
        for alpha, image in zip(alphas, images):
            residual = residual - alpha[:1] * image[span, :].astype(F32)
        wide_r[span, :] = residual
        narrow_r[span, :] = residual.astype(BF16)


def unpack_kernel(core_axis, own_x, own_r, pair_x, pair_r, x_ref, r_ref):
    core = lax.rem(lax.axis_index(core_axis), 2)
    for own, pair, out in ((own_x, pair_x, x_ref), (own_r, pair_r, r_ref)):
        for at in range(0, own.shape[0], 128):
            span = pl.ds(at, 128)
            mine, theirs = own[span, :], pair[span, :].astype(F32)
            first = jnp.where(core == 0, mine, theirs)
            second = jnp.where(core == 0, theirs, mine)
            low = low_half(mine.shape)
            out[0, span, :] = jnp.where(low, first, turn(second))
            out[1, span, :] = jnp.where(low, turn(first), second)


def solution(mesh):
    hyds, srcs = mesh.shape["hyd"], mesh.shape["src"]
    zs = srcs // 2

    def swap(value, axis, size, offset):
        return lax.ppermute(value, axis, [(i, i ^ offset) for i in range(size)])

    hyd_order = tuple(range(1, hyds))
    z_order = (zs - 1, *range(1, zs - 1))

    def over_hyd(values, order):
        return [swap(v, "hyd", hyds, o) for v, o in zip(values, order)]

    def over_z(values, order):
        return [swap(v, "src", srcs, 2 * o) for v, o in zip(values, order)]

    hyd_back, z_back = hyd_order[::-1], z_order[::-1]

    def body(record, tile_data, tile_rows, tile_cols, tile_counts):
        own_tiles = tile_data[0, 0]
        slot_count, _, size, _ = own_tiles.shape
        rows, shots = record.shape[1:]
        cols = 2 * SRC_DEV
        row_tiles, col_tiles = rows // size, cols // size
        row_part, col_part = rows // zs, cols // hyds
        norm = ((8, shots), F32)
        row_sends = [((row_part + TAIL, shots), BF16)] * (zs - 1)
        col_sends = [((2 * col_part + TAIL, shots), BF16)] * (hyds - 1)
        row_total, col_total = ((rows + size, shots), F32), ((cols + size, shots), F32)
        vector = lambda n, dtype: ((n, shots), dtype)

        pair_tiles = swap(own_tiles, "src", srcs, 1)
        index = jnp.stack([tile_rows[0, 0], tile_cols[0, 0], jnp.broadcast_to(tile_counts[0, 0], (slot_count,))])
        pair_index = swap(index, "src", srcs, 1)
        turned_shape = ((slot_count, size, 2 * size), BF16)
        turned_own, total, plain, turned = call(
            functools.partial(pack_kernel, "src", col_tiles), "pack",
            [turned_shape, col_total, vector(rows, BF16), vector(rows, BF16)],
            [],
            record, own_tiles, index,
        )
        turned_pair, own, *sends = call(
            functools.partial(first_adjoint_kernel, "hyd", hyd_order, col_tiles), "first_adjoint",
            [turned_shape, vector(2 * col_part, F32)] + [vector(2 * col_part, BF16)] * (hyds - 1), [col_total],
            pair_tiles, pair_index, total, plain, turned,
        )
        gradient, narrow = call(
            functools.partial(start_kernel, hyds - 1), "start",
            [vector(2 * col_part, F32), vector(2 * col_part, BF16)], [],
            own, *over_hyd(sends, hyd_order),
        )

        alphas, betas, own_g, pair_g, images = [], [], [], [], []
        image = gamma = None
        for step in range(ITERS):
            last = step + 1 == ITERS
            plain_a, plain_b, own, own_norm, *sends = call(
                functools.partial(forward_kernel, "hyd", "src", hyd_back, z_order, row_tiles), "forward",
                [vector(cols, BF16), vector(cols, BF16), vector(row_part, F32), norm] + row_sends,
                [vector(cols, BF16), vector(cols, BF16), row_total],
                own_tiles, pair_tiles, index, pair_index, narrow, *over_hyd([narrow] * (hyds - 1), hyd_back),
            )
            own_g.append(plain_a)
            pair_g.append(plain_b)
            narrow, gamma, *more = call(
                functools.partial(image_kernel, zs - 1, step > 0, last), "image",
                [vector(row_part, BF16), norm] + [norm] * (step > 0) + [vector(row_part, F32)] * (not last), [],
                own, own_norm, *over_z(sends, z_order), *([image, gamma] if step else []),
            )
            image = None if last else more.pop()
            betas += more
            chunks = [narrow] + over_z([narrow] * (zs - 1), z_back)
            if last:
                break
            plain, own, own_norm, *sends = call(
                functools.partial(adjoint_kernel, "hyd", "src", hyd_order, z_back, col_tiles), "adjoint",
                [vector(rows, BF16), vector(2 * col_part, F32), norm] + col_sends,
                [vector(rows, BF16), col_total, col_total],
                turned_own, turned_pair, index, pair_index, *chunks,
            )
            images.append(plain)
            more_steps = step + 2 < ITERS
            narrow, alpha, *wide = call(
                functools.partial(gradient_kernel, hyds - 1), "gradient",
                [vector(2 * col_part, BF16), norm] + [vector(2 * col_part, F32)] * more_steps, [],
                own, own_norm, *over_hyd(sends, hyd_order), gradient, gamma,
            )
            gradient = wide[0] if more_steps else None
            alphas.append(alpha)

        plain, own_norm = call(functools.partial(gather_kernel, "src", z_back), "gather", [vector(rows, BF16), norm], [], *chunks)
        images.append(plain)
        norms = [own_norm] + over_hyd([own_norm] * (hyds - 1), hyd_back)
        own_x, pair_x, wide_r, narrow_r = call(
            functools.partial(answer_kernel, "src", hyds), "answer",
            [vector(cols, F32), vector(cols, BF16), vector(rows, F32), vector(rows, BF16)], [],
            record, gamma, *norms, *alphas, *betas, *own_g, *pair_g, *images,
        )
        return call(
            functools.partial(unpack_kernel, "src"), "unpack",
            [((2, cols, shots), F32), ((2, rows, shots), F32)], [],
            own_x, wide_r, swap(pair_x, "src", srcs, 1), swap(narrow_r, "src", srcs, 1),
        )

    in_specs = (
        P(None, "hyd", None),
        P("hyd", "src", None, None, None, None),
        P("hyd", "src", None),
        P("hyd", "src", None),
        P("hyd", "src"),
    )
    out_specs = (P(None, "src", None), P(None, "hyd", None))
    return jax.shard_map(body, mesh=mesh, in_specs=in_specs, out_specs=out_specs, check_vma=False)
```

```python
import functools
from typing import NamedTuple

import jax
import jax.numpy as jnp
from jax import lax
from jax.experimental import pallas as pl
from jax.experimental.pallas import tpu as pltpu
from jax.sharding import PartitionSpec as P

SRC_DEV = 512
ITERS = 3
EPSILON = 1e-06
GROUP = 8
TAIL = 16
VMEM_BYTES = 16 << 20

F32 = jnp.float32
BF16 = jnp.bfloat16
F32_INDEX = jnp.int32


class Way(NamedTuple):
    source: int
    sign: float
    size: int
    part: int
    halves: int
    length: int
    target_part: int
    target_begins: tuple
    target_shift: int
    spare: int
    send_order: tuple
    source_place: object
    target_place: object
    weights: object


def call(kernel, name, outs, scratch, *ins, vector=False, alias=None):
    def space(dtype):
        return pltpu.SMEM if dtype == jnp.int32 and not vector else pltpu.VMEM

    return pl.pallas_call(
        kernel,
        name=name,
        out_shape=[jax.ShapeDtypeStruct(s, d) for s, d in outs],
        in_specs=[pl.BlockSpec(memory_space=space(a.dtype)) for a in ins],
        out_specs=[pl.BlockSpec(memory_space=pltpu.VMEM) for _ in outs],
        scratch_shapes=[pltpu.VMEM(s, d) for s, d in scratch],
        input_output_aliases=alias or {},
        compiler_params=pltpu.CompilerParams(vmem_limit_bytes=VMEM_BYTES),
    )(*ins)


def low_half(shape):
    return lax.broadcasted_iota(jnp.int32, shape, len(shape) - 1) < shape[-1] // 2


def turn(value):
    return pltpu.roll(value, value.shape[-1] // 2, value.ndim - 1)


def times_i(value, sign):
    rolled = turn(value)
    return jnp.where(low_half(value.shape), -sign * rolled, sign * rolled)


def both_parts(row):
    return row + turn(row)


def fold_squares(value):
    return jnp.sum((value * value).reshape(-1, 8, value.shape[-1]), axis=0)


def rows_of_norm(folded):
    row = both_parts(jnp.sum(folded, axis=0, keepdims=True))
    return jnp.broadcast_to(row, (8, folded.shape[-1]))


def norm_tail(norm):
    row = jnp.broadcast_to(norm[:1], (TAIL, norm.shape[-1]))
    high = row.astype(BF16).astype(F32)
    at = lax.broadcasted_iota(jnp.int32, row.shape, 0)
    return jnp.where(at == 0, high, jnp.where(at == 1, row - high, 0.0)).astype(BF16)


def norm_from(tail):
    tail = tail.astype(F32)
    return jnp.broadcast_to(tail[:1] + tail[1:2], (8, tail.shape[-1]))


def spans(size, count):
    return pl.ds(pl.multiple_of(count * size, size), size)


def slots(index_ref, step):
    used = index_ref[2, 0]

    def turn_of(group, carry):
        for lane in range(GROUP):
            slot = group * GROUP + lane
            step(slot, slot < used, index_ref[0, slot], index_ref[1, slot])
        return carry

    lax.fori_loop(0, (used + GROUP - 1) // GROUP, turn_of, 0)


def add_tile(acc_ref, weights, plain_ref, turned_ref, source, target):
    size = weights.shape[0]
    right = jnp.concatenate([plain_ref[spans(size, source), :], turned_ref[spans(size, source), :]], axis=0)
    at = spans(size, target)
    acc_ref[at, :] = acc_ref[at, :] + jnp.dot(weights, right, preferred_element_type=F32)


def put_chunk(chunk, plain_ref, turned_ref, at, sign):
    wide = chunk.astype(F32)
    plain_ref[at, :] = chunk
    turned_ref[at, :] = times_i(wide, sign).astype(BF16)
    return fold_squares(wide)


def packed_record(core, real, imag):
    first = jnp.where(core == 0, real, turn(real))
    second = jnp.where(core == 0, turn(imag), imag)
    return jnp.where(low_half(real.shape), first, second)


def pack_kernel(core_axis, tiles, record_ref, tile_ref, index_ref, turned_tile_ref, total_ref, plain_ref, turned_ref):
    core = lax.rem(lax.axis_index(core_axis), 2)
    for at in range(0, plain_ref.shape[0], 128):
        span = pl.ds(at, 128)
        packed = packed_record(core, record_ref[0, span, :], record_ref[1, span, :])
        put_chunk(packed.astype(BF16), plain_ref, turned_ref, span, -1.0)
    total_ref[...] = jnp.zeros_like(total_ref)
    slots(index_ref, turn_step(tiles, tile_ref, turned_tile_ref, total_ref, plain_ref, turned_ref))


def turn_step(tiles, tile_ref, turned_tile_ref, total_ref, plain_ref, turned_ref):
    def step(slot, valid, row, col):
        weights = jnp.concatenate([tile_ref[slot, 0].T, tile_ref[slot, 1].T], axis=1)
        turned_tile_ref[slot] = weights
        add_tile(total_ref, weights, plain_ref, turned_ref, row, jnp.where(valid, col, tiles))

    return step


def first_adjoint_kernel(hyd_axis, order, tiles, tile_ref, index_ref, own_total_ref, plain_ref, turned_ref, *refs):
    turned_tile_ref, own_ref, sends, total_ref = refs[0], refs[1], refs[2:-1], refs[-1]
    total_ref[...] = jnp.zeros_like(total_ref)
    slots(index_ref, turn_step(tiles, tile_ref, turned_tile_ref, total_ref, plain_ref, turned_ref))
    give_columns(hyd_axis, order, own_total_ref, total_ref, own_ref, sends, None)


def give_columns(hyd_axis, order, first_ref, second_ref, own_ref, sends, tail):
    here = lax.axis_index(hyd_axis)
    part = own_ref.shape[0] // 2
    own_ref[:part, :] = first_ref[spans(part, here), :]
    own_ref[part:, :] = second_ref[spans(part, here), :]
    for send, offset in zip(sends, order):
        there = here ^ offset
        send[:part, :] = first_ref[spans(part, there), :].astype(BF16)
        send[part : 2 * part, :] = second_ref[spans(part, there), :].astype(BF16)
        if tail is not None:
            send[2 * part :, :] = tail


def list_kernel(keys, index_a, index_b, *lists):
    slot_count = index_a.shape[1]
    down = lax.broadcasted_iota(F32_INDEX, (slot_count, slot_count), 0)
    along = lax.broadcasted_iota(F32_INDEX, (slot_count, slot_count), 1)
    for list_ref, (row, width, buckets) in zip(lists, keys):
        down_f, wide = down.astype(F32), lax.broadcasted_iota(F32_INDEX, (slot_count, list_ref.shape[1]), 1).astype(F32)
        slot_f = lax.broadcasted_iota(F32_INDEX, wide.shape, 0).astype(F32)
        for k, index_ref in enumerate((index_a, index_b)):
            bucket = index_ref[row : row + 1, :] // width
            used = along[:1, :] < index_ref[2:3, :]
            key = jnp.broadcast_to(jnp.where(used, bucket, buckets).astype(F32), down.shape)
            order_along = key * slot_count + along.astype(F32)
            here = down == along
            key_down = jnp.sum(jnp.where(here, key, 0.0), axis=1, keepdims=True)
            order_down = key_down * slot_count + down_f[:, :1]
            rank = jnp.sum(jnp.where(order_along < order_down, 1.0, 0.0), axis=1, keepdims=True)
            order = jnp.sum(jnp.where(rank == wide, slot_f, 0.0), axis=0, keepdims=True)
            begin = jnp.sum(jnp.where(key_down < wide, 1.0, 0.0), axis=0, keepdims=True)
            list_ref[k : k + 1, :] = order.astype(jnp.int32)
            list_ref[k + 2 : k + 3, :] = begin.astype(jnp.int32)


def step_kernel(way, pick, first, last, *refs):
    (tile_a, tile_b, index_a, index_b, list_ref), refs = refs[:5], refs[5:]
    chunks, refs = refs[: len(pick)], refs[len(pick) :]
    if not first:
        folded, refs = refs[1][...], refs[2:]
    total_ref, refs = refs[0], refs[1:]
    here, there = way.source_place(), way.target_place()
    single = len(pick) == 1
    if first:
        total_ref[...] = jnp.zeros_like(total_ref)
        folded = jnp.zeros((8, total_ref.shape[-1]), F32)
    if single:
        turned_ref, plain_ref = refs[-1], chunks[0]
        wide = plain_ref[...].astype(F32)
        turned_ref[...] = times_i(wide, way.sign).astype(BF16)
        folded += fold_squares(wide)
    else:
        plain_ref, turned_ref = refs[-2:]
        for chunk, offset in zip(chunks, pick):
            for half in range(way.halves):
                at = pl.ds(pl.multiple_of((here ^ offset) * way.part + half * way.length, way.part), way.part)
                folded += put_chunk(chunk[half * way.part : (half + 1) * way.part, :], plain_ref, turned_ref, at, way.sign)
    place = here ^ pick[0]
    base = place * (way.part // way.size) if single else 0
    stride = plain_ref.shape[0] // way.halves
    width = 4 if single else GROUP
    for k, (tile_ref, index_ref) in enumerate(((tile_a, index_a), (tile_b, index_b))):
        low = list_ref[k + 2, place] if single else 0
        high = list_ref[k + 2, place + 1] if single else index_ref[2, 0]

        def turn_of(group, carry):
            for lane in range(width):
                at = low + group * width + lane
                valid = at < high
                slot = list_ref[k, at] if single else at
                source = jnp.where(valid, index_ref[way.source, slot] - base, 0)
                target = jnp.where(valid, index_ref[1 - way.source, slot] + k * way.target_shift, way.spare)
                start = pl.multiple_of(source * way.size + k * (way.halves - 1) * stride, way.size)
                span = pl.ds(start, way.size)
                right = jnp.concatenate([plain_ref[span, :], turned_ref[span, :]], axis=0)
                goal = spans(way.size, target)
                product = jnp.dot(way.weights(tile_ref, slot), right, preferred_element_type=F32)
                total_ref[goal, :] = total_ref[goal, :] + product
            return carry

        lax.fori_loop(0, (high - low + width - 1) // width, turn_of, 0)
    if not last:
        refs[0][...] = folded
        return
    own_ref, norm_ref, sends = refs[0], refs[1], refs[2 : 2 + len(way.send_order)]
    norm = rows_of_norm(folded)
    norm_ref[...] = norm
    tail = norm_tail(norm)
    part = way.target_part
    for j, begin in enumerate(way.target_begins):
        def piece(position):
            return total_ref[pl.ds(pl.multiple_of(position * part + begin, part), part), :]

        own_ref[j * part : (j + 1) * part, :] = piece(there)
        for send, offset in zip(sends, way.send_order):
            send[j * part : (j + 1) * part, :] = piece(there ^ offset).astype(BF16)
    for send in sends:
        send[len(way.target_begins) * part :, :] = tail


def summed(own_ref, others):
    value = own_ref[...]
    for other in others:
        value = value + other[: own_ref.shape[0], :].astype(F32)
    return value


def norm_sum(own_norm, others, size):
    norm = own_norm
    for other in others:
        norm = norm + norm_from(other[size:, :])
    return norm


def start_kernel(others, own_ref, *refs):
    gradient = summed(own_ref, refs[:others])
    refs[-2][...] = gradient
    refs[-1][...] = gradient.astype(BF16)


def image_kernel(others, later, last, own_ref, norm_ref, *refs):
    ins, refs = refs[:others], refs[others:]
    image = summed(own_ref, ins)
    gamma = norm_sum(norm_ref[...], ins, own_ref.shape[0])
    if later:
        before_ref, gamma_ref = refs[:2]
        beta = gamma / (gamma_ref[...] + EPSILON)
        image = image + beta[:1] * before_ref[...]
        refs = refs[2:]
        refs[2][...] = beta
    refs[0][...] = image.astype(BF16)
    refs[1][...] = gamma
    if not last:
        refs[-1][...] = image


def gradient_kernel(others, own_ref, norm_ref, *refs):
    ins, (before_ref, gamma_ref, narrow_ref, alpha_ref, *wide) = refs[:others], refs[others:]
    change = summed(own_ref, ins)
    alpha = gamma_ref[...] / (norm_sum(norm_ref[...], ins, own_ref.shape[0]) + EPSILON)
    gradient = before_ref[...] - alpha[:1] * change
    narrow_ref[...] = gradient.astype(BF16)
    alpha_ref[...] = alpha
    for wide_ref in wide:
        wide_ref[...] = gradient


def norm_kernel(*refs):
    folded = sum(fold_squares(chunk[...].astype(F32)) for chunk in refs[:-1])
    refs[-1][...] = rows_of_norm(folded)


def answer_kernel(hyd_axis, core_axis, g_order, image_order, record_ref, gamma_ref, *refs):
    norms = len(g_order)
    norm = refs[0][...]
    for other in refs[1:norms]:
        norm = norm + other[...]
    refs = refs[norms:]
    alphas = [ref[...] for ref in refs[: ITERS - 1]] + [gamma_ref[...] / (norm + EPSILON)]
    refs = refs[ITERS - 1 :]
    betas = [ref[...] for ref in refs[: ITERS - 1]]
    refs = refs[ITERS - 1 :]
    g_count, image_count = ITERS * len(g_order), ITERS * len(image_order)
    g_chunks, images, (own_x, pair_x, wide_r, narrow_r) = refs[:g_count], refs[g_count : g_count + image_count], refs[g_count + image_count :]
    weights = [None] * ITERS
    weights[-1] = alphas[-1]
    for k in range(ITERS - 2, -1, -1):
        weights[k] = alphas[k] + betas[k] * weights[k + 1]
    core = lax.rem(lax.axis_index(core_axis), 2)
    here = lax.axis_index(hyd_axis)
    for at, offset in enumerate(g_order):
        mine = g_chunks[at :: len(g_order)]
        part = mine[0].shape[0] // 2
        span = spans(part, here ^ offset)
        own_x[span, :] = sum(w[:1] * g[:part, :].astype(F32) for w, g in zip(weights, mine))
        pair_x[span, :] = sum(w[:1] * g[part:, :].astype(F32) for w, g in zip(weights, mine)).astype(BF16)
    here = lax.axis_index(core_axis) // 2
    for at, offset in enumerate(image_order):
        mine = images[at :: len(image_order)]
        span = spans(mine[0].shape[0], here ^ offset)
        residual = packed_record(core, record_ref[0, span, :], record_ref[1, span, :])
        for alpha, image in zip(alphas, mine):
            residual = residual - alpha[:1] * image[...].astype(F32)
        wide_r[span, :] = residual
        narrow_r[span, :] = residual.astype(BF16)


def unpack_kernel(core_axis, own_x, own_r, pair_x, pair_r, x_ref, r_ref):
    core = lax.rem(lax.axis_index(core_axis), 2)
    for own, pair, out in ((own_x, pair_x, x_ref), (own_r, pair_r, r_ref)):
        for at in range(0, own.shape[0], 128):
            span = pl.ds(at, 128)
            mine, theirs = own[span, :], pair[span, :].astype(F32)
            first = jnp.where(core == 0, mine, theirs)
            second = jnp.where(core == 0, theirs, mine)
            low = low_half(mine.shape)
            out[0, span, :] = jnp.where(low, first, turn(second))
            out[1, span, :] = jnp.where(low, turn(first), second)


def solution(mesh):
    hyds, srcs = mesh.shape["hyd"], mesh.shape["src"]
    zs = srcs // 2

    def swap(value, axis, size, offset):
        return lax.ppermute(value, axis, [(i, i ^ offset) for i in range(size)])

    hyd_order = tuple(range(1, hyds))
    z_order = (zs - 1, *range(1, zs - 1))

    def over_hyd(values, order):
        return [swap(v, "hyd", hyds, o) for v, o in zip(values, order)]

    def over_z(values, order):
        return [swap(v, "src", srcs, 2 * o) for v, o in zip(values, order)]

    hyd_back, z_back = hyd_order[::-1], z_order[::-1]

    def body(record, tile_data, tile_rows, tile_cols, tile_counts):
        own_tiles = tile_data[0, 0]
        slot_count, _, size, _ = own_tiles.shape
        rows, shots = record.shape[1:]
        cols = 2 * SRC_DEV
        row_tiles, col_tiles = rows // size, cols // size
        row_part, col_part = rows // zs, cols // hyds
        norm = ((8, shots), F32)
        row_sends = [((row_part + TAIL, shots), BF16)] * (zs - 1)
        col_sends = [((2 * col_part + TAIL, shots), BF16)] * (hyds - 1)
        col_total = ((cols + size, shots), F32)
        vector = lambda n, dtype: ((n, shots), dtype)

        pair_tiles = swap(own_tiles, "src", srcs, 1)
        index = jnp.stack([tile_rows[0, 0], tile_cols[0, 0], jnp.broadcast_to(tile_counts[0, 0], (slot_count,))])
        pair_index = swap(index, "src", srcs, 1)
        turned_shape = ((slot_count, size, 2 * size), BF16)
        turned_own, total, plain, turned = call(
            functools.partial(pack_kernel, "src", col_tiles), "pack",
            [turned_shape, col_total, vector(rows, BF16), vector(rows, BF16)],
            [],
            record, own_tiles, index,
        )
        turned_pair, own, *sends = call(
            functools.partial(first_adjoint_kernel, "hyd", hyd_order, col_tiles), "first_adjoint",
            [turned_shape, vector(2 * col_part, F32)] + [vector(2 * col_part, BF16)] * (hyds - 1), [col_total],
            pair_tiles, pair_index, total, plain, turned,
        )
        gradient, narrow = call(
            functools.partial(start_kernel, hyds - 1), "start",
            [vector(2 * col_part, F32), vector(2 * col_part, BF16)], [],
            own, *over_hyd(sends, hyd_order),
        )

        hyd_place = lambda: lax.axis_index("hyd")
        z_place = lambda: lax.axis_index("src") // 2
        flat = lambda tile_ref, slot: jnp.concatenate([tile_ref[slot, 0], tile_ref[slot, 1]], axis=1)
        forward = Way(1, 1.0, size, col_part, 2, cols, row_part, (0,), 0, row_tiles, z_order, hyd_place, z_place, flat)
        adjoint = Way(
            0, -1.0, size, row_part, 1, rows, col_part, (0, cols), col_tiles, 2 * col_tiles, hyd_order,
            z_place, hyd_place, lambda tile_ref, slot: tile_ref[slot],
        )
        lists = call(
            functools.partial(list_kernel, [(w.source, max(w.part // size, 1), w.length // w.part) for w in (forward, adjoint)]),
            "lists", [((8, 128), jnp.int32)] * 2, [], index, pair_index, vector=True,
        )

        def apply(way, name, tiles, slot_list, chunks, order, outs):
            picks = [(k,) for k in range(len(order))] if way.part % size == 0 else [tuple(range(len(order)))]
            total = (((len(way.target_begins) * (way.spare // len(way.target_begins)) + 1) * size, shots), F32)
            carry = []
            for at, pick in enumerate(picks):
                last = at + 1 == len(picks)
                length = sum(chunks[k].shape[0] for k in pick)
                carry = call(
                    functools.partial(step_kernel, way, tuple(order[k] for k in pick), at == 0, last), name,
                    [total] + (outs if last else [norm]),
                    [vector(length, BF16)] * (1 if len(pick) == 1 else 2),
                    *tiles, index, pair_index, slot_list, *(chunks[k] for k in pick), *carry,
                    alias={6: 0} if at else None,
                )
            return carry[1:]

        alphas, betas, g_chunks, images = [], [], [], []
        image = gamma = None
        g_order, image_order = (0, *hyd_back), (0, *z_back)
        for step in range(ITERS):
            last = step + 1 == ITERS
            chunks = [narrow, *over_hyd([narrow] * (hyds - 1), hyd_back)]
            g_chunks += chunks
            own, own_norm, *sends = apply(
                forward, "forward", (own_tiles, pair_tiles), lists[0], chunks, g_order, [vector(row_part, F32), norm] + row_sends
            )
            narrow, gamma, *more = call(
                functools.partial(image_kernel, zs - 1, step > 0, last), "image",
                [vector(row_part, BF16), norm] + [norm] * (step > 0) + [vector(row_part, F32)] * (not last), [],
                own, own_norm, *over_z(sends, z_order), *([image, gamma] if step else []),
            )
            image = None if last else more.pop()
            betas += more
            chunks = [narrow, *over_z([narrow] * (zs - 1), z_back)]
            images += chunks
            if last:
                break
            own, own_norm, *sends = apply(
                adjoint, "adjoint", (turned_own, turned_pair), lists[1], chunks, image_order, [vector(2 * col_part, F32), norm] + col_sends
            )
            more_steps = step + 2 < ITERS
            narrow, alpha, *wide = call(
                functools.partial(gradient_kernel, hyds - 1), "gradient",
                [vector(2 * col_part, BF16), norm] + [vector(2 * col_part, F32)] * more_steps, [],
                own, own_norm, *over_hyd(sends, hyd_order), gradient, gamma,
            )
            gradient = wide[0] if more_steps else None
            alphas.append(alpha)

        (own_norm,) = call(norm_kernel, "norm", [norm], [], *chunks)
        norms = [own_norm] + over_hyd([own_norm] * (hyds - 1), hyd_back)
        own_x, pair_x, wide_r, narrow_r = call(
            functools.partial(answer_kernel, "hyd", "src", g_order, image_order), "answer",
            [vector(cols, F32), vector(cols, BF16), vector(rows, F32), vector(rows, BF16)], [],
            record, gamma, *norms, *alphas, *betas, *g_chunks, *images,
        )
        return call(
            functools.partial(unpack_kernel, "src"), "unpack",
            [((2, cols, shots), F32), ((2, rows, shots), F32)], [],
            own_x, wide_r, swap(pair_x, "src", srcs, 1), swap(narrow_r, "src", srcs, 1),
        )

    in_specs = (
        P(None, "hyd", None),
        P("hyd", "src", None, None, None, None),
        P("hyd", "src", None),
        P("hyd", "src", None),
        P("hyd", "src"),
    )
    out_specs = (P(None, "src", None), P(None, "hyd", None))
    return jax.shard_map(body, mesh=mesh, in_specs=in_specs, out_specs=out_specs, check_vma=False)
```

```python
import functools
from typing import NamedTuple

import jax
import jax.numpy as jnp
from jax import lax
from jax.experimental import pallas as pl
from jax.experimental.pallas import tpu as pltpu
from jax.sharding import PartitionSpec as P

SRC_DEV = 512
ITERS = 3
EPSILON = 1e-06
GROUP = 8
TAIL = 16
VMEM_BYTES = 16 << 20

F32 = jnp.float32
BF16 = jnp.bfloat16


class Way(NamedTuple):
    source: int
    sign: float
    size: int
    part: int
    halves: int
    length: int
    target_part: int
    target_begins: tuple
    target_shift: int
    spare: int
    send_order: tuple
    source_place: object
    target_place: object
    weights: object


def call(kernel, name, outs, scratch, *ins, vector=False, alias=None):
    def space(dtype):
        return pltpu.SMEM if dtype == jnp.int32 and not vector else pltpu.VMEM

    return pl.pallas_call(
        kernel,
        name=name,
        out_shape=[jax.ShapeDtypeStruct(s, d) for s, d in outs],
        in_specs=[pl.BlockSpec(memory_space=space(a.dtype)) for a in ins],
        out_specs=[pl.BlockSpec(memory_space=pltpu.VMEM) for _ in outs],
        scratch_shapes=[pltpu.VMEM(s, d) for s, d in scratch],
        input_output_aliases=alias or {},
        compiler_params=pltpu.CompilerParams(vmem_limit_bytes=VMEM_BYTES),
    )(*ins)


def low_half(shape):
    return lax.broadcasted_iota(jnp.int32, shape, len(shape) - 1) < shape[-1] // 2


def turn(value):
    return pltpu.roll(value, value.shape[-1] // 2, value.ndim - 1)


def times_i(value, sign):
    rolled = turn(value)
    return jnp.where(low_half(value.shape), -sign * rolled, sign * rolled)


def both_parts(row):
    return row + turn(row)


def fold_squares(value):
    return jnp.sum((value * value).reshape(-1, 8, value.shape[-1]), axis=0)


def rows_of_norm(folded):
    row = both_parts(jnp.sum(folded, axis=0, keepdims=True))
    return jnp.broadcast_to(row, (8, folded.shape[-1]))


def norm_tail(norm):
    row = jnp.broadcast_to(norm[:1], (TAIL, norm.shape[-1]))
    high = row.astype(BF16).astype(F32)
    at = lax.broadcasted_iota(jnp.int32, row.shape, 0)
    return jnp.where(at == 0, high, jnp.where(at == 1, row - high, 0.0)).astype(BF16)


def norm_from(tail):
    tail = tail.astype(F32)
    return jnp.broadcast_to(tail[:1] + tail[1:2], (8, tail.shape[-1]))


def spans(size, count):
    return pl.ds(pl.multiple_of(count * size, size), size)


def slots(index_ref, step):
    used = index_ref[2, 0]

    def turn_of(group, carry):
        for lane in range(GROUP):
            slot = group * GROUP + lane
            step(slot, slot < used, index_ref[0, slot], index_ref[1, slot])
        return carry

    lax.fori_loop(0, (used + GROUP - 1) // GROUP, turn_of, 0)


def add_tile(acc_ref, weights, plain_ref, turned_ref, source, target):
    size = weights.shape[0]
    right = jnp.concatenate([plain_ref[spans(size, source), :], turned_ref[spans(size, source), :]], axis=0)
    at = spans(size, target)
    acc_ref[at, :] = acc_ref[at, :] + jnp.dot(weights, right, preferred_element_type=F32)


def put_chunk(chunk, plain_ref, turned_ref, at, sign):
    wide = chunk.astype(F32)
    plain_ref[at, :] = chunk
    turned_ref[at, :] = times_i(wide, sign).astype(BF16)
    return fold_squares(wide)


def packed_record(core, real, imag):
    first = jnp.where(core == 0, real, turn(real))
    second = jnp.where(core == 0, turn(imag), imag)
    return jnp.where(low_half(real.shape), first, second)


def pack_kernel(core_axis, tiles, record_ref, tile_ref, index_ref, turned_tile_ref, total_ref, plain_ref, turned_ref):
    core = lax.rem(lax.axis_index(core_axis), 2)
    for at in range(0, plain_ref.shape[0], 128):
        span = pl.ds(at, 128)
        packed = packed_record(core, record_ref[0, span, :], record_ref[1, span, :])
        put_chunk(packed.astype(BF16), plain_ref, turned_ref, span, -1.0)
    total_ref[...] = jnp.zeros_like(total_ref)
    slots(index_ref, turn_step(tiles, tile_ref, turned_tile_ref, total_ref, plain_ref, turned_ref))


def turn_step(tiles, tile_ref, turned_tile_ref, total_ref, plain_ref, turned_ref):
    def step(slot, valid, row, col):
        weights = jnp.concatenate([tile_ref[slot, 0].T, tile_ref[slot, 1].T], axis=1)
        turned_tile_ref[slot] = weights
        add_tile(total_ref, weights, plain_ref, turned_ref, row, jnp.where(valid, col, tiles))

    return step


def first_adjoint_kernel(hyd_axis, order, tiles, tile_ref, index_ref, own_total_ref, plain_ref, turned_ref, *refs):
    turned_tile_ref, own_ref, sends, total_ref = refs[0], refs[1], refs[2:-1], refs[-1]
    total_ref[...] = jnp.zeros_like(total_ref)
    slots(index_ref, turn_step(tiles, tile_ref, turned_tile_ref, total_ref, plain_ref, turned_ref))
    give_columns(hyd_axis, order, own_total_ref, total_ref, own_ref, sends, None)


def give_columns(hyd_axis, order, first_ref, second_ref, own_ref, sends, tail):
    here = lax.axis_index(hyd_axis)
    part = own_ref.shape[0] // 2
    own_ref[:part, :] = first_ref[spans(part, here), :]
    own_ref[part:, :] = second_ref[spans(part, here), :]
    for send, offset in zip(sends, order):
        there = here ^ offset
        send[:part, :] = first_ref[spans(part, there), :].astype(BF16)
        send[part : 2 * part, :] = second_ref[spans(part, there), :].astype(BF16)
        if tail is not None:
            send[2 * part :, :] = tail


def list_kernel(plans, index_a, index_b, *lists):
    slot_count = index_a.shape[1]
    square = (slot_count, slot_count)
    down, along = (lax.broadcasted_iota(jnp.int32, square, k) for k in (0, 1))
    down_f, along_f, here = down.astype(F32), along.astype(F32), down == along
    for list_ref, (way, groups) in zip(lists, plans):
        wide = lax.broadcasted_iota(jnp.int32, (slot_count, list_ref.shape[1]), 1).astype(F32)
        slot_f = lax.broadcasted_iota(jnp.int32, wide.shape, 0).astype(F32)
        place = way.source_place()
        for k, index_ref in enumerate((index_a, index_b)):
            offset = (index_ref[way.source : way.source + 1, :] * way.size // way.part) ^ place
            bucket = jnp.zeros(offset.shape, F32)
            for at, group in enumerate(groups):
                for member in group:
                    bucket = jnp.where(offset == member, float(at), bucket)
            bucket = jnp.where(along[:1, :] < index_ref[2:3, :], bucket, float(len(groups)))
            key = jnp.broadcast_to(bucket, square)
            order_along = key * slot_count + along_f
            key_down = jnp.sum(jnp.where(here, key, 0.0), axis=1, keepdims=True)
            order_down = key_down * slot_count + down_f[:, :1]
            rank = jnp.sum(jnp.where(order_along < order_down, 1.0, 0.0), axis=1, keepdims=True)
            order = jnp.sum(jnp.where(rank == wide, slot_f, 0.0), axis=0, keepdims=True)
            begin = jnp.sum(jnp.where(key_down < wide, 1.0, 0.0), axis=0, keepdims=True)
            list_ref[k : k + 1, :] = order.astype(jnp.int32)
            list_ref[k + 2 : k + 3, :] = begin.astype(jnp.int32)


def step_kernel(way, pick, at_group, last, *refs):
    (tile_a, tile_b, index_a, index_b, list_ref), refs = refs[:5], refs[5:]
    chunks, refs = refs[: len(pick)], refs[len(pick) :]
    if at_group:
        folded, refs = refs[1][...], refs[2:]
    total_ref, refs = refs[0], refs[1:]
    here, there = way.source_place(), way.target_place()
    if not at_group:
        total_ref[...] = jnp.zeros_like(total_ref)
        folded = jnp.zeros((8, total_ref.shape[-1]), F32)
    plain_ref, turned_ref = refs[-2:]
    for chunk, offset in zip(chunks, pick):
        for half in range(way.halves):
            at = pl.ds(pl.multiple_of((here ^ offset) * way.part + half * way.length, way.part), way.part)
            folded += put_chunk(chunk[half * way.part : (half + 1) * way.part, :], plain_ref, turned_ref, at, way.sign)
    for k, (tile_ref, index_ref) in enumerate(((tile_a, index_a), (tile_b, index_b))):
        low, high = list_ref[k + 2, at_group], list_ref[k + 2, at_group + 1]

        def turn_of(group, carry):
            for lane in range(GROUP):
                at = low + group * GROUP + lane
                slot = list_ref[k, at]
                source = index_ref[way.source, slot]
                target = jnp.where(at < high, index_ref[1 - way.source, slot] + k * way.target_shift, way.spare)
                span = pl.ds(pl.multiple_of(source * way.size + k * (way.halves - 1) * way.length, way.size), way.size)
                right = jnp.concatenate([plain_ref[span, :], turned_ref[span, :]], axis=0)
                goal = spans(way.size, target)
                product = jnp.dot(way.weights(tile_ref, slot), right, preferred_element_type=F32)
                total_ref[goal, :] = total_ref[goal, :] + product
            return carry

        lax.fori_loop(0, (high - low + GROUP - 1) // GROUP, turn_of, 0)
    if not last:
        refs[0][...] = folded
        return
    own_ref, norm_ref, sends = refs[0], refs[1], refs[2 : 2 + len(way.send_order)]
    norm = rows_of_norm(folded)
    norm_ref[...] = norm
    tail = norm_tail(norm)
    part = way.target_part
    for j, begin in enumerate(way.target_begins):
        def piece(position):
            return total_ref[pl.ds(pl.multiple_of(position * part + begin, part), part), :]

        own_ref[j * part : (j + 1) * part, :] = piece(there)
        for send, offset in zip(sends, way.send_order):
            send[j * part : (j + 1) * part, :] = piece(there ^ offset).astype(BF16)
    for send in sends:
        send[len(way.target_begins) * part :, :] = tail


def summed(own_ref, others):
    value = own_ref[...]
    for other in others:
        value = value + other[: own_ref.shape[0], :].astype(F32)
    return value


def norm_sum(own_norm, others, size):
    norm = own_norm
    for other in others:
        norm = norm + norm_from(other[size:, :])
    return norm


def start_kernel(others, own_ref, *refs):
    gradient = summed(own_ref, refs[:others])
    refs[-2][...] = gradient
    refs[-1][...] = gradient.astype(BF16)


def image_kernel(others, later, last, own_ref, norm_ref, *refs):
    ins, refs = refs[:others], refs[others:]
    image = summed(own_ref, ins)
    gamma = norm_sum(norm_ref[...], ins, own_ref.shape[0])
    if later:
        before_ref, gamma_ref = refs[:2]
        beta = gamma / (gamma_ref[...] + EPSILON)
        image = image + beta[:1] * before_ref[...]
        refs = refs[2:]
        refs[2][...] = beta
    refs[0][...] = image.astype(BF16)
    refs[1][...] = gamma
    if not last:
        refs[-1][...] = image


def gradient_kernel(others, own_ref, norm_ref, *refs):
    ins, (before_ref, gamma_ref, narrow_ref, alpha_ref, *wide) = refs[:others], refs[others:]
    change = summed(own_ref, ins)
    alpha = gamma_ref[...] / (norm_sum(norm_ref[...], ins, own_ref.shape[0]) + EPSILON)
    gradient = before_ref[...] - alpha[:1] * change
    narrow_ref[...] = gradient.astype(BF16)
    alpha_ref[...] = alpha
    for wide_ref in wide:
        wide_ref[...] = gradient


def norm_kernel(*refs):
    folded = sum(fold_squares(chunk[...].astype(F32)) for chunk in refs[:-1])
    refs[-1][...] = rows_of_norm(folded)


def answer_kernel(hyd_axis, core_axis, g_order, image_order, record_ref, gamma_ref, *refs):
    norms = len(g_order)
    norm = refs[0][...]
    for other in refs[1:norms]:
        norm = norm + other[...]
    refs = refs[norms:]
    alphas = [ref[...] for ref in refs[: ITERS - 1]] + [gamma_ref[...] / (norm + EPSILON)]
    refs = refs[ITERS - 1 :]
    betas = [ref[...] for ref in refs[: ITERS - 1]]
    refs = refs[ITERS - 1 :]
    g_count, image_count = ITERS * len(g_order), ITERS * len(image_order)
    g_chunks, images, (own_x, pair_x, wide_r, narrow_r) = refs[:g_count], refs[g_count : g_count + image_count], refs[g_count + image_count :]
    weights = [None] * ITERS
    weights[-1] = alphas[-1]
    for k in range(ITERS - 2, -1, -1):
        weights[k] = alphas[k] + betas[k] * weights[k + 1]
    core = lax.rem(lax.axis_index(core_axis), 2)
    here = lax.axis_index(hyd_axis)
    for at, offset in enumerate(g_order):
        mine = g_chunks[at :: len(g_order)]
        part = mine[0].shape[0] // 2
        span = spans(part, here ^ offset)
        own_x[span, :] = sum(w[:1] * g[:part, :].astype(F32) for w, g in zip(weights, mine))
        pair_x[span, :] = sum(w[:1] * g[part:, :].astype(F32) for w, g in zip(weights, mine)).astype(BF16)
    here = lax.axis_index(core_axis) // 2
    for at, offset in enumerate(image_order):
        mine = images[at :: len(image_order)]
        span = spans(mine[0].shape[0], here ^ offset)
        residual = packed_record(core, record_ref[0, span, :], record_ref[1, span, :])
        for alpha, image in zip(alphas, mine):
            residual = residual - alpha[:1] * image[...].astype(F32)
        wide_r[span, :] = residual
        narrow_r[span, :] = residual.astype(BF16)


def unpack_kernel(core_axis, own_x, own_r, pair_x, pair_r, x_ref, r_ref):
    core = lax.rem(lax.axis_index(core_axis), 2)
    for own, pair, out in ((own_x, pair_x, x_ref), (own_r, pair_r, r_ref)):
        for at in range(0, own.shape[0], 128):
            span = pl.ds(at, 128)
            mine, theirs = own[span, :], pair[span, :].astype(F32)
            first = jnp.where(core == 0, mine, theirs)
            second = jnp.where(core == 0, theirs, mine)
            low = low_half(mine.shape)
            out[0, span, :] = jnp.where(low, first, turn(second))
            out[1, span, :] = jnp.where(low, turn(first), second)


def solution(mesh):
    hyds, srcs = mesh.shape["hyd"], mesh.shape["src"]
    zs = srcs // 2

    def swap(value, axis, size, offset):
        return lax.ppermute(value, axis, [(i, i ^ offset) for i in range(size)])

    hyd_order = tuple(range(1, hyds))
    z_order = (zs - 1, *range(1, zs - 1))

    def over_hyd(values, order):
        return [swap(v, "hyd", hyds, o) for v, o in zip(values, order)]

    def over_z(values, order):
        return [swap(v, "src", srcs, 2 * o) for v, o in zip(values, order)]

    def groups_of(order, way):
        half = len(order) // 2
        return (order[:half], order[half:]) if way.part % way.size == 0 else (order,)

    def body(record, tile_data, tile_rows, tile_cols, tile_counts):
        own_tiles = tile_data[0, 0]
        slot_count, _, size, _ = own_tiles.shape
        rows, shots = record.shape[1:]
        cols = 2 * SRC_DEV
        row_tiles, col_tiles = rows // size, cols // size
        row_part, col_part = rows // zs, cols // hyds
        norm = ((8, shots), F32)
        row_sends = [((row_part + TAIL, shots), BF16)] * (zs - 1)
        col_sends = [((2 * col_part + TAIL, shots), BF16)] * (hyds - 1)
        col_total = ((cols + size, shots), F32)
        vector = lambda n, dtype: ((n, shots), dtype)

        pair_tiles = swap(own_tiles, "src", srcs, 1)
        index = jnp.stack([tile_rows[0, 0], tile_cols[0, 0], jnp.broadcast_to(tile_counts[0, 0], (slot_count,))])
        pair_index = swap(index, "src", srcs, 1)
        turned_shape = ((slot_count, size, 2 * size), BF16)
        turned_own, total, plain, turned = call(
            functools.partial(pack_kernel, "src", col_tiles), "pack",
            [turned_shape, col_total, vector(rows, BF16), vector(rows, BF16)],
            [],
            record, own_tiles, index,
        )
        turned_pair, own, *sends = call(
            functools.partial(first_adjoint_kernel, "hyd", hyd_order, col_tiles), "first_adjoint",
            [turned_shape, vector(2 * col_part, F32)] + [vector(2 * col_part, BF16)] * (hyds - 1), [col_total],
            pair_tiles, pair_index, total, plain, turned,
        )
        gradient, narrow = call(
            functools.partial(start_kernel, hyds - 1), "start",
            [vector(2 * col_part, F32), vector(2 * col_part, BF16)], [],
            own, *over_hyd(sends, hyd_order),
        )

        hyd_place = lambda: lax.axis_index("hyd")
        z_place = lambda: lax.axis_index("src") // 2
        flat = lambda tile_ref, slot: jnp.concatenate([tile_ref[slot, 0], tile_ref[slot, 1]], axis=1)
        forward = Way(1, 1.0, size, col_part, 2, cols, row_part, (0,), 0, row_tiles, z_order, hyd_place, z_place, flat)
        adjoint = Way(
            0, -1.0, size, row_part, 1, rows, col_part, (0, cols), col_tiles, 2 * col_tiles, hyd_order,
            z_place, hyd_place, lambda tile_ref, slot: tile_ref[slot],
        )
        g_order, image_order = ((0, *o[: len(o) // 2], *o[len(o) // 2 :][::-1]) for o in (hyd_order, z_order))
        g_groups, image_groups = (groups_of(order, w) for order, w in ((g_order, forward), (image_order, adjoint)))
        lists = call(
            functools.partial(list_kernel, ((forward, g_groups), (adjoint, image_groups))),
            "lists", [((8, 128), jnp.int32)] * 2, [], index, pair_index, vector=True,
        )

        def apply(way, name, tiles, slot_list, chunks, groups, outs):
            total = (((len(way.target_begins) * (way.spare // len(way.target_begins)) + 1) * size, shots), F32)
            carry, at = [], 0
            for k, group in enumerate(groups):
                last = k + 1 == len(groups)
                carry = call(
                    functools.partial(step_kernel, way, group, k, last), name,
                    [total] + (outs if last else [norm]), [vector(way.halves * way.length, BF16)] * 2,
                    *tiles, index, pair_index, slot_list, *chunks[at : at + len(group)], *carry,
                    alias={5 + len(group): 0} if k else None,
                )
                at += len(group)
            return carry[1:]

        alphas, betas, g_chunks, images = [], [], [], []
        image = gamma = None
        for step in range(ITERS):
            last = step + 1 == ITERS
            chunks = [narrow, *over_hyd([narrow] * (hyds - 1), g_order[1:])]
            g_chunks += chunks
            own, own_norm, *sends = apply(
                forward, "forward", (own_tiles, pair_tiles), lists[0], chunks, g_groups, [vector(row_part, F32), norm] + row_sends
            )
            narrow, gamma, *more = call(
                functools.partial(image_kernel, zs - 1, step > 0, last), "image",
                [vector(row_part, BF16), norm] + [norm] * (step > 0) + [vector(row_part, F32)] * (not last), [],
                own, own_norm, *over_z(sends, z_order), *([image, gamma] if step else []),
            )
            image = None if last else more.pop()
            betas += more
            if last:
                issued = z_order[::-1]
                arrived = dict(zip(issued, over_z([narrow] * (zs - 1), issued)))
                chunks = [narrow, *(arrived[o] for o in image_order[1:])]
            else:
                chunks = [narrow, *over_z([narrow] * (zs - 1), image_order[1:])]
            images += chunks
            if last:
                break
            own, own_norm, *sends = apply(
                adjoint, "adjoint", (turned_own, turned_pair), lists[1], chunks, image_groups, [vector(2 * col_part, F32), norm] + col_sends
            )
            more_steps = step + 2 < ITERS
            narrow, alpha, *wide = call(
                functools.partial(gradient_kernel, hyds - 1), "gradient",
                [vector(2 * col_part, BF16), norm] + [vector(2 * col_part, F32)] * more_steps, [],
                own, own_norm, *over_hyd(sends, hyd_order), gradient, gamma,
            )
            gradient = wide[0] if more_steps else None
            alphas.append(alpha)

        (own_norm,) = call(norm_kernel, "norm", [norm], [], *chunks)
        norms = [own_norm] + over_hyd([own_norm] * (hyds - 1), hyd_order[::-1])
        own_x, pair_x, wide_r, narrow_r = call(
            functools.partial(answer_kernel, "hyd", "src", g_order, image_order), "answer",
            [vector(cols, F32), vector(cols, BF16), vector(rows, F32), vector(rows, BF16)], [],
            record, gamma, *norms, *alphas, *betas, *g_chunks, *images,
        )
        return call(
            functools.partial(unpack_kernel, "src"), "unpack",
            [((2, cols, shots), F32), ((2, rows, shots), F32)], [],
            own_x, wide_r, swap(pair_x, "src", srcs, 1), swap(narrow_r, "src", srcs, 1),
        )

    in_specs = (
        P(None, "hyd", None),
        P("hyd", "src", None, None, None, None),
        P("hyd", "src", None),
        P("hyd", "src", None),
        P("hyd", "src"),
    )
    out_specs = (P(None, "src", None), P(None, "hyd", None))
    return jax.shard_map(body, mesh=mesh, in_specs=in_specs, out_specs=out_specs, check_vma=False)
```

```python
import functools
from typing import NamedTuple

import jax
import jax.numpy as jnp
from jax import lax
from jax.experimental import pallas as pl
from jax.experimental.pallas import tpu as pltpu
from jax.sharding import PartitionSpec as P

SRC_DEV = 512
ITERS = 3
EPSILON = 1e-06
GROUP = 8
TAIL = 16
VMEM_BYTES = 16 << 20

F32 = jnp.float32
BF16 = jnp.bfloat16


class Way(NamedTuple):
    source: int
    sign: float
    size: int
    part: int
    halves: int
    length: int
    target_part: int
    target_begins: tuple
    target_shift: int
    spare: int
    send_order: tuple
    source_place: object
    target_place: object
    weights: object


def call(kernel, name, outs, scratch, *ins, vector=False, alias=None, away=0):
    def space(place, dtype):
        if place < away:
            return pltpu.HBM
        return pltpu.SMEM if dtype == jnp.int32 and not vector else pltpu.VMEM

    def room(shape, dtype):
        if dtype is pltpu.SemaphoreType.DMA:
            return dtype((shape,))
        return (pltpu.SMEM if dtype == jnp.int32 else pltpu.VMEM)(shape, dtype)

    return pl.pallas_call(
        kernel,
        name=name,
        out_shape=[jax.ShapeDtypeStruct(s, d) for s, d in outs],
        in_specs=[pl.BlockSpec(memory_space=space(i, a.dtype)) for i, a in enumerate(ins)],
        out_specs=[pl.BlockSpec(memory_space=pltpu.VMEM) for _ in outs],
        scratch_shapes=[room(s, d) for s, d in scratch],
        input_output_aliases=alias or {},
        compiler_params=pltpu.CompilerParams(vmem_limit_bytes=VMEM_BYTES),
    )(*[pltpu.with_memory_space_constraint(a, pltpu.HBM) if i < away else a for i, a in enumerate(ins)])


def low_half(shape):
    return lax.broadcasted_iota(jnp.int32, shape, len(shape) - 1) < shape[-1] // 2


def turn(value):
    return pltpu.roll(value, value.shape[-1] // 2, value.ndim - 1)


def times_i(value, sign):
    rolled = turn(value)
    return jnp.where(low_half(value.shape), -sign * rolled, sign * rolled)


def both_parts(row):
    return row + turn(row)


def fold_squares(value):
    return jnp.sum((value * value).reshape(-1, 8, value.shape[-1]), axis=0)


def rows_of_norm(folded):
    row = both_parts(jnp.sum(folded, axis=0, keepdims=True))
    return jnp.broadcast_to(row, (8, folded.shape[-1]))


def norm_tail(norm):
    row = jnp.broadcast_to(norm[:1], (TAIL, norm.shape[-1]))
    high = row.astype(BF16).astype(F32)
    at = lax.broadcasted_iota(jnp.int32, row.shape, 0)
    return jnp.where(at == 0, high, jnp.where(at == 1, row - high, 0.0)).astype(BF16)


def norm_from(tail):
    tail = tail.astype(F32)
    return jnp.broadcast_to(tail[:1] + tail[1:2], (8, tail.shape[-1]))


def spans(size, count):
    return pl.ds(pl.multiple_of(count * size, size), size)


def group_of(index, group, step):
    for lane in range(GROUP):
        slot = group * GROUP + lane
        step(slot, slot < index[2][0], index[0][slot], index[1][slot])


def slots(index, step):
    def turn_of(group, carry):
        group_of(index, group, step)
        return carry

    lax.fori_loop(0, (index[2][0] + GROUP - 1) // GROUP, turn_of, 0)


def add_tile(acc_ref, weights, plain_ref, turned_ref, source, target):
    size = weights.shape[0]
    right = jnp.concatenate([plain_ref[spans(size, source), :], turned_ref[spans(size, source), :]], axis=0)
    at = spans(size, target)
    acc_ref[at, :] = acc_ref[at, :] + jnp.dot(weights, right, preferred_element_type=F32)


def put_chunk(chunk, plain_ref, turned_ref, at, sign):
    wide = chunk.astype(F32)
    plain_ref[at, :] = chunk
    turned_ref[at, :] = times_i(wide, sign).astype(BF16)
    return fold_squares(wide)


def packed_record(core, real, imag):
    first = jnp.where(core == 0, real, turn(real))
    second = jnp.where(core == 0, turn(imag), imag)
    return jnp.where(low_half(real.shape), first, second)


def pack_kernel(core_axis, tiles, record_hbm, tile_hbm, row_hbm, col_hbm, used_ref, *refs):
    turned_tile_ref, total_ref, plain_ref, turned_ref, record_ref, tile_ref, row_ref, col_ref, record_sem, tile_sem, index_sem = refs
    core = lax.rem(lax.axis_index(core_axis), 2)
    rows, slot_count = plain_ref.shape[0], tile_ref.shape[0]
    pieces = record_sem.shape[0]
    piece, groups = rows // pieces, slot_count // GROUP

    def record_copy(k):
        span = pl.ds(k * piece, piece)
        return pltpu.make_async_copy(record_hbm.at[:, span, :], record_ref.at[:, span, :], record_sem.at[k])

    def tile_copy(k):
        span = pl.ds(k * GROUP, GROUP)
        return pltpu.make_async_copy(tile_hbm.at[span], tile_ref.at[span], tile_sem.at[k])

    index_copies = [
        pltpu.make_async_copy(source, target, index_sem.at[k])
        for k, (source, target) in enumerate(((row_hbm, row_ref), (col_hbm, col_ref)))
    ]
    for k in range(pieces):
        record_copy(k).start()
    for copy in index_copies:
        copy.start()
    for k in range(groups):
        tile_copy(k).start()
    total_ref[...] = jnp.zeros_like(total_ref)
    for k in range(pieces):
        record_copy(k).wait()
        span = pl.ds(k * piece, piece)
        packed = packed_record(core, record_ref[0, span, :], record_ref[1, span, :])
        put_chunk(packed.astype(BF16), plain_ref, turned_ref, span, -1.0)
    for copy in index_copies:
        copy.wait()
    step = turn_step(tiles, tile_ref, turned_tile_ref, total_ref, plain_ref, turned_ref)
    for k in range(groups):
        tile_copy(k).wait()

        @pl.when(k * GROUP < used_ref[0, 0])
        def _():
            group_of((row_ref.at[0], col_ref.at[0], used_ref.at[0]), k, step)


def turn_step(tiles, tile_ref, turned_tile_ref, total_ref, plain_ref, turned_ref):
    def step(slot, valid, row, col):
        weights = jnp.concatenate([tile_ref[slot, 0].T, tile_ref[slot, 1].T], axis=1)
        turned_tile_ref[slot] = weights
        add_tile(total_ref, weights, plain_ref, turned_ref, row, jnp.where(valid, col, tiles))

    return step


def first_adjoint_kernel(hyd_axis, order, tiles, tile_ref, row_ref, col_ref, used_ref, own_total_ref, plain_ref, turned_ref, *refs):
    turned_tile_ref, own_ref, sends, total_ref = refs[0], refs[1], refs[2:-1], refs[-1]
    total_ref[...] = jnp.zeros_like(total_ref)
    slots((row_ref.at[0], col_ref.at[0], used_ref.at[0]), turn_step(tiles, tile_ref, turned_tile_ref, total_ref, plain_ref, turned_ref))
    give_columns(hyd_axis, order, own_total_ref, total_ref, own_ref, sends, None)


def give_columns(hyd_axis, order, first_ref, second_ref, own_ref, sends, tail):
    here = lax.axis_index(hyd_axis)
    part = own_ref.shape[0] // 2
    own_ref[:part, :] = first_ref[spans(part, here), :]
    own_ref[part:, :] = second_ref[spans(part, here), :]
    for send, offset in zip(sends, order):
        there = here ^ offset
        send[:part, :] = first_ref[spans(part, there), :].astype(BF16)
        send[part : 2 * part, :] = second_ref[spans(part, there), :].astype(BF16)
        if tail is not None:
            send[2 * part :, :] = tail


def list_kernel(plans, *refs):
    indices, lists = (refs[:3], refs[3:6]), refs[6:]
    slot_count = refs[0].shape[1]
    square = (slot_count, slot_count)
    down, along = (lax.broadcasted_iota(jnp.int32, square, k) for k in (0, 1))
    down_f, along_f, here = down.astype(F32), along.astype(F32), down == along
    for list_ref, (way, groups) in zip(lists, plans):
        wide = lax.broadcasted_iota(jnp.int32, (slot_count, list_ref.shape[1]), 1).astype(F32)
        slot_f = lax.broadcasted_iota(jnp.int32, wide.shape, 0).astype(F32)
        place = way.source_place()
        for k, index in enumerate(indices):
            offset = (index[way.source][...] * way.size // way.part) ^ place
            bucket = jnp.zeros(offset.shape, F32)
            for at, group in enumerate(groups):
                for member in group:
                    bucket = jnp.where(offset == member, float(at), bucket)
            bucket = jnp.where(along[:1, :] < jnp.broadcast_to(index[2][...], (1, slot_count)), bucket, float(len(groups)))
            key = jnp.broadcast_to(bucket, square)
            order_along = key * slot_count + along_f
            key_down = jnp.sum(jnp.where(here, key, 0.0), axis=1, keepdims=True)
            order_down = key_down * slot_count + down_f[:, :1]
            rank = jnp.sum(jnp.where(order_along < order_down, 1.0, 0.0), axis=1, keepdims=True)
            order = jnp.sum(jnp.where(rank == wide, slot_f, 0.0), axis=0, keepdims=True)
            begin = jnp.sum(jnp.where(key_down < wide, 1.0, 0.0), axis=0, keepdims=True)
            ordered = rank == wide
            rows = [order, begin]
            for which in (way.source, 1 - way.source):
                value = jnp.broadcast_to(index[which][...].astype(F32), square)
                value_down = jnp.sum(jnp.where(here, value, 0.0), axis=1, keepdims=True)
                rows.append(jnp.sum(jnp.where(ordered, value_down, 0.0), axis=0, keepdims=True))
            for at, row in enumerate(rows):
                list_ref[2 * at + k : 2 * at + k + 1, :] = row.astype(jnp.int32)


def step_kernel(way, pick, at_group, last, *refs):
    (tile_a, tile_b, list_ref), refs = refs[:3], refs[3:]
    chunks, refs = refs[: len(pick)], refs[len(pick) :]
    if at_group:
        folded, refs = refs[1][...], refs[2:]
    total_ref, refs = refs[0], refs[1:]
    here, there = way.source_place(), way.target_place()
    if not at_group:
        total_ref[...] = jnp.zeros_like(total_ref)
        folded = jnp.zeros((8, total_ref.shape[-1]), F32)
    plain_ref, turned_ref = refs[-2:]
    for chunk, offset in zip(chunks, pick):
        for half in range(way.halves):
            at = pl.ds(pl.multiple_of((here ^ offset) * way.part + half * way.length, way.part), way.part)
            folded += put_chunk(chunk[half * way.part : (half + 1) * way.part, :], plain_ref, turned_ref, at, way.sign)
    for k, tile_ref in enumerate((tile_a, tile_b)):
        low, high = list_ref[k + 2, at_group], list_ref[k + 2, at_group + 1]

        def turn_of(group, carry):
            for lane in range(GROUP):
                at = low + group * GROUP + lane
                slot = list_ref[k, at]
                source = list_ref[k + 4, at]
                target = jnp.where(at < high, list_ref[k + 6, at] + k * way.target_shift, way.spare)
                span = pl.ds(pl.multiple_of(source * way.size + k * (way.halves - 1) * way.length, way.size), way.size)
                right = jnp.concatenate([plain_ref[span, :], turned_ref[span, :]], axis=0)
                goal = spans(way.size, target)
                product = jnp.dot(way.weights(tile_ref, slot), right, preferred_element_type=F32)
                total_ref[goal, :] = total_ref[goal, :] + product
            return carry

        lax.fori_loop(0, (high - low + GROUP - 1) // GROUP, turn_of, 0)
    if not last:
        refs[0][...] = folded
        return
    own_ref, norm_ref, sends = refs[0], refs[1], refs[2 : 2 + len(way.send_order)]
    norm = rows_of_norm(folded)
    norm_ref[...] = norm
    tail = norm_tail(norm)
    part = way.target_part
    for j, begin in enumerate(way.target_begins):
        def piece(position):
            return total_ref[pl.ds(pl.multiple_of(position * part + begin, part), part), :]

        own_ref[j * part : (j + 1) * part, :] = piece(there)
        for send, offset in zip(sends, way.send_order):
            send[j * part : (j + 1) * part, :] = piece(there ^ offset).astype(BF16)
    for send in sends:
        send[len(way.target_begins) * part :, :] = tail


def summed(own_ref, others):
    value = own_ref[...]
    for other in others:
        value = value + other[: own_ref.shape[0], :].astype(F32)
    return value


def norm_sum(own_norm, others, size):
    norm = own_norm
    for other in others:
        norm = norm + norm_from(other[size:, :])
    return norm


def start_kernel(others, own_ref, *refs):
    gradient = summed(own_ref, refs[:others])
    refs[-2][...] = gradient
    refs[-1][...] = gradient.astype(BF16)


def image_kernel(others, later, last, own_ref, norm_ref, *refs):
    ins, refs = refs[:others], refs[others:]
    image = summed(own_ref, ins)
    gamma = norm_sum(norm_ref[...], ins, own_ref.shape[0])
    if later:
        before_ref, gamma_ref = refs[:2]
        beta = gamma / (gamma_ref[...] + EPSILON)
        image = image + beta[:1] * before_ref[...]
        refs = refs[2:]
        refs[2][...] = beta
    refs[0][...] = image.astype(BF16)
    refs[1][...] = gamma
    if not last:
        refs[-1][...] = image


def gradient_kernel(others, own_ref, norm_ref, *refs):
    ins, (before_ref, gamma_ref, narrow_ref, alpha_ref, *wide) = refs[:others], refs[others:]
    change = summed(own_ref, ins)
    alpha = gamma_ref[...] / (norm_sum(norm_ref[...], ins, own_ref.shape[0]) + EPSILON)
    gradient = before_ref[...] - alpha[:1] * change
    narrow_ref[...] = gradient.astype(BF16)
    alpha_ref[...] = alpha
    for wide_ref in wide:
        wide_ref[...] = gradient


def norm_kernel(*refs):
    folded = sum(fold_squares(chunk[...].astype(F32)) for chunk in refs[:-1])
    refs[-1][...] = rows_of_norm(folded)


def answer_kernel(hyd_axis, core_axis, g_order, image_order, record_ref, gamma_ref, *refs):
    norms = len(g_order)
    norm = refs[0][...]
    for other in refs[1:norms]:
        norm = norm + other[...]
    refs = refs[norms:]
    alphas = [ref[...] for ref in refs[: ITERS - 1]] + [gamma_ref[...] / (norm + EPSILON)]
    refs = refs[ITERS - 1 :]
    betas = [ref[...] for ref in refs[: ITERS - 1]]
    refs = refs[ITERS - 1 :]
    g_count, image_count = ITERS * len(g_order), ITERS * len(image_order)
    g_chunks, images, (own_x, pair_x, wide_r, narrow_r) = refs[:g_count], refs[g_count : g_count + image_count], refs[g_count + image_count :]
    weights = [None] * ITERS
    weights[-1] = alphas[-1]
    for k in range(ITERS - 2, -1, -1):
        weights[k] = alphas[k] + betas[k] * weights[k + 1]
    core = lax.rem(lax.axis_index(core_axis), 2)
    here = lax.axis_index(hyd_axis)
    for at, offset in enumerate(g_order):
        mine = g_chunks[at :: len(g_order)]
        part = mine[0].shape[0] // 2
        span = spans(part, here ^ offset)
        own_x[span, :] = sum(w[:1] * g[:part, :].astype(F32) for w, g in zip(weights, mine))
        pair_x[span, :] = sum(w[:1] * g[part:, :].astype(F32) for w, g in zip(weights, mine)).astype(BF16)
    here = lax.axis_index(core_axis) // 2
    for at, offset in enumerate(image_order):
        mine = images[at :: len(image_order)]
        span = spans(mine[0].shape[0], here ^ offset)
        residual = packed_record(core, record_ref[0, span, :], record_ref[1, span, :])
        for alpha, image in zip(alphas, mine):
            residual = residual - alpha[:1] * image[...].astype(F32)
        wide_r[span, :] = residual
        narrow_r[span, :] = residual.astype(BF16)


def unpack_kernel(core_axis, own_x, own_r, pair_x, pair_r, x_ref, r_ref):
    core = lax.rem(lax.axis_index(core_axis), 2)
    for own, pair, out in ((own_x, pair_x, x_ref), (own_r, pair_r, r_ref)):
        for at in range(0, own.shape[0], 128):
            span = pl.ds(at, 128)
            mine, theirs = own[span, :], pair[span, :].astype(F32)
            first = jnp.where(core == 0, mine, theirs)
            second = jnp.where(core == 0, theirs, mine)
            low = low_half(mine.shape)
            out[0, span, :] = jnp.where(low, first, turn(second))
            out[1, span, :] = jnp.where(low, turn(first), second)


def solution(mesh):
    hyds, srcs = mesh.shape["hyd"], mesh.shape["src"]
    zs = srcs // 2

    def swap(value, axis, size, offset):
        return lax.ppermute(value, axis, [(i, i ^ offset) for i in range(size)])

    hyd_order = tuple(range(1, hyds))
    z_order = (zs - 1, *range(1, zs - 1))

    def over_hyd(values, order):
        return [swap(v, "hyd", hyds, o) for v, o in zip(values, order)]

    def over_z(values, order):
        return [swap(v, "src", srcs, 2 * o) for v, o in zip(values, order)]

    def groups_of(order, way):
        half = len(order) // 2
        return (order[:half], order[half:]) if way.part % way.size == 0 else (order,)

    def body(record, tile_data, tile_rows, tile_cols, tile_counts):
        own_tiles = tile_data[0, 0]
        slot_count, _, size, _ = own_tiles.shape
        rows, shots = record.shape[1:]
        cols = 2 * SRC_DEV
        row_tiles, col_tiles = rows // size, cols // size
        row_part, col_part = rows // zs, cols // hyds
        norm = ((8, shots), F32)
        row_sends = [((row_part + TAIL, shots), BF16)] * (zs - 1)
        col_sends = [((2 * col_part + TAIL, shots), BF16)] * (hyds - 1)
        col_total = ((cols + size, shots), F32)
        vector = lambda n, dtype: ((n, shots), dtype)

        pair_tiles = swap(own_tiles, "src", srcs, 1)
        index = (tile_rows[0], tile_cols[0], tile_counts)
        pair_index = tuple(swap(v, "src", srcs, 1) for v in index)
        pieces, groups = 4, slot_count // GROUP
        turned_shape = ((slot_count, size, 2 * size), BF16)
        turned_own, total, plain, turned = call(
            functools.partial(pack_kernel, "src", col_tiles), "pack",
            [turned_shape, col_total, vector(rows, BF16), vector(rows, BF16)],
            [(record.shape, F32), (own_tiles.shape, BF16), (index[0].shape, jnp.int32), (index[1].shape, jnp.int32)]
            + [(n, pltpu.SemaphoreType.DMA) for n in (pieces, groups, 2)],
            record, own_tiles, *index, away=4,
        )
        turned_pair, own, *sends = call(
            functools.partial(first_adjoint_kernel, "hyd", hyd_order, col_tiles), "first_adjoint",
            [turned_shape, vector(2 * col_part, F32)] + [vector(2 * col_part, BF16)] * (hyds - 1), [col_total],
            pair_tiles, *pair_index, total, plain, turned,
        )
        gradient, narrow = call(
            functools.partial(start_kernel, hyds - 1), "start",
            [vector(2 * col_part, F32), vector(2 * col_part, BF16)], [],
            own, *over_hyd(sends, hyd_order),
        )

        hyd_place = lambda: lax.axis_index("hyd")
        z_place = lambda: lax.axis_index("src") // 2
        flat = lambda tile_ref, slot: jnp.concatenate([tile_ref[slot, 0], tile_ref[slot, 1]], axis=1)
        forward = Way(1, 1.0, size, col_part, 2, cols, row_part, (0,), 0, row_tiles, z_order, hyd_place, z_place, flat)
        adjoint = Way(
            0, -1.0, size, row_part, 1, rows, col_part, (0, cols), col_tiles, 2 * col_tiles, hyd_order,
            z_place, hyd_place, lambda tile_ref, slot: tile_ref[slot],
        )
        g_order, image_order = ((0, *o[: len(o) // 2], *o[len(o) // 2 :][::-1]) for o in (hyd_order, z_order))
        g_groups, image_groups = (groups_of(order, w) for order, w in ((g_order, forward), (image_order, adjoint)))
        lists = call(
            functools.partial(list_kernel, ((forward, g_groups), (adjoint, image_groups))),
            "lists", [((8, 128), jnp.int32)] * 2, [], *index, *pair_index, vector=True,
        )

        def apply(way, name, tiles, slot_list, chunks, groups, outs):
            total = (((len(way.target_begins) * (way.spare // len(way.target_begins)) + 1) * size, shots), F32)
            carry, at = [], 0
            for k, group in enumerate(groups):
                last = k + 1 == len(groups)
                carry = call(
                    functools.partial(step_kernel, way, group, k, last), name,
                    [total] + (outs if last else [norm]), [vector(way.halves * way.length, BF16)] * 2,
                    *tiles, slot_list, *chunks[at : at + len(group)], *carry,
                    alias={3 + len(group): 0} if k else None,
                )
                at += len(group)
            return carry[1:]

        alphas, betas, g_chunks, images = [], [], [], []
        image = gamma = None
        for step in range(ITERS):
            last = step + 1 == ITERS
            chunks = [narrow, *over_hyd([narrow] * (hyds - 1), g_order[1:])]
            g_chunks += chunks
            own, own_norm, *sends = apply(
                forward, "forward", (own_tiles, pair_tiles), lists[0], chunks, g_groups, [vector(row_part, F32), norm] + row_sends
            )
            narrow, gamma, *more = call(
                functools.partial(image_kernel, zs - 1, step > 0, last), "image",
                [vector(row_part, BF16), norm] + [norm] * (step > 0) + [vector(row_part, F32)] * (not last), [],
                own, own_norm, *over_z(sends, z_order), *([image, gamma] if step else []),
            )
            image = None if last else more.pop()
            betas += more
            if last:
                issued = z_order[::-1]
                arrived = dict(zip(issued, over_z([narrow] * (zs - 1), issued)))
                chunks = [narrow, *(arrived[o] for o in image_order[1:])]
            else:
                chunks = [narrow, *over_z([narrow] * (zs - 1), image_order[1:])]
            images += chunks
            if last:
                break
            own, own_norm, *sends = apply(
                adjoint, "adjoint", (turned_own, turned_pair), lists[1], chunks, image_groups, [vector(2 * col_part, F32), norm] + col_sends
            )
            more_steps = step + 2 < ITERS
            narrow, alpha, *wide = call(
                functools.partial(gradient_kernel, hyds - 1), "gradient",
                [vector(2 * col_part, BF16), norm] + [vector(2 * col_part, F32)] * more_steps, [],
                own, own_norm, *over_hyd(sends, hyd_order), gradient, gamma,
            )
            gradient = wide[0] if more_steps else None
            alphas.append(alpha)

        (own_norm,) = call(norm_kernel, "norm", [norm], [], *chunks)
        norms = [own_norm] + over_hyd([own_norm] * (hyds - 1), hyd_order[::-1])
        own_x, pair_x, wide_r, narrow_r = call(
            functools.partial(answer_kernel, "hyd", "src", g_order, image_order), "answer",
            [vector(cols, F32), vector(cols, BF16), vector(rows, F32), vector(rows, BF16)], [],
            record, gamma, *norms, *alphas, *betas, *g_chunks, *images,
        )
        return call(
            functools.partial(unpack_kernel, "src"), "unpack",
            [((2, cols, shots), F32), ((2, rows, shots), F32)], [],
            own_x, wide_r, swap(pair_x, "src", srcs, 1), swap(narrow_r, "src", srcs, 1),
        )

    in_specs = (
        P(None, "hyd", None),
        P("hyd", "src", None, None, None, None),
        P("hyd", "src", None),
        P("hyd", "src", None),
        P("hyd", "src"),
    )
    out_specs = (P(None, "src", None), P(None, "hyd", None))
    return jax.shard_map(body, mesh=mesh, in_specs=in_specs, out_specs=out_specs, check_vma=False)
```

```python
import functools
from typing import NamedTuple

import jax
import jax.numpy as jnp
from jax import lax
from jax.experimental import pallas as pl
from jax.experimental.pallas import tpu as pltpu
from jax.sharding import PartitionSpec as P

SRC_DEV = 512
ITERS = 3
EPSILON = 1e-06
GROUP = 8
TAIL = 16
VMEM_BYTES = 16 << 20

F32 = jnp.float32
BF16 = jnp.bfloat16


class Way(NamedTuple):
    source: int
    sign: float
    size: int
    part: int
    halves: int
    length: int
    target_part: int
    target_begins: tuple
    target_shift: int
    spare: int
    send_order: tuple
    source_place: object
    target_place: object
    weights: object


def call(kernel, name, outs, scratch, *ins, vector=False, alias=None, away=0, out_space=pltpu.VMEM):
    def space(place, dtype):
        if place < away:
            return pltpu.HBM
        return pltpu.SMEM if dtype == jnp.int32 and not vector else pltpu.VMEM

    def room(shape, dtype):
        if dtype is pltpu.SemaphoreType.DMA:
            return dtype(shape if isinstance(shape, tuple) else (shape,))
        return (pltpu.SMEM if dtype == jnp.int32 else pltpu.VMEM)(shape, dtype)

    return pl.pallas_call(
        kernel,
        name=name,
        out_shape=[jax.ShapeDtypeStruct(s, d) for s, d in outs],
        in_specs=[pl.BlockSpec(memory_space=space(i, a.dtype)) for i, a in enumerate(ins)],
        out_specs=[pl.BlockSpec(memory_space=out_space) for _ in outs],
        scratch_shapes=[room(s, d) for s, d in scratch],
        input_output_aliases=alias or {},
        compiler_params=pltpu.CompilerParams(vmem_limit_bytes=VMEM_BYTES),
    )(*[pltpu.with_memory_space_constraint(a, pltpu.HBM) if i < away else a for i, a in enumerate(ins)])


def low_half(shape):
    return lax.broadcasted_iota(jnp.int32, shape, len(shape) - 1) < shape[-1] // 2


def turn(value):
    return pltpu.roll(value, value.shape[-1] // 2, value.ndim - 1)


def times_i(value, sign):
    rolled = turn(value)
    return jnp.where(low_half(value.shape), -sign * rolled, sign * rolled)


def both_parts(row):
    return row + turn(row)


def fold_squares(value):
    return jnp.sum((value * value).reshape(-1, 8, value.shape[-1]), axis=0)


def rows_of_norm(folded):
    row = both_parts(jnp.sum(folded, axis=0, keepdims=True))
    return jnp.broadcast_to(row, (8, folded.shape[-1]))


def norm_tail(norm):
    row = jnp.broadcast_to(norm[:1], (TAIL, norm.shape[-1]))
    high = row.astype(BF16).astype(F32)
    at = lax.broadcasted_iota(jnp.int32, row.shape, 0)
    return jnp.where(at == 0, high, jnp.where(at == 1, row - high, 0.0)).astype(BF16)


def norm_from(tail):
    tail = tail.astype(F32)
    return jnp.broadcast_to(tail[:1] + tail[1:2], (8, tail.shape[-1]))


def spans(size, count):
    return pl.ds(pl.multiple_of(count * size, size), size)


def group_of(index, group, step):
    for lane in range(GROUP):
        slot = group * GROUP + lane
        step(slot, slot < index[2][0], index[0][slot], index[1][slot])


def slots(index, step):
    def turn_of(group, carry):
        group_of(index, group, step)
        return carry

    lax.fori_loop(0, (index[2][0] + GROUP - 1) // GROUP, turn_of, 0)


def add_tile(acc_ref, weights, plain_ref, turned_ref, source, target):
    size = weights.shape[0]
    right = jnp.concatenate([plain_ref[spans(size, source), :], turned_ref[spans(size, source), :]], axis=0)
    at = spans(size, target)
    acc_ref[at, :] = acc_ref[at, :] + jnp.dot(weights, right, preferred_element_type=F32)


def put_chunk(chunk, plain_ref, turned_ref, at, sign):
    wide = chunk.astype(F32)
    plain_ref[at, :] = chunk
    turned_ref[at, :] = times_i(wide, sign).astype(BF16)
    return fold_squares(wide)


def packed_record(core, real, imag):
    first = jnp.where(core == 0, real, turn(real))
    second = jnp.where(core == 0, turn(imag), imag)
    return jnp.where(low_half(real.shape), first, second)


def pack_kernel(core_axis, tiles, record_hbm, tile_hbm, row_hbm, col_hbm, used_ref, *refs):
    turned_tile_ref, total_ref, plain_ref, turned_ref, record_ref, tile_ref, row_ref, col_ref, record_sem, tile_sem, index_sem = refs
    core = lax.rem(lax.axis_index(core_axis), 2)
    rows, slot_count = plain_ref.shape[0], tile_ref.shape[0]
    pieces = record_sem.shape[0]
    piece, groups = rows // pieces, slot_count // GROUP

    def record_copy(k):
        span = pl.ds(k * piece, piece)
        return pltpu.make_async_copy(record_hbm.at[:, span, :], record_ref.at[:, span, :], record_sem.at[k])

    def tile_copy(k):
        span = pl.ds(k * GROUP, GROUP)
        return pltpu.make_async_copy(tile_hbm.at[span], tile_ref.at[span], tile_sem.at[k])

    index_copies = [
        pltpu.make_async_copy(source, target, index_sem.at[k])
        for k, (source, target) in enumerate(((row_hbm, row_ref), (col_hbm, col_ref)))
    ]
    for k in range(pieces):
        record_copy(k).start()
    for copy in index_copies:
        copy.start()
    for k in range(groups):
        tile_copy(k).start()
    total_ref[...] = jnp.zeros_like(total_ref)
    for k in range(pieces):
        record_copy(k).wait()
        span = pl.ds(k * piece, piece)
        packed = packed_record(core, record_ref[0, span, :], record_ref[1, span, :])
        put_chunk(packed.astype(BF16), plain_ref, turned_ref, span, -1.0)
    for copy in index_copies:
        copy.wait()
    step = turn_step(tiles, tile_ref, turned_tile_ref, total_ref, plain_ref, turned_ref)
    for k in range(groups):
        tile_copy(k).wait()

        @pl.when(k * GROUP < used_ref[0, 0])
        def _():
            group_of((row_ref.at[0], col_ref.at[0], used_ref.at[0]), k, step)


def turn_step(tiles, tile_ref, turned_tile_ref, total_ref, plain_ref, turned_ref):
    def step(slot, valid, row, col):
        weights = jnp.concatenate([tile_ref[slot, 0].T, tile_ref[slot, 1].T], axis=1)
        turned_tile_ref[slot] = weights
        add_tile(total_ref, weights, plain_ref, turned_ref, row, jnp.where(valid, col, tiles))

    return step


def first_adjoint_kernel(hyd_axis, order, tiles, tile_ref, row_vmem, col_vmem, used_vmem, own_total_ref, plain_ref, turned_ref, *refs):
    turned_tile_ref, own_ref, sends = refs[0], refs[1], refs[2:-5]
    total_ref, *index, index_sem = refs[-5:]
    copies = [
        pltpu.make_async_copy(source, target, index_sem.at[k])
        for k, (source, target) in enumerate(zip((row_vmem, col_vmem, used_vmem), index))
    ]
    for copy in copies:
        copy.start()
    total_ref[...] = jnp.zeros_like(total_ref)
    for copy in copies:
        copy.wait()
    slots([ref.at[0] for ref in index], turn_step(tiles, tile_ref, turned_tile_ref, total_ref, plain_ref, turned_ref))
    give_columns(hyd_axis, order, own_total_ref, total_ref, own_ref, sends)


def give_columns(hyd_axis, order, first_ref, second_ref, own_ref, sends):
    here = lax.axis_index(hyd_axis)
    part = own_ref.shape[0] // 2
    own_ref[:part, :] = first_ref[spans(part, here), :]
    own_ref[part:, :] = second_ref[spans(part, here), :]
    for send, offset in zip(sends, order):
        there = here ^ offset
        send[:part, :] = first_ref[spans(part, there), :].astype(BF16)
        send[part : 2 * part, :] = second_ref[spans(part, there), :].astype(BF16)


def list_kernel(plans, *refs):
    indices, lists = (refs[:3], refs[3:6]), refs[6:]
    slot_count = refs[0].shape[1]
    square = (slot_count, slot_count)
    down, along = (lax.broadcasted_iota(jnp.int32, square, k) for k in (0, 1))
    down_f, along_f, here = down.astype(F32), along.astype(F32), down == along
    for list_ref, (way, groups) in zip(lists, plans):
        wide = lax.broadcasted_iota(jnp.int32, (slot_count, list_ref.shape[1]), 1).astype(F32)
        slot_f = lax.broadcasted_iota(jnp.int32, wide.shape, 0).astype(F32)
        place = way.source_place()
        for k, index in enumerate(indices):
            offset = (index[way.source][...] * way.size // way.part) ^ place
            bucket = jnp.zeros(offset.shape, F32)
            for at, group in enumerate(groups):
                for member in group:
                    bucket = jnp.where(offset == member, float(at), bucket)
            bucket = jnp.where(along[:1, :] < jnp.broadcast_to(index[2][...], (1, slot_count)), bucket, float(len(groups)))
            key = jnp.broadcast_to(bucket, square)
            order_along = key * slot_count + along_f
            key_down = jnp.sum(jnp.where(here, key, 0.0), axis=1, keepdims=True)
            order_down = key_down * slot_count + down_f[:, :1]
            rank = jnp.sum(jnp.where(order_along < order_down, 1.0, 0.0), axis=1, keepdims=True)
            order = jnp.sum(jnp.where(rank == wide, slot_f, 0.0), axis=0, keepdims=True)
            begin = jnp.sum(jnp.where(key_down < wide, 1.0, 0.0), axis=0, keepdims=True)
            ordered = rank == wide
            rows = [order, begin]
            for which in (way.source, 1 - way.source):
                value = jnp.broadcast_to(index[which][...].astype(F32), square)
                value_down = jnp.sum(jnp.where(here, value, 0.0), axis=1, keepdims=True)
                rows.append(jnp.sum(jnp.where(ordered, value_down, 0.0), axis=0, keepdims=True))
            for at, row in enumerate(rows):
                list_ref[2 * at + k : 2 * at + k + 1, :] = row.astype(jnp.int32)


def step_kernel(way, pick, at_group, last, *refs):
    (tile_a, tile_b, list_ref), refs = refs[:3], refs[3:]
    chunks, refs = refs[: len(pick)], refs[len(pick) :]
    if at_group:
        folded, refs = refs[1][...], refs[2:]
    total_ref, refs = refs[0], refs[1:]
    here, there = way.source_place(), way.target_place()
    if not at_group:
        total_ref[...] = jnp.zeros_like(total_ref)
        folded = jnp.zeros((8, total_ref.shape[-1]), F32)
    plain_ref, turned_ref = refs[-2:]
    for chunk, offset in zip(chunks, pick):
        for half in range(way.halves):
            at = pl.ds(pl.multiple_of((here ^ offset) * way.part + half * way.length, way.part), way.part)
            folded += put_chunk(chunk[half * way.part : (half + 1) * way.part, :], plain_ref, turned_ref, at, way.sign)
    for k, tile_ref in enumerate((tile_a, tile_b)):
        low, high = list_ref[k + 2, at_group], list_ref[k + 2, at_group + 1]

        def turn_of(group, carry):
            for lane in range(GROUP):
                at = low + group * GROUP + lane
                slot = list_ref[k, at]
                source = list_ref[k + 4, at]
                target = jnp.where(at < high, list_ref[k + 6, at] + k * way.target_shift, way.spare)
                span = pl.ds(pl.multiple_of(source * way.size + k * (way.halves - 1) * way.length, way.size), way.size)
                right = jnp.concatenate([plain_ref[span, :], turned_ref[span, :]], axis=0)
                goal = spans(way.size, target)
                product = jnp.dot(way.weights(tile_ref, slot), right, preferred_element_type=F32)
                total_ref[goal, :] = total_ref[goal, :] + product
            return carry

        lax.fori_loop(0, (high - low + GROUP - 1) // GROUP, turn_of, 0)
    if not last:
        refs[0][...] = folded
        return
    own_ref, norm_ref, sends = refs[0], refs[1], refs[2 : 2 + len(way.send_order)]
    norm = rows_of_norm(folded)
    norm_ref[...] = norm
    tail = norm_tail(norm)
    part = way.target_part
    for j, begin in enumerate(way.target_begins):
        def piece(position):
            return total_ref[pl.ds(pl.multiple_of(position * part + begin, part), part), :]

        own_ref[j * part : (j + 1) * part, :] = piece(there)
        for send, offset in zip(sends, way.send_order):
            send[j * part : (j + 1) * part, :] = piece(there ^ offset).astype(BF16)
    for send in sends:
        send[len(way.target_begins) * part :, :] = tail


def summed(own_ref, others):
    value = own_ref[...]
    for other in others:
        value = value + other[: own_ref.shape[0], :].astype(F32)
    return value


def norm_sum(own_norm, others, size):
    norm = own_norm
    for other in others:
        norm = norm + norm_from(other[size:, :])
    return norm


def start_kernel(others, own_ref, *refs):
    gradient = summed(own_ref, refs[:others])
    refs[-2][...] = gradient
    refs[-1][...] = gradient.astype(BF16)


def image_kernel(others, later, last, own_ref, norm_ref, *refs):
    ins, refs = refs[:others], refs[others:]
    image = summed(own_ref, ins)
    gamma = norm_sum(norm_ref[...], ins, own_ref.shape[0])
    if later:
        before_ref, gamma_ref = refs[:2]
        beta = gamma / (gamma_ref[...] + EPSILON)
        image = image + beta[:1] * before_ref[...]
        refs = refs[2:]
        refs[2][...] = beta
    refs[0][...] = image.astype(BF16)
    refs[1][...] = gamma
    if not last:
        refs[-1][...] = image


def gradient_kernel(others, own_ref, norm_ref, *refs):
    ins, (before_ref, gamma_ref, narrow_ref, alpha_ref, *wide) = refs[:others], refs[others:]
    change = summed(own_ref, ins)
    alpha = gamma_ref[...] / (norm_sum(norm_ref[...], ins, own_ref.shape[0]) + EPSILON)
    gradient = before_ref[...] - alpha[:1] * change
    narrow_ref[...] = gradient.astype(BF16)
    alpha_ref[...] = alpha
    for wide_ref in wide:
        wide_ref[...] = gradient


def norm_kernel(*refs):
    folded = sum(fold_squares(chunk[...].astype(F32)) for chunk in refs[:-1])
    refs[-1][...] = rows_of_norm(folded)


def answer_kernel(hyd_axis, core_axis, g_order, image_order, record_ref, gamma_ref, *refs):
    norms = len(g_order)
    norm = refs[0][...]
    for other in refs[1:norms]:
        norm = norm + other[...]
    refs = refs[norms:]
    alphas = [ref[...] for ref in refs[: ITERS - 1]] + [gamma_ref[...] / (norm + EPSILON)]
    refs = refs[ITERS - 1 :]
    betas = [ref[...] for ref in refs[: ITERS - 1]]
    refs = refs[ITERS - 1 :]
    g_count, image_count = ITERS * len(g_order), ITERS * len(image_order)
    g_chunks, images, (own_x, pair_x, wide_r, narrow_r) = refs[:g_count], refs[g_count : g_count + image_count], refs[g_count + image_count :]
    weights = [None] * ITERS
    weights[-1] = alphas[-1]
    for k in range(ITERS - 2, -1, -1):
        weights[k] = alphas[k] + betas[k] * weights[k + 1]
    core = lax.rem(lax.axis_index(core_axis), 2)
    here = lax.axis_index(hyd_axis)
    for at, offset in enumerate(g_order):
        mine = g_chunks[at :: len(g_order)]
        part = mine[0].shape[0] // 2
        span = spans(part, here ^ offset)
        own_x[span, :] = sum(w[:1] * g[:part, :].astype(F32) for w, g in zip(weights, mine))
        pair_x[span, :] = sum(w[:1] * g[part:, :].astype(F32) for w, g in zip(weights, mine)).astype(BF16)
    here = lax.axis_index(core_axis) // 2
    for at, offset in enumerate(image_order):
        mine = images[at :: len(image_order)]
        span = spans(mine[0].shape[0], here ^ offset)
        residual = packed_record(core, record_ref[0, span, :], record_ref[1, span, :])
        for alpha, image in zip(alphas, mine):
            residual = residual - alpha[:1] * image[...].astype(F32)
        wide_r[span, :] = residual
        narrow_r[span, :] = residual.astype(BF16)


def unpack_kernel(core_axis, own_x, own_r, pair_x, pair_r, x_hbm, r_hbm, x_ref, r_ref, sems):
    core = lax.rem(lax.axis_index(core_axis), 2)
    copies = []
    for k, (own, pair, out, target) in enumerate(((own_x, pair_x, x_ref, x_hbm), (own_r, pair_r, r_ref, r_hbm))):
        piece = own.shape[0] // sems.shape[1]
        for j in range(sems.shape[1]):
            span = pl.ds(j * piece, piece)
            mine, theirs = own[span, :], pair[span, :].astype(F32)
            first = jnp.where(core == 0, mine, theirs)
            second = jnp.where(core == 0, theirs, mine)
            low = low_half(mine.shape)
            out[0, span, :] = jnp.where(low, first, turn(second))
            out[1, span, :] = jnp.where(low, turn(first), second)
            copies.append(pltpu.make_async_copy(out.at[:, span, :], target.at[:, span, :], sems.at[k, j]))
            copies[-1].start()
    for copy in copies:
        copy.wait()


def solution(mesh):
    hyds, srcs = mesh.shape["hyd"], mesh.shape["src"]
    zs = srcs // 2

    def swap(value, axis, size, offset):
        return lax.ppermute(value, axis, [(i, i ^ offset) for i in range(size)])

    hyd_order = tuple(range(1, hyds))
    z_order = (zs - 1, *range(1, zs - 1))

    def over_hyd(values, order):
        return [swap(v, "hyd", hyds, o) for v, o in zip(values, order)]

    def over_z(values, order):
        return [swap(v, "src", srcs, 2 * o) for v, o in zip(values, order)]

    def groups_of(order, way):
        half = len(order) // 2
        return (order[:half], order[half:]) if way.part % way.size == 0 else (order,)

    def body(record, tile_data, tile_rows, tile_cols, tile_counts):
        own_tiles = tile_data[0, 0]
        slot_count, _, size, _ = own_tiles.shape
        rows, shots = record.shape[1:]
        cols = 2 * SRC_DEV
        row_tiles, col_tiles = rows // size, cols // size
        row_part, col_part = rows // zs, cols // hyds
        norm = ((8, shots), F32)
        row_sends = [((row_part + TAIL, shots), BF16)] * (zs - 1)
        col_sends = [((2 * col_part + TAIL, shots), BF16)] * (hyds - 1)
        col_total = ((cols + size, shots), F32)
        vector = lambda n, dtype: ((n, shots), dtype)

        pair_tiles = swap(own_tiles, "src", srcs, 1)
        index = (tile_rows[0], tile_cols[0], jnp.broadcast_to(tile_counts, tile_rows.shape[1:]))
        pair_index = tuple(swap(v, "src", srcs, 1) for v in index)
        pieces, groups = 4, slot_count // GROUP
        table = [(v.shape, jnp.int32) for v in index]
        turned_shape = ((slot_count, size, 2 * size), BF16)
        turned_own, total, plain, turned = call(
            functools.partial(pack_kernel, "src", col_tiles), "pack",
            [turned_shape, col_total, vector(rows, BF16), vector(rows, BF16)],
            [(record.shape, F32), (own_tiles.shape, BF16)] + table[:2]
            + [(n, pltpu.SemaphoreType.DMA) for n in (pieces, groups, 2)],
            record, own_tiles, *index, away=4,
        )
        turned_pair, own, *sends = call(
            functools.partial(first_adjoint_kernel, "hyd", hyd_order, col_tiles), "first_adjoint",
            [turned_shape, vector(2 * col_part, F32)] + [vector(2 * col_part, BF16)] * (hyds - 1),
            [col_total] + table + [(len(table), pltpu.SemaphoreType.DMA)],
            pair_tiles, *(pltpu.with_memory_space_constraint(v, pltpu.VMEM) for v in pair_index), total, plain, turned, vector=True,
        )
        gradient, narrow = call(
            functools.partial(start_kernel, hyds - 1), "start",
            [vector(2 * col_part, F32), vector(2 * col_part, BF16)], [],
            own, *over_hyd(sends, hyd_order),
        )

        hyd_place = lambda: lax.axis_index("hyd")
        z_place = lambda: lax.axis_index("src") // 2
        flat = lambda tile_ref, slot: jnp.concatenate([tile_ref[slot, 0], tile_ref[slot, 1]], axis=1)
        forward = Way(1, 1.0, size, col_part, 2, cols, row_part, (0,), 0, row_tiles, z_order, hyd_place, z_place, flat)
        adjoint = Way(
            0, -1.0, size, row_part, 1, rows, col_part, (0, cols), col_tiles, 2 * col_tiles, hyd_order,
            z_place, hyd_place, lambda tile_ref, slot: tile_ref[slot],
        )
        g_order, image_order = ((0, *o[: len(o) // 2], *o[len(o) // 2 :][::-1]) for o in (hyd_order, z_order))
        g_groups, image_groups = (groups_of(order, w) for order, w in ((g_order, forward), (image_order, adjoint)))
        lists = call(
            functools.partial(list_kernel, ((forward, g_groups), (adjoint, image_groups))),
            "lists", [((8, 128), jnp.int32)] * 2, [], *index, *pair_index, vector=True,
        )

        def apply(way, name, tiles, slot_list, chunks, groups, outs):
            total = (((len(way.target_begins) * (way.spare // len(way.target_begins)) + 1) * size, shots), F32)
            carry, at = [], 0
            for k, group in enumerate(groups):
                last = k + 1 == len(groups)
                carry = call(
                    functools.partial(step_kernel, way, group, k, last), name,
                    [total] + (outs if last else [norm]), [vector(way.halves * way.length, BF16)] * 2,
                    *tiles, slot_list, *chunks[at : at + len(group)], *carry,
                    alias={3 + len(group): 0} if k else None,
                )
                at += len(group)
            return carry[1:]

        alphas, betas, g_chunks, images = [], [], [], []
        image = gamma = None
        for step in range(ITERS):
            last = step + 1 == ITERS
            chunks = [narrow, *over_hyd([narrow] * (hyds - 1), g_order[1:])]
            g_chunks += chunks
            own, own_norm, *sends = apply(
                forward, "forward", (own_tiles, pair_tiles), lists[0], chunks, g_groups, [vector(row_part, F32), norm] + row_sends
            )
            narrow, gamma, *more = call(
                functools.partial(image_kernel, zs - 1, step > 0, last), "image",
                [vector(row_part, BF16), norm] + [norm] * (step > 0) + [vector(row_part, F32)] * (not last), [],
                own, own_norm, *over_z(sends, z_order), *([image, gamma] if step else []),
            )
            image = None if last else more.pop()
            betas += more
            if last:
                issued = z_order[::-1]
                arrived = dict(zip(issued, over_z([narrow] * (zs - 1), issued)))
                chunks = [narrow, *(arrived[o] for o in image_order[1:])]
            else:
                chunks = [narrow, *over_z([narrow] * (zs - 1), image_order[1:])]
            images += chunks
            if last:
                break
            own, own_norm, *sends = apply(
                adjoint, "adjoint", (turned_own, turned_pair), lists[1], chunks, image_groups, [vector(2 * col_part, F32), norm] + col_sends
            )
            more_steps = step + 2 < ITERS
            narrow, alpha, *wide = call(
                functools.partial(gradient_kernel, hyds - 1), "gradient",
                [vector(2 * col_part, BF16), norm] + [vector(2 * col_part, F32)] * more_steps, [],
                own, own_norm, *over_hyd(sends, hyd_order), gradient, gamma,
            )
            gradient = wide[0] if more_steps else None
            alphas.append(alpha)

        (own_norm,) = call(norm_kernel, "norm", [norm], [], *chunks)
        norms = [own_norm] + over_hyd([own_norm] * (hyds - 1), hyd_order[::-1])
        own_x, pair_x, wide_r, narrow_r = call(
            functools.partial(answer_kernel, "hyd", "src", g_order, image_order), "answer",
            [vector(cols, F32), vector(cols, BF16), vector(rows, F32), vector(rows, BF16)], [],
            record, gamma, *norms, *alphas, *betas, *g_chunks, *images,
        )
        return call(
            functools.partial(unpack_kernel, "src"), "unpack",
            [((2, cols, shots), F32), ((2, rows, shots), F32)],
            [((2, cols, shots), F32), ((2, rows, shots), F32), ((2, 4), pltpu.SemaphoreType.DMA)],
            own_x, wide_r, swap(pair_x, "src", srcs, 1), swap(narrow_r, "src", srcs, 1), out_space=pltpu.HBM,
        )

    in_specs = (
        P(None, "hyd", None),
        P("hyd", "src", None, None, None, None),
        P("hyd", "src", None),
        P("hyd", "src", None),
        P("hyd", "src"),
    )
    out_specs = (P(None, "src", None), P(None, "hyd", None))
    return jax.shard_map(body, mesh=mesh, in_specs=in_specs, out_specs=out_specs, check_vma=False)
```

```python
import functools
from typing import NamedTuple

import jax
import jax.numpy as jnp
from jax import lax
from jax.experimental import pallas as pl
from jax.experimental.pallas import tpu as pltpu
from jax.sharding import PartitionSpec as P

SRC_DEV = 512
ITERS = 3
EPSILON = 1e-06
GROUP = 8
WIDTH = 4
TAIL = 16
VMEM_BYTES = 16 << 20

F32 = jnp.float32
BF16 = jnp.bfloat16


class Way(NamedTuple):
    source: int
    sign: float
    size: int
    part: int
    halves: int
    length: int
    target_part: int
    target_begins: tuple
    target_shift: int
    spare: int
    send_order: tuple
    source_place: object
    target_place: object
    weights: object


def call(kernel, name, outs, scratch, *ins, vector=False, alias=None, away=0, out_space=pltpu.VMEM):
    def space(place, dtype):
        if place < away:
            return pltpu.HBM
        return pltpu.SMEM if dtype == jnp.int32 and not vector else pltpu.VMEM

    def room(shape, dtype):
        if dtype is pltpu.SemaphoreType.DMA:
            return dtype(shape if isinstance(shape, tuple) else (shape,))
        return (pltpu.SMEM if dtype == jnp.int32 else pltpu.VMEM)(shape, dtype)

    return pl.pallas_call(
        kernel,
        name=name,
        out_shape=[jax.ShapeDtypeStruct(s, d) for s, d in outs],
        in_specs=[pl.BlockSpec(memory_space=space(i, a.dtype)) for i, a in enumerate(ins)],
        out_specs=[pl.BlockSpec(memory_space=out_space) for _ in outs],
        scratch_shapes=[room(s, d) for s, d in scratch],
        input_output_aliases=alias or {},
        compiler_params=pltpu.CompilerParams(vmem_limit_bytes=VMEM_BYTES),
    )(*[pltpu.with_memory_space_constraint(a, pltpu.HBM) if i < away else a for i, a in enumerate(ins)])


def low_half(shape):
    return lax.broadcasted_iota(jnp.int32, shape, len(shape) - 1) < shape[-1] // 2


def turn(value):
    return pltpu.roll(value, value.shape[-1] // 2, value.ndim - 1)


def times_i(value, sign):
    rolled = turn(value)
    return jnp.where(low_half(value.shape), -sign * rolled, sign * rolled)


def both_parts(row):
    return row + turn(row)


def fold_squares(value):
    return jnp.sum((value * value).reshape(-1, 8, value.shape[-1]), axis=0)


def rows_of_norm(folded):
    row = both_parts(jnp.sum(folded, axis=0, keepdims=True))
    return jnp.broadcast_to(row, (8, folded.shape[-1]))


def norm_tail(norm):
    row = jnp.broadcast_to(norm[:1], (TAIL, norm.shape[-1]))
    high = row.astype(BF16).astype(F32)
    at = lax.broadcasted_iota(jnp.int32, row.shape, 0)
    return jnp.where(at == 0, high, jnp.where(at == 1, row - high, 0.0)).astype(BF16)


def norm_from(tail):
    tail = tail.astype(F32)
    return jnp.broadcast_to(tail[:1] + tail[1:2], (8, tail.shape[-1]))


def spans(size, count):
    return pl.ds(pl.multiple_of(count * size, size), size)


def group_of(index, group, step):
    for lane in range(GROUP):
        slot = group * GROUP + lane
        step(slot, slot < index[2][0], index[0][slot], index[1][slot])


def slots(index, step):
    def turn_of(group, carry):
        group_of(index, group, step)
        return carry

    lax.fori_loop(0, (index[2][0] + GROUP - 1) // GROUP, turn_of, 0)


def add_tile(acc_ref, weights, plain_ref, turned_ref, source, target):
    size = weights.shape[0]
    right = jnp.concatenate([plain_ref[spans(size, source), :], turned_ref[spans(size, source), :]], axis=0)
    at = spans(size, target)
    acc_ref[at, :] = acc_ref[at, :] + jnp.dot(weights, right, preferred_element_type=F32)


def put_chunk(chunk, plain_ref, turned_ref, at, sign):
    wide = chunk.astype(F32)
    plain_ref[at, :] = chunk
    turned_ref[at, :] = times_i(wide, sign).astype(BF16)
    return fold_squares(wide)


def packed_record(core, real, imag):
    first = jnp.where(core == 0, real, turn(real))
    second = jnp.where(core == 0, turn(imag), imag)
    return jnp.where(low_half(real.shape), first, second)


def pack_kernel(core_axis, tiles, record_hbm, tile_hbm, row_hbm, col_hbm, used_ref, *refs):
    turned_tile_ref, total_ref, plain_ref, turned_ref, record_ref, tile_ref, row_ref, col_ref, record_sem, tile_sem, index_sem = refs
    core = lax.rem(lax.axis_index(core_axis), 2)
    rows, slot_count = plain_ref.shape[0], tile_ref.shape[0]
    pieces = record_sem.shape[0]
    piece, groups = rows // pieces, slot_count // GROUP

    def record_copy(k):
        span = pl.ds(k * piece, piece)
        return pltpu.make_async_copy(record_hbm.at[:, span, :], record_ref.at[:, span, :], record_sem.at[k])

    def tile_copy(k):
        span = pl.ds(k * GROUP, GROUP)
        return pltpu.make_async_copy(tile_hbm.at[span], tile_ref.at[span], tile_sem.at[k])

    index_copies = [
        pltpu.make_async_copy(source, target, index_sem.at[k])
        for k, (source, target) in enumerate(((row_hbm, row_ref), (col_hbm, col_ref)))
    ]
    for k in range(pieces):
        record_copy(k).start()
    for copy in index_copies:
        copy.start()
    for k in range(groups):
        tile_copy(k).start()
    total_ref[...] = jnp.zeros_like(total_ref)
    for k in range(pieces):
        record_copy(k).wait()
        span = pl.ds(k * piece, piece)
        packed = packed_record(core, record_ref[0, span, :], record_ref[1, span, :])
        put_chunk(packed.astype(BF16), plain_ref, turned_ref, span, -1.0)
    for copy in index_copies:
        copy.wait()
    step = turn_step(tiles, tile_ref, turned_tile_ref, total_ref, plain_ref, turned_ref)
    for k in range(groups):
        tile_copy(k).wait()

        @pl.when(k * GROUP < used_ref[0, 0])
        def _():
            group_of((row_ref.at[0], col_ref.at[0], used_ref.at[0]), k, step)


def turn_step(tiles, tile_ref, turned_tile_ref, total_ref, plain_ref, turned_ref):
    def step(slot, valid, row, col):
        weights = jnp.concatenate([tile_ref[slot, 0].T, tile_ref[slot, 1].T], axis=1)
        turned_tile_ref[slot] = weights
        add_tile(total_ref, weights, plain_ref, turned_ref, row, jnp.where(valid, col, tiles))

    return step


def first_adjoint_kernel(hyd_axis, order, tiles, tile_ref, row_vmem, col_vmem, used_vmem, own_total_ref, plain_ref, turned_ref, *refs):
    turned_tile_ref, own_ref, sends = refs[0], refs[1], refs[2:-5]
    total_ref, *index, index_sem = refs[-5:]
    copies = [
        pltpu.make_async_copy(source, target, index_sem.at[k])
        for k, (source, target) in enumerate(zip((row_vmem, col_vmem, used_vmem), index))
    ]
    for copy in copies:
        copy.start()
    total_ref[...] = jnp.zeros_like(total_ref)
    for copy in copies:
        copy.wait()
    slots([ref.at[0] for ref in index], turn_step(tiles, tile_ref, turned_tile_ref, total_ref, plain_ref, turned_ref))
    give_columns(hyd_axis, order, own_total_ref, total_ref, own_ref, sends)


def give_columns(hyd_axis, order, first_ref, second_ref, own_ref, sends):
    here = lax.axis_index(hyd_axis)
    part = own_ref.shape[0] // 2
    own_ref[:part, :] = first_ref[spans(part, here), :]
    own_ref[part:, :] = second_ref[spans(part, here), :]
    for send, offset in zip(sends, order):
        there = here ^ offset
        send[:part, :] = first_ref[spans(part, there), :].astype(BF16)
        send[part : 2 * part, :] = second_ref[spans(part, there), :].astype(BF16)


def list_kernel(plans, *refs):
    indices, lists = (refs[:3], refs[3:6]), refs[6:]
    slot_count = refs[0].shape[1]
    square = (slot_count, slot_count)
    down, along = (lax.broadcasted_iota(jnp.int32, square, k) for k in (0, 1))
    down_f, along_f, here = down.astype(F32), along.astype(F32), down == along
    for list_ref, (way, groups) in zip(lists, plans):
        wide = lax.broadcasted_iota(jnp.int32, (slot_count, list_ref.shape[1]), 1).astype(F32)
        slot_f = lax.broadcasted_iota(jnp.int32, wide.shape, 0).astype(F32)
        place = way.source_place()
        for k, index in enumerate(indices):
            offset = (index[way.source][...] * way.size // way.part) ^ place
            bucket = jnp.zeros(offset.shape, F32)
            for at, group in enumerate(groups):
                for member in group:
                    bucket = jnp.where(offset == member, float(at), bucket)
            bucket = jnp.where(along[:1, :] < jnp.broadcast_to(index[2][...], (1, slot_count)), bucket, float(len(groups)))
            key = jnp.broadcast_to(bucket, square)
            order_along = key * slot_count + along_f
            key_down = jnp.sum(jnp.where(here, key, 0.0), axis=1, keepdims=True)
            order_down = key_down * slot_count + down_f[:, :1]
            rank = jnp.sum(jnp.where(order_along < order_down, 1.0, 0.0), axis=1, keepdims=True)
            order = jnp.sum(jnp.where(rank == wide, slot_f, 0.0), axis=0, keepdims=True)
            begin = jnp.sum(jnp.where(key_down < wide, 1.0, 0.0), axis=0, keepdims=True)
            ordered = rank == wide
            rows = [order, begin]
            for which in (way.source, 1 - way.source):
                value = jnp.broadcast_to(index[which][...].astype(F32), square)
                value_down = jnp.sum(jnp.where(here, value, 0.0), axis=1, keepdims=True)
                rows.append(jnp.sum(jnp.where(ordered, value_down, 0.0), axis=0, keepdims=True))
            for at, row in enumerate(rows):
                list_ref[2 * at + k : 2 * at + k + 1, :] = row.astype(jnp.int32)


def step_kernel(way, pick, at_group, last, *refs):
    (tile_a, tile_b, list_ref), refs = refs[:3], refs[3:]
    chunks, refs = refs[: len(pick)], refs[len(pick) :]
    if at_group:
        folded, refs = refs[1][...], refs[2:]
    total_ref, refs = refs[0], refs[1:]
    here, there = way.source_place(), way.target_place()
    if not at_group:
        total_ref[...] = jnp.zeros_like(total_ref)
        folded = jnp.zeros((8, total_ref.shape[-1]), F32)
    plain_ref, turned_ref = refs[-2:]
    for chunk, offset in zip(chunks, pick):
        for half in range(way.halves):
            at = pl.ds(pl.multiple_of((here ^ offset) * way.part + half * way.length, way.part), way.part)
            folded += put_chunk(chunk[half * way.part : (half + 1) * way.part, :], plain_ref, turned_ref, at, way.sign)
    for k, tile_ref in enumerate((tile_a, tile_b)):
        low, high = list_ref[k + 2, at_group], list_ref[k + 2, at_group + 1]

        def turn_of(group, carry):
            for lane in range(WIDTH):
                at = low + group * WIDTH + lane
                slot = list_ref[k, at]
                source = list_ref[k + 4, at]
                target = jnp.where(at < high, list_ref[k + 6, at] + k * way.target_shift, way.spare)
                span = pl.ds(pl.multiple_of(source * way.size + k * (way.halves - 1) * way.length, way.size), way.size)
                right = jnp.concatenate([plain_ref[span, :], turned_ref[span, :]], axis=0)
                goal = spans(way.size, target)
                product = jnp.dot(way.weights(tile_ref, slot), right, preferred_element_type=F32)
                total_ref[goal, :] = total_ref[goal, :] + product
            return carry

        lax.fori_loop(0, (high - low + WIDTH - 1) // WIDTH, turn_of, 0)
    if not last:
        refs[0][...] = folded
        return
    own_ref, norm_ref, sends = refs[0], refs[1], refs[2 : 2 + len(way.send_order)]
    norm = rows_of_norm(folded)
    norm_ref[...] = norm
    tail = norm_tail(norm)
    part = way.target_part
    for j, begin in enumerate(way.target_begins):
        def piece(position):
            return total_ref[pl.ds(pl.multiple_of(position * part + begin, part), part), :]

        own_ref[j * part : (j + 1) * part, :] = piece(there)
        for send, offset in zip(sends, way.send_order):
            send[j * part : (j + 1) * part, :] = piece(there ^ offset).astype(BF16)
    for send in sends:
        send[len(way.target_begins) * part :, :] = tail


def summed(own_ref, others):
    value = own_ref[...]
    for other in others:
        value = value + other[: own_ref.shape[0], :].astype(F32)
    return value


def norm_sum(own_norm, others, size):
    norm = own_norm
    for other in others:
        norm = norm + norm_from(other[size:, :])
    return norm


def start_kernel(others, own_ref, *refs):
    gradient = summed(own_ref, refs[:others])
    refs[-2][...] = gradient
    refs[-1][...] = gradient.astype(BF16)


def image_kernel(others, later, last, own_ref, norm_ref, *refs):
    ins, refs = refs[:others], refs[others:]
    image = summed(own_ref, ins)
    gamma = norm_sum(norm_ref[...], ins, own_ref.shape[0])
    if later:
        before_ref, gamma_ref = refs[:2]
        beta = gamma / (gamma_ref[...] + EPSILON)
        image = image + beta[:1] * before_ref[...]
        refs = refs[2:]
        refs[2][...] = beta
    refs[0][...] = image.astype(BF16)
    refs[1][...] = gamma
    if not last:
        refs[-1][...] = image


def gradient_kernel(others, own_ref, norm_ref, *refs):
    ins, (before_ref, gamma_ref, narrow_ref, alpha_ref, *wide) = refs[:others], refs[others:]
    change = summed(own_ref, ins)
    alpha = gamma_ref[...] / (norm_sum(norm_ref[...], ins, own_ref.shape[0]) + EPSILON)
    gradient = before_ref[...] - alpha[:1] * change
    narrow_ref[...] = gradient.astype(BF16)
    alpha_ref[...] = alpha
    for wide_ref in wide:
        wide_ref[...] = gradient


def norm_kernel(*refs):
    folded = sum(fold_squares(chunk[...].astype(F32)) for chunk in refs[:-1])
    refs[-1][...] = rows_of_norm(folded)


def answer_kernel(hyd_axis, core_axis, g_order, image_order, record_ref, gamma_ref, *refs):
    norms = len(g_order)
    norm = refs[0][...]
    for other in refs[1:norms]:
        norm = norm + other[...]
    refs = refs[norms:]
    alphas = [ref[...] for ref in refs[: ITERS - 1]] + [gamma_ref[...] / (norm + EPSILON)]
    refs = refs[ITERS - 1 :]
    betas = [ref[...] for ref in refs[: ITERS - 1]]
    refs = refs[ITERS - 1 :]
    g_count, image_count = ITERS * len(g_order), ITERS * len(image_order)
    g_chunks, images, (own_x, pair_x, wide_r, narrow_r) = refs[:g_count], refs[g_count : g_count + image_count], refs[g_count + image_count :]
    weights = [None] * ITERS
    weights[-1] = alphas[-1]
    for k in range(ITERS - 2, -1, -1):
        weights[k] = alphas[k] + betas[k] * weights[k + 1]
    core = lax.rem(lax.axis_index(core_axis), 2)
    here = lax.axis_index(hyd_axis)
    for at, offset in enumerate(g_order):
        mine = g_chunks[at :: len(g_order)]
        part = mine[0].shape[0] // 2
        span = spans(part, here ^ offset)
        own_x[span, :] = sum(w[:1] * g[:part, :].astype(F32) for w, g in zip(weights, mine))
        pair_x[span, :] = sum(w[:1] * g[part:, :].astype(F32) for w, g in zip(weights, mine)).astype(BF16)
    here = lax.axis_index(core_axis) // 2
    for at, offset in enumerate(image_order):
        mine = images[at :: len(image_order)]
        span = spans(mine[0].shape[0], here ^ offset)
        residual = packed_record(core, record_ref[0, span, :], record_ref[1, span, :])
        for alpha, image in zip(alphas, mine):
            residual = residual - alpha[:1] * image[...].astype(F32)
        wide_r[span, :] = residual
        narrow_r[span, :] = residual.astype(BF16)


def unpack_kernel(core_axis, own_x, own_r, pair_x, pair_r, x_hbm, r_hbm, x_ref, r_ref, sems):
    core = lax.rem(lax.axis_index(core_axis), 2)
    copies = []
    for k, (own, pair, out, target) in enumerate(((own_x, pair_x, x_ref, x_hbm), (own_r, pair_r, r_ref, r_hbm))):
        piece = own.shape[0] // sems.shape[1]
        for j in range(sems.shape[1]):
            span = pl.ds(j * piece, piece)
            mine, theirs = own[span, :], pair[span, :].astype(F32)
            first = jnp.where(core == 0, mine, theirs)
            second = jnp.where(core == 0, theirs, mine)
            low = low_half(mine.shape)
            out[0, span, :] = jnp.where(low, first, turn(second))
            out[1, span, :] = jnp.where(low, turn(first), second)
            copies.append(pltpu.make_async_copy(out.at[:, span, :], target.at[:, span, :], sems.at[k, j]))
            copies[-1].start()
    for copy in copies:
        copy.wait()


def solution(mesh):
    hyds, srcs = mesh.shape["hyd"], mesh.shape["src"]
    zs = srcs // 2

    def swap(value, axis, size, offset):
        return lax.ppermute(value, axis, [(i, i ^ offset) for i in range(size)])

    hyd_order = tuple(range(1, hyds))
    z_order = (zs - 1, *range(1, zs - 1))

    def over_hyd(values, order):
        return [swap(v, "hyd", hyds, o) for v, o in zip(values, order)]

    def over_z(values, order):
        return [swap(v, "src", srcs, 2 * o) for v, o in zip(values, order)]

    def groups_of(order, way):
        half = len(order) // 2
        return (order[:1], order[1:half], order[half:]) if way.part % way.size == 0 else (order,)

    def body(record, tile_data, tile_rows, tile_cols, tile_counts):
        own_tiles = tile_data[0, 0]
        slot_count, _, size, _ = own_tiles.shape
        rows, shots = record.shape[1:]
        cols = 2 * SRC_DEV
        row_tiles, col_tiles = rows // size, cols // size
        row_part, col_part = rows // zs, cols // hyds
        norm = ((8, shots), F32)
        row_sends = [((row_part + TAIL, shots), BF16)] * (zs - 1)
        col_sends = [((2 * col_part + TAIL, shots), BF16)] * (hyds - 1)
        col_total = ((cols + size, shots), F32)
        vector = lambda n, dtype: ((n, shots), dtype)

        pair_tiles = swap(own_tiles, "src", srcs, 1)
        index = (tile_rows[0], tile_cols[0], jnp.broadcast_to(tile_counts, tile_rows.shape[1:]))
        pair_index = tuple(swap(v, "src", srcs, 1) for v in index)
        pieces, groups = 4, slot_count // GROUP
        table = [(v.shape, jnp.int32) for v in index]
        turned_shape = ((slot_count, size, 2 * size), BF16)
        turned_own, total, plain, turned = call(
            functools.partial(pack_kernel, "src", col_tiles), "pack",
            [turned_shape, col_total, vector(rows, BF16), vector(rows, BF16)],
            [(record.shape, F32), (own_tiles.shape, BF16)] + table[:2]
            + [(n, pltpu.SemaphoreType.DMA) for n in (pieces, groups, 2)],
            record, own_tiles, *index, away=4,
        )
        turned_pair, own, *sends = call(
            functools.partial(first_adjoint_kernel, "hyd", hyd_order, col_tiles), "first_adjoint",
            [turned_shape, vector(2 * col_part, F32)] + [vector(2 * col_part, BF16)] * (hyds - 1),
            [col_total] + table + [(len(table), pltpu.SemaphoreType.DMA)],
            pair_tiles, *(pltpu.with_memory_space_constraint(v, pltpu.VMEM) for v in pair_index), total, plain, turned, vector=True,
        )
        gradient, narrow = call(
            functools.partial(start_kernel, hyds - 1), "start",
            [vector(2 * col_part, F32), vector(2 * col_part, BF16)], [],
            own, *over_hyd(sends, hyd_order),
        )

        hyd_place = lambda: lax.axis_index("hyd")
        z_place = lambda: lax.axis_index("src") // 2
        flat = lambda tile_ref, slot: jnp.concatenate([tile_ref[slot, 0], tile_ref[slot, 1]], axis=1)
        forward = Way(1, 1.0, size, col_part, 2, cols, row_part, (0,), 0, row_tiles, z_order, hyd_place, z_place, flat)
        adjoint = Way(
            0, -1.0, size, row_part, 1, rows, col_part, (0, cols), col_tiles, 2 * col_tiles, hyd_order,
            z_place, hyd_place, lambda tile_ref, slot: tile_ref[slot],
        )
        g_order, image_order = ((0, *o[: len(o) // 2], *o[len(o) // 2 :][::-1]) for o in (hyd_order, z_order))
        g_groups, image_groups = (groups_of(order, w) for order, w in ((g_order, forward), (image_order, adjoint)))
        lists = call(
            functools.partial(list_kernel, ((forward, g_groups), (adjoint, image_groups))),
            "lists", [((8, 128), jnp.int32)] * 2, [], *index, *pair_index, vector=True,
        )

        def apply(way, name, tiles, slot_list, chunks, groups, outs):
            total = (((len(way.target_begins) * (way.spare // len(way.target_begins)) + 1) * size, shots), F32)
            carry, at = [], 0
            for k, group in enumerate(groups):
                last = k + 1 == len(groups)
                carry = call(
                    functools.partial(step_kernel, way, group, k, last), name,
                    [total] + (outs if last else [norm]), [vector(way.halves * way.length, BF16)] * 2,
                    *tiles, slot_list, *chunks[at : at + len(group)], *carry,
                    alias={3 + len(group): 0} if k else None,
                )
                at += len(group)
            return carry[1:]

        alphas, betas, g_chunks, images = [], [], [], []
        image = gamma = None
        for step in range(ITERS):
            last = step + 1 == ITERS
            chunks = [narrow, *over_hyd([narrow] * (hyds - 1), g_order[1:])]
            g_chunks += chunks
            own, own_norm, *sends = apply(
                forward, "forward", (own_tiles, pair_tiles), lists[0], chunks, g_groups, [vector(row_part, F32), norm] + row_sends
            )
            narrow, gamma, *more = call(
                functools.partial(image_kernel, zs - 1, step > 0, last), "image",
                [vector(row_part, BF16), norm] + [norm] * (step > 0) + [vector(row_part, F32)] * (not last), [],
                own, own_norm, *over_z(sends, z_order), *([image, gamma] if step else []),
            )
            image = None if last else more.pop()
            betas += more
            chunks = [narrow, *over_z([narrow] * (zs - 1), image_order[1:])]
            images += chunks
            if last:
                break
            own, own_norm, *sends = apply(
                adjoint, "adjoint", (turned_own, turned_pair), lists[1], chunks, image_groups, [vector(2 * col_part, F32), norm] + col_sends
            )
            more_steps = step + 2 < ITERS
            narrow, alpha, *wide = call(
                functools.partial(gradient_kernel, hyds - 1), "gradient",
                [vector(2 * col_part, BF16), norm] + [vector(2 * col_part, F32)] * more_steps, [],
                own, own_norm, *over_hyd(sends, hyd_order), gradient, gamma,
            )
            gradient = wide[0] if more_steps else None
            alphas.append(alpha)

        chunks = [chunks[image_order.index(o)] for o in (0, *z_order[::-1])]
        (own_norm,) = call(norm_kernel, "norm", [norm], [], *chunks)
        norms = [own_norm] + over_hyd([own_norm] * (hyds - 1), hyd_order[::-1])
        own_x, pair_x, wide_r, narrow_r = call(
            functools.partial(answer_kernel, "hyd", "src", g_order, image_order), "answer",
            [vector(cols, F32), vector(cols, BF16), vector(rows, F32), vector(rows, BF16)], [],
            record, gamma, *norms, *alphas, *betas, *g_chunks, *images,
        )
        return call(
            functools.partial(unpack_kernel, "src"), "unpack",
            [((2, cols, shots), F32), ((2, rows, shots), F32)],
            [((2, cols, shots), F32), ((2, rows, shots), F32), ((2, 4), pltpu.SemaphoreType.DMA)],
            own_x, wide_r, swap(pair_x, "src", srcs, 1), swap(narrow_r, "src", srcs, 1), out_space=pltpu.HBM,
        )

    in_specs = (
        P(None, "hyd", None),
        P("hyd", "src", None, None, None, None),
        P("hyd", "src", None),
        P("hyd", "src", None),
        P("hyd", "src"),
    )
    out_specs = (P(None, "src", None), P(None, "hyd", None))
    return jax.shard_map(body, mesh=mesh, in_specs=in_specs, out_specs=out_specs, check_vma=False)
```

```python
import functools
from typing import NamedTuple

import jax
import jax.numpy as jnp
from jax import lax
from jax.experimental import pallas as pl
from jax.experimental.pallas import tpu as pltpu
from jax.sharding import PartitionSpec as P

SRC_DEV = 512
ITERS = 3
EPSILON = 1e-06
GROUP = 8
WIDTH = 8
LAST_WIDTH = 12
TAIL = 16
VMEM_BYTES = 16 << 20

F32 = jnp.float32
BF16 = jnp.bfloat16


class Way(NamedTuple):
    source: int
    sign: float
    size: int
    part: int
    halves: int
    length: int
    target_part: int
    target_begins: tuple
    target_shift: int
    spare: int
    send_order: tuple
    source_place: object
    target_place: object
    weights: object


def call(kernel, name, outs, scratch, *ins, vector=False, alias=None, away=0, out_space=pltpu.VMEM):
    def space(place, dtype):
        if place < away:
            return pltpu.HBM
        return pltpu.SMEM if dtype == jnp.int32 and not vector else pltpu.VMEM

    def room(shape, dtype):
        if dtype is pltpu.SemaphoreType.DMA:
            return dtype(shape if isinstance(shape, tuple) else (shape,))
        return (pltpu.SMEM if dtype == jnp.int32 else pltpu.VMEM)(shape, dtype)

    return pl.pallas_call(
        kernel,
        name=name,
        out_shape=[jax.ShapeDtypeStruct(s, d) for s, d in outs],
        in_specs=[pl.BlockSpec(memory_space=space(i, a.dtype)) for i, a in enumerate(ins)],
        out_specs=[pl.BlockSpec(memory_space=out_space) for _ in outs],
        scratch_shapes=[room(s, d) for s, d in scratch],
        input_output_aliases=alias or {},
        compiler_params=pltpu.CompilerParams(vmem_limit_bytes=VMEM_BYTES),
    )(*[pltpu.with_memory_space_constraint(a, pltpu.HBM) if i < away else a for i, a in enumerate(ins)])


def low_half(shape):
    return lax.broadcasted_iota(jnp.int32, shape, len(shape) - 1) < shape[-1] // 2


def turn(value):
    return pltpu.roll(value, value.shape[-1] // 2, value.ndim - 1)


def times_i(value, sign):
    rolled = turn(value)
    return jnp.where(low_half(value.shape), -sign * rolled, sign * rolled)


def both_parts(row):
    return row + turn(row)


def fold_squares(value):
    return jnp.sum((value * value).reshape(-1, 8, value.shape[-1]), axis=0)


def rows_of_norm(folded):
    row = both_parts(jnp.sum(folded, axis=0, keepdims=True))
    return jnp.broadcast_to(row, (8, folded.shape[-1]))


def norm_tail(norm):
    row = jnp.broadcast_to(norm[:1], (TAIL, norm.shape[-1]))
    high = row.astype(BF16).astype(F32)
    at = lax.broadcasted_iota(jnp.int32, row.shape, 0)
    return jnp.where(at == 0, high, jnp.where(at == 1, row - high, 0.0)).astype(BF16)


def norm_from(tail):
    tail = tail.astype(F32)
    return jnp.broadcast_to(tail[:1] + tail[1:2], (8, tail.shape[-1]))


def spans(size, count):
    return pl.ds(pl.multiple_of(count * size, size), size)


def group_of(index, group, step):
    for lane in range(GROUP):
        slot = group * GROUP + lane
        step(slot, slot < index[2][0], index[0][slot], index[1][slot])


def slots(index, step):
    def turn_of(group, carry):
        group_of(index, group, step)
        return carry

    lax.fori_loop(0, (index[2][0] + GROUP - 1) // GROUP, turn_of, 0)


def add_tile(acc_ref, weights, plain_ref, turned_ref, source, target):
    size = weights.shape[0]
    right = jnp.concatenate([plain_ref[spans(size, source), :], turned_ref[spans(size, source), :]], axis=0)
    at = spans(size, target)
    acc_ref[at, :] = acc_ref[at, :] + jnp.dot(weights, right, preferred_element_type=F32)


def put_chunk(chunk, plain_ref, turned_ref, at, sign):
    wide = chunk.astype(F32)
    plain_ref[at, :] = chunk
    turned_ref[at, :] = times_i(wide, sign).astype(BF16)
    return fold_squares(wide)


def packed_record(core, real, imag):
    first = jnp.where(core == 0, real, turn(real))
    second = jnp.where(core == 0, turn(imag), imag)
    return jnp.where(low_half(real.shape), first, second)


def pack_kernel(core_axis, tiles, record_hbm, tile_hbm, row_hbm, col_hbm, used_ref, *refs):
    tile_ref, turned_tile_ref, total_ref, plain_ref, turned_ref, record_ref, row_ref, col_ref, record_sem, tile_sem, index_sem = refs
    core = lax.rem(lax.axis_index(core_axis), 2)
    rows, slot_count = plain_ref.shape[0], tile_hbm.shape[0]
    pieces = record_sem.shape[0]
    piece, groups = rows // pieces, slot_count // GROUP

    def record_copy(k):
        span = pl.ds(k * piece, piece)
        return pltpu.make_async_copy(record_hbm.at[:, span, :], record_ref.at[:, span, :], record_sem.at[k])

    def tile_copy(k):
        span = pl.ds(k * GROUP, GROUP)
        return pltpu.make_async_copy(tile_hbm.at[span], tile_ref.at[span], tile_sem.at[k])

    index_copies = [
        pltpu.make_async_copy(source, target, index_sem.at[k])
        for k, (source, target) in enumerate(((row_hbm, row_ref), (col_hbm, col_ref)))
    ]
    for k in range(pieces):
        record_copy(k).start()
    for copy in index_copies:
        copy.start()
    for k in range(groups):
        tile_copy(k).start()
    total_ref[...] = jnp.zeros_like(total_ref)
    for k in range(pieces):
        record_copy(k).wait()
        span = pl.ds(k * piece, piece)
        packed = packed_record(core, record_ref[0, span, :], record_ref[1, span, :])
        put_chunk(packed.astype(BF16), plain_ref, turned_ref, span, -1.0)
    for copy in index_copies:
        copy.wait()
    step = turn_step(tiles, tile_ref, turned_tile_ref, 0, total_ref, plain_ref, turned_ref)
    for k in range(groups):
        tile_copy(k).wait()

        @pl.when(k * GROUP < used_ref[0, 0])
        def _():
            group_of((row_ref.at[0], col_ref.at[0], used_ref.at[0]), k, step)


def turn_step(tiles, tile_ref, turned_tile_ref, begin, total_ref, plain_ref, turned_ref):
    def step(slot, valid, row, col):
        weights = jnp.concatenate([tile_ref[slot, 0].T, tile_ref[slot, 1].T], axis=1)
        turned_tile_ref[begin + slot] = weights
        add_tile(total_ref, weights, plain_ref, turned_ref, row, jnp.where(valid, col, tiles))

    return step


def first_adjoint_kernel(hyd_axis, order, tiles, tile_ref, row_vmem, col_vmem, used_vmem, _, __, own_total_ref, plain_ref, turned_ref, *refs):
    tiles_ref, turned_tile_ref, own_ref, sends = refs[0], refs[1], refs[2], refs[3:-6]
    total_ref, *index, index_sem, tile_sem = refs[-6:]
    copies = [
        pltpu.make_async_copy(source, target, index_sem.at[k])
        for k, (source, target) in enumerate(zip((row_vmem, col_vmem, used_vmem), index))
    ]
    for copy in copies:
        copy.start()
    count = tile_ref.shape[0]
    join = pltpu.make_async_copy(tile_ref, tiles_ref.at[pl.ds(count, count)], tile_sem.at[0])
    join.start()
    total_ref[...] = jnp.zeros_like(total_ref)
    for copy in copies:
        copy.wait()
    slots([ref.at[0] for ref in index], turn_step(tiles, tile_ref, turned_tile_ref, count, total_ref, plain_ref, turned_ref))
    give_columns(hyd_axis, order, own_total_ref, total_ref, own_ref, sends)
    join.wait()


def give_columns(hyd_axis, order, first_ref, second_ref, own_ref, sends):
    here = lax.axis_index(hyd_axis)
    part = own_ref.shape[0] // 2
    own_ref[:part, :] = first_ref[spans(part, here), :]
    own_ref[part:, :] = second_ref[spans(part, here), :]
    for send, offset in zip(sends, order):
        there = here ^ offset
        send[:part, :] = first_ref[spans(part, there), :].astype(BF16)
        send[part : 2 * part, :] = second_ref[spans(part, there), :].astype(BF16)


def list_kernel(plans, *refs):
    indices, lists = (refs[:3], refs[3:6]), refs[6:]
    slot_count = refs[0].shape[1]
    square = (slot_count, slot_count)
    down, along = (lax.broadcasted_iota(jnp.int32, square, k) for k in (0, 1))
    here = down == along

    def stand(row):
        return jnp.sum(jnp.where(here, jnp.broadcast_to(row, square), 0.0), axis=1, keepdims=True)

    def count(condition):
        return jnp.sum(jnp.where(condition, 1.0, 0.0), axis=1, keepdims=True)

    for list_ref, (way, groups) in zip(lists, plans):
        wide = lax.broadcasted_iota(jnp.int32, (slot_count, list_ref.shape[1]), 1).astype(F32)
        place = way.source_place()
        keys = []
        for index in indices:
            offset = (index[way.source][...] * way.size // way.part) ^ place
            bucket = jnp.zeros(offset.shape, F32)
            for at, group in enumerate(groups):
                for member in group:
                    bucket = jnp.where(offset == member, float(at), bucket)
            used = along[:1, :] < jnp.broadcast_to(index[2][...], (1, slot_count))
            bucket = jnp.where(used, bucket, float(len(groups)))
            keys.append((jnp.broadcast_to(bucket, square), stand(bucket)))
        rows = [jnp.zeros((1, list_ref.shape[1]), F32) for _ in range(4)]
        for k, index in enumerate(indices):
            (key, key_down), (other, _) = keys[k], keys[1 - k]
            place_down = count((key < key_down) | ((key == key_down) & (along < down)))
            place_down += count(other <= key_down) if k else count(other < key_down)
            source = index[way.source][...].astype(F32) + float(k * (way.halves - 1) * (way.length // way.size))
            target = index[1 - way.source][...].astype(F32) + float(k * way.target_shift)
            slot = (down[:, :1] + k * slot_count).astype(F32)
            found = place_down == wide
            for at, value in ((0, slot), (2, stand(source)), (3, stand(target))):
                rows[at] = rows[at] + jnp.sum(jnp.where(found, value, 0.0), axis=0, keepdims=True)
            rows[1] = rows[1] + jnp.sum(jnp.where(key_down < wide, 1.0, 0.0), axis=0, keepdims=True)
        for at, row in enumerate(rows):
            list_ref[at : at + 1, :] = row.astype(jnp.int32)


def step_kernel(way, pick, at_group, last, *refs):
    (tile_ref, list_ref), refs = refs[:2], refs[2:]
    chunks, refs = refs[: len(pick)], refs[len(pick) :]
    if at_group:
        folded, refs = refs[1][...], refs[2:]
    total_ref, refs = refs[0], refs[1:]
    here, there = way.source_place(), way.target_place()
    if not at_group:
        total_ref[...] = jnp.zeros_like(total_ref)
        folded = jnp.zeros((8, total_ref.shape[-1]), F32)
    plain_ref, turned_ref = refs[-2:]
    for chunk, offset in zip(chunks, pick):
        for half in range(way.halves):
            at = pl.ds(pl.multiple_of((here ^ offset) * way.part + half * way.length, way.part), way.part)
            folded += put_chunk(chunk[half * way.part : (half + 1) * way.part, :], plain_ref, turned_ref, at, way.sign)
    low, high = list_ref[1, at_group], list_ref[1, at_group + 1]
    width = LAST_WIDTH if last else WIDTH

    def turn_of(group, carry):
        for lane in range(width):
            at = low + group * width + lane
            target = jnp.where(at < high, list_ref[3, at], way.spare)
            span = spans(way.size, list_ref[2, at])
            right = jnp.concatenate([plain_ref[span, :], turned_ref[span, :]], axis=0)
            goal = spans(way.size, target)
            product = jnp.dot(way.weights(tile_ref, list_ref[0, at]), right, preferred_element_type=F32)
            total_ref[goal, :] = total_ref[goal, :] + product
        return carry

    lax.fori_loop(0, (high - low + width - 1) // width, turn_of, 0)
    if not last:
        refs[0][...] = folded
        return
    own_ref, norm_ref, sends = refs[0], refs[1], refs[2 : 2 + len(way.send_order)]
    norm = rows_of_norm(folded)
    norm_ref[...] = norm
    tail = norm_tail(norm)
    part = way.target_part
    for j, begin in enumerate(way.target_begins):
        def piece(position):
            return total_ref[pl.ds(pl.multiple_of(position * part + begin, part), part), :]

        own_ref[j * part : (j + 1) * part, :] = piece(there)
        for send, offset in zip(sends, way.send_order):
            send[j * part : (j + 1) * part, :] = piece(there ^ offset).astype(BF16)
    for send in sends:
        send[len(way.target_begins) * part :, :] = tail


def summed(own_ref, others):
    value = own_ref[...]
    for other in others:
        value = value + other[: own_ref.shape[0], :].astype(F32)
    return value


def norm_sum(own_norm, others, size):
    norm = own_norm
    for other in others:
        norm = norm + norm_from(other[size:, :])
    return norm


def start_kernel(others, own_ref, *refs):
    gradient = summed(own_ref, refs[:others])
    refs[-2][...] = gradient
    refs[-1][...] = gradient.astype(BF16)


def image_kernel(others, later, last, own_ref, norm_ref, *refs):
    ins, refs = refs[:others], refs[others:]
    image = summed(own_ref, ins)
    gamma = norm_sum(norm_ref[...], ins, own_ref.shape[0])
    if later:
        before_ref, gamma_ref = refs[:2]
        beta = gamma / (gamma_ref[...] + EPSILON)
        image = image + beta[:1] * before_ref[...]
        refs = refs[2:]
        refs[2][...] = beta
    refs[0][...] = image.astype(BF16)
    refs[1][...] = gamma
    if not last:
        refs[-1][...] = image


def gradient_kernel(others, own_ref, norm_ref, *refs):
    ins, (before_ref, gamma_ref, narrow_ref, alpha_ref, *wide) = refs[:others], refs[others:]
    change = summed(own_ref, ins)
    alpha = gamma_ref[...] / (norm_sum(norm_ref[...], ins, own_ref.shape[0]) + EPSILON)
    gradient = before_ref[...] - alpha[:1] * change
    narrow_ref[...] = gradient.astype(BF16)
    alpha_ref[...] = alpha
    for wide_ref in wide:
        wide_ref[...] = gradient


def norm_kernel(*refs):
    folded = sum(fold_squares(chunk[...].astype(F32)) for chunk in refs[:-1])
    refs[-1][...] = rows_of_norm(folded)


def answer_kernel(hyd_axis, core_axis, g_order, image_order, record_ref, gamma_ref, *refs):
    norms = len(g_order)
    norm = refs[0][...]
    for other in refs[1:norms]:
        norm = norm + other[...]
    refs = refs[norms:]
    alphas = [ref[...] for ref in refs[: ITERS - 1]] + [gamma_ref[...] / (norm + EPSILON)]
    refs = refs[ITERS - 1 :]
    betas = [ref[...] for ref in refs[: ITERS - 1]]
    refs = refs[ITERS - 1 :]
    g_count, image_count = ITERS * len(g_order), ITERS * len(image_order)
    g_chunks, images, (own_x, pair_x, wide_r, narrow_r) = refs[:g_count], refs[g_count : g_count + image_count], refs[g_count + image_count :]
    weights = [None] * ITERS
    weights[-1] = alphas[-1]
    for k in range(ITERS - 2, -1, -1):
        weights[k] = alphas[k] + betas[k] * weights[k + 1]
    core = lax.rem(lax.axis_index(core_axis), 2)
    here = lax.axis_index(hyd_axis)
    for at, offset in enumerate(g_order):
        mine = g_chunks[at :: len(g_order)]
        part = mine[0].shape[0] // 2
        span = spans(part, here ^ offset)
        own_x[span, :] = sum(w[:1] * g[:part, :].astype(F32) for w, g in zip(weights, mine))
        pair_x[span, :] = sum(w[:1] * g[part:, :].astype(F32) for w, g in zip(weights, mine)).astype(BF16)
    here = lax.axis_index(core_axis) // 2
    for at, offset in enumerate(image_order):
        mine = images[at :: len(image_order)]
        span = spans(mine[0].shape[0], here ^ offset)
        residual = packed_record(core, record_ref[0, span, :], record_ref[1, span, :])
        for alpha, image in zip(alphas, mine):
            residual = residual - alpha[:1] * image[...].astype(F32)
        wide_r[span, :] = residual
        narrow_r[span, :] = residual.astype(BF16)


def unpack_kernel(core_axis, own_x, own_r, pair_x, pair_r, x_hbm, r_hbm, x_ref, r_ref, sems):
    core = lax.rem(lax.axis_index(core_axis), 2)
    copies = []
    for k, (own, pair, out, target) in enumerate(((own_x, pair_x, x_ref, x_hbm), (own_r, pair_r, r_ref, r_hbm))):
        piece = own.shape[0] // sems.shape[1]
        for j in range(sems.shape[1]):
            span = pl.ds(j * piece, piece)
            mine, theirs = own[span, :], pair[span, :].astype(F32)
            first = jnp.where(core == 0, mine, theirs)
            second = jnp.where(core == 0, theirs, mine)
            low = low_half(mine.shape)
            out[0, span, :] = jnp.where(low, first, turn(second))
            out[1, span, :] = jnp.where(low, turn(first), second)
            copies.append(pltpu.make_async_copy(out.at[:, span, :], target.at[:, span, :], sems.at[k, j]))
            copies[-1].start()
    for copy in copies:
        copy.wait()


def solution(mesh):
    hyds, srcs = mesh.shape["hyd"], mesh.shape["src"]
    zs = srcs // 2

    def swap(value, axis, size, offset):
        return lax.ppermute(value, axis, [(i, i ^ offset) for i in range(size)])

    hyd_order = tuple(range(1, hyds))
    z_order = (zs - 1, *range(1, zs - 1))

    def over_hyd(values, order):
        return [swap(v, "hyd", hyds, o) for v, o in zip(values, order)]

    def over_z(values, order):
        return [swap(v, "src", srcs, 2 * o) for v, o in zip(values, order)]

    def groups_of(order, way):
        half = len(order) // 2
        return (order[:1], order[1:half], order[half:]) if way.part % way.size == 0 else (order,)

    def body(record, tile_data, tile_rows, tile_cols, tile_counts):
        own_tiles = tile_data[0, 0]
        slot_count, _, size, _ = own_tiles.shape
        rows, shots = record.shape[1:]
        cols = 2 * SRC_DEV
        row_tiles, col_tiles = rows // size, cols // size
        row_part, col_part = rows // zs, cols // hyds
        norm = ((8, shots), F32)
        row_sends = [((row_part + TAIL, shots), BF16)] * (zs - 1)
        col_sends = [((2 * col_part + TAIL, shots), BF16)] * (hyds - 1)
        col_total = ((cols + size, shots), F32)
        vector = lambda n, dtype: ((n, shots), dtype)

        pair_tiles = swap(own_tiles, "src", srcs, 1)
        index = (tile_rows[0], tile_cols[0], jnp.broadcast_to(tile_counts, tile_rows.shape[1:]))
        pair_index = tuple(swap(v, "src", srcs, 1) for v in index)
        pieces, groups = 4, slot_count // GROUP
        table = [(v.shape, jnp.int32) for v in index]
        joined = [((2 * slot_count, 2, size, size), BF16), ((2 * slot_count, size, 2 * size), BF16)]
        both_tiles, both_turned, total, plain, turned = call(
            functools.partial(pack_kernel, "src", col_tiles), "pack",
            [*joined, col_total, vector(rows, BF16), vector(rows, BF16)],
            [(record.shape, F32)] + table[:2] + [(n, pltpu.SemaphoreType.DMA) for n in (pieces, groups, 2)],
            record, own_tiles, *index, away=4,
        )
        both_tiles, both_turned, own, *sends = call(
            functools.partial(first_adjoint_kernel, "hyd", hyd_order, col_tiles), "first_adjoint",
            [*joined, vector(2 * col_part, F32)] + [vector(2 * col_part, BF16)] * (hyds - 1),
            [col_total] + table + [(len(table), pltpu.SemaphoreType.DMA), (1, pltpu.SemaphoreType.DMA)],
            pair_tiles, *(pltpu.with_memory_space_constraint(v, pltpu.VMEM) for v in pair_index),
            both_tiles, both_turned, total, plain, turned, vector=True, alias={4: 0, 5: 1},
        )
        gradient, narrow = call(
            functools.partial(start_kernel, hyds - 1), "start",
            [vector(2 * col_part, F32), vector(2 * col_part, BF16)], [],
            own, *over_hyd(sends, hyd_order),
        )

        hyd_place = lambda: lax.axis_index("hyd")
        z_place = lambda: lax.axis_index("src") // 2
        flat = lambda tile_ref, slot: jnp.concatenate([tile_ref[slot, 0], tile_ref[slot, 1]], axis=1)
        forward = Way(1, 1.0, size, col_part, 2, cols, row_part, (0,), 0, row_tiles, z_order, hyd_place, z_place, flat)
        adjoint = Way(
            0, -1.0, size, row_part, 1, rows, col_part, (0, cols), col_tiles, 2 * col_tiles, hyd_order,
            z_place, hyd_place, lambda tile_ref, slot: tile_ref[slot],
        )
        g_order, image_order = ((0, *o[: len(o) // 2], *o[len(o) // 2 :][::-1]) for o in (hyd_order, z_order))
        g_groups, image_groups = (groups_of(order, w) for order, w in ((g_order, forward), (image_order, adjoint)))
        lists = call(
            functools.partial(list_kernel, ((forward, g_groups), (adjoint, image_groups))),
            "lists", [((8, 128), jnp.int32)] * 2, [], *index, *pair_index, vector=True,
        )

        def apply(way, name, tiles, slot_list, chunks, groups, outs):
            total = (((len(way.target_begins) * (way.spare // len(way.target_begins)) + 1) * size, shots), F32)
            carry, at = [], 0
            for k, group in enumerate(groups):
                last = k + 1 == len(groups)
                carry = call(
                    functools.partial(step_kernel, way, group, k, last), name,
                    [total] + (outs if last else [norm]), [vector(way.halves * way.length, BF16)] * 2,
                    tiles, slot_list, *chunks[at : at + len(group)], *carry,
                    alias={2 + len(group): 0} if k else None,
                )
                at += len(group)
            return carry[1:]

        alphas, betas, g_chunks, images = [], [], [], []
        image = gamma = None
        for step in range(ITERS):
            last = step + 1 == ITERS
            chunks = [narrow, *over_hyd([narrow] * (hyds - 1), g_order[1:])]
            g_chunks += chunks
            own, own_norm, *sends = apply(
                forward, "forward", both_tiles, lists[0], chunks, g_groups, [vector(row_part, F32), norm] + row_sends
            )
            narrow, gamma, *more = call(
                functools.partial(image_kernel, zs - 1, step > 0, last), "image",
                [vector(row_part, BF16), norm] + [norm] * (step > 0) + [vector(row_part, F32)] * (not last), [],
                own, own_norm, *over_z(sends, z_order), *([image, gamma] if step else []),
            )
            image = None if last else more.pop()
            betas += more
            chunks = [narrow, *over_z([narrow] * (zs - 1), image_order[1:])]
            images += chunks
            if last:
                break
            own, own_norm, *sends = apply(
                adjoint, "adjoint", both_turned, lists[1], chunks, image_groups, [vector(2 * col_part, F32), norm] + col_sends
            )
            more_steps = step + 2 < ITERS
            narrow, alpha, *wide = call(
                functools.partial(gradient_kernel, hyds - 1), "gradient",
                [vector(2 * col_part, BF16), norm] + [vector(2 * col_part, F32)] * more_steps, [],
                own, own_norm, *over_hyd(sends, hyd_order), gradient, gamma,
            )
            gradient = wide[0] if more_steps else None
            alphas.append(alpha)

        chunks = [chunks[image_order.index(o)] for o in (0, *z_order[::-1])]
        (own_norm,) = call(norm_kernel, "norm", [norm], [], *chunks)
        norms = [own_norm] + over_hyd([own_norm] * (hyds - 1), hyd_order[::-1])
        own_x, pair_x, wide_r, narrow_r = call(
            functools.partial(answer_kernel, "hyd", "src", g_order, image_order), "answer",
            [vector(cols, F32), vector(cols, BF16), vector(rows, F32), vector(rows, BF16)], [],
            record, gamma, *norms, *alphas, *betas, *g_chunks, *images,
        )
        return call(
            functools.partial(unpack_kernel, "src"), "unpack",
            [((2, cols, shots), F32), ((2, rows, shots), F32)],
            [((2, cols, shots), F32), ((2, rows, shots), F32), ((2, 4), pltpu.SemaphoreType.DMA)],
            own_x, wide_r, swap(pair_x, "src", srcs, 1), swap(narrow_r, "src", srcs, 1), out_space=pltpu.HBM,
        )

    in_specs = (
        P(None, "hyd", None),
        P("hyd", "src", None, None, None, None),
        P("hyd", "src", None),
        P("hyd", "src", None),
        P("hyd", "src"),
    )
    out_specs = (P(None, "src", None), P(None, "hyd", None))
    return jax.shard_map(body, mesh=mesh, in_specs=in_specs, out_specs=out_specs, check_vma=False)
```

```python
import functools
from typing import NamedTuple

import jax
import jax.numpy as jnp
from jax import lax
from jax.experimental import pallas as pl
from jax.experimental.pallas import tpu as pltpu
from jax.sharding import PartitionSpec as P

SRC_DEV = 512
ITERS = 3
EPSILON = 1e-06
GROUP = 8
WIDTH = 8
LAST_WIDTH = 12
TAIL = 16
VMEM_BYTES = 16 << 20

F32 = jnp.float32
BF16 = jnp.bfloat16


class Way(NamedTuple):
    source: int
    sign: float
    size: int
    part: int
    halves: int
    length: int
    target_part: int
    target_begins: tuple
    target_shift: int
    spare: int
    send_order: tuple
    source_place: object
    target_place: object
    weights: object


def call(kernel, name, outs, scratch, *ins, vector=False, alias=None, away=0, out_space=pltpu.VMEM):
    def space(place, dtype):
        if place < away:
            return pltpu.HBM
        return pltpu.SMEM if dtype == jnp.int32 and not vector else pltpu.VMEM

    def room(shape, dtype):
        if dtype is pltpu.SemaphoreType.DMA:
            return dtype(shape if isinstance(shape, tuple) else (shape,))
        return (pltpu.SMEM if dtype == jnp.int32 else pltpu.VMEM)(shape, dtype)

    return pl.pallas_call(
        kernel,
        name=name,
        out_shape=[jax.ShapeDtypeStruct(s, d) for s, d in outs],
        in_specs=[pl.BlockSpec(memory_space=space(i, a.dtype)) for i, a in enumerate(ins)],
        out_specs=[pl.BlockSpec(memory_space=out_space) for _ in outs],
        scratch_shapes=[room(s, d) for s, d in scratch],
        input_output_aliases=alias or {},
        compiler_params=pltpu.CompilerParams(vmem_limit_bytes=VMEM_BYTES),
    )(*[pltpu.with_memory_space_constraint(a, pltpu.HBM) if i < away else a for i, a in enumerate(ins)])


def low_half(shape):
    return lax.broadcasted_iota(jnp.int32, shape, len(shape) - 1) < shape[-1] // 2


def turn(value):
    return pltpu.roll(value, value.shape[-1] // 2, value.ndim - 1)


def times_i(value, sign):
    rolled = turn(value)
    return jnp.where(low_half(value.shape), -sign * rolled, sign * rolled)


def both_parts(row):
    return row + turn(row)


def fold_squares(value):
    return jnp.sum((value * value).reshape(-1, 8, value.shape[-1]), axis=0)


def rows_of_norm(folded):
    row = both_parts(jnp.sum(folded, axis=0, keepdims=True))
    return jnp.broadcast_to(row, (8, folded.shape[-1]))


def norm_tail(norm):
    row = jnp.broadcast_to(norm[:1], (TAIL, norm.shape[-1]))
    high = row.astype(BF16).astype(F32)
    at = lax.broadcasted_iota(jnp.int32, row.shape, 0)
    return jnp.where(at == 0, high, jnp.where(at == 1, row - high, 0.0)).astype(BF16)


def norm_from(tail):
    tail = tail.astype(F32)
    return jnp.broadcast_to(tail[:1] + tail[1:2], (8, tail.shape[-1]))


def spans(size, count):
    return pl.ds(pl.multiple_of(count * size, size), size)


def group_of(index, group, step):
    for lane in range(GROUP):
        slot = group * GROUP + lane
        step(slot, slot < index[2][0], index[0][slot], index[1][slot])


def slots(index, step):
    def turn_of(group, carry):
        group_of(index, group, step)
        return carry

    lax.fori_loop(0, (index[2][0] + GROUP - 1) // GROUP, turn_of, 0)


def add_tile(acc_ref, weights, plain_ref, turned_ref, source, target):
    size = weights.shape[0]
    right = jnp.concatenate([plain_ref[spans(size, source), :], turned_ref[spans(size, source), :]], axis=0)
    at = spans(size, target)
    acc_ref[at, :] = acc_ref[at, :] + jnp.dot(weights, right, preferred_element_type=F32)


def put_chunk(chunk, plain_ref, turned_ref, at, sign):
    wide = chunk.astype(F32)
    plain_ref[at, :] = chunk
    turned_ref[at, :] = times_i(wide, sign).astype(BF16)
    return fold_squares(wide)


def packed_record(core, real, imag):
    first = jnp.where(core == 0, real, turn(real))
    second = jnp.where(core == 0, turn(imag), imag)
    return jnp.where(low_half(real.shape), first, second)


def pack_kernel(core_axis, tiles, record_hbm, tile_hbm, row_hbm, col_hbm, used_ref, *refs):
    tile_ref, turned_tile_ref, total_ref, plain_ref, turned_ref, record_ref, row_ref, col_ref, record_sem, tile_sem, index_sem = refs
    core = lax.rem(lax.axis_index(core_axis), 2)
    rows, slot_count = plain_ref.shape[0], tile_hbm.shape[0]
    pieces = record_sem.shape[0]
    piece, groups = rows // pieces, slot_count // GROUP

    def record_copy(k):
        span = pl.ds(k * piece, piece)
        return pltpu.make_async_copy(record_hbm.at[:, span, :], record_ref.at[:, span, :], record_sem.at[k])

    def tile_copy(k):
        span = pl.ds(k * GROUP, GROUP)
        return pltpu.make_async_copy(tile_hbm.at[span], tile_ref.at[span], tile_sem.at[k])

    index_copies = [
        pltpu.make_async_copy(source, target, index_sem.at[k])
        for k, (source, target) in enumerate(((row_hbm, row_ref), (col_hbm, col_ref)))
    ]
    for k in range(pieces):
        record_copy(k).start()
    for copy in index_copies:
        copy.start()
    for k in range(groups):
        tile_copy(k).start()
    total_ref[...] = jnp.zeros_like(total_ref)
    for k in range(pieces):
        record_copy(k).wait()
        span = pl.ds(k * piece, piece)
        packed = packed_record(core, record_ref[0, span, :], record_ref[1, span, :])
        put_chunk(packed.astype(BF16), plain_ref, turned_ref, span, -1.0)
    for copy in index_copies:
        copy.wait()
    step = turn_step(tiles, tile_ref, turned_tile_ref, 0, total_ref, plain_ref, turned_ref)
    for k in range(groups):
        tile_copy(k).wait()

        @pl.when(k * GROUP < used_ref[0, 0])
        def _():
            group_of((row_ref.at[0], col_ref.at[0], used_ref.at[0]), k, step)


def turn_step(tiles, tile_ref, turned_tile_ref, begin, total_ref, plain_ref, turned_ref):
    def step(slot, valid, row, col):
        weights = jnp.concatenate([tile_ref[slot, 0].T, tile_ref[slot, 1].T], axis=1)
        turned_tile_ref[begin + slot] = weights
        add_tile(total_ref, weights, plain_ref, turned_ref, row, jnp.where(valid, col, tiles))

    return step


def first_adjoint_kernel(hyd_axis, order, tiles, tile_ref, row_vmem, col_vmem, used_vmem, _, __, own_total_ref, plain_ref, turned_ref, *refs):
    tiles_ref, turned_tile_ref, own_ref, sends = refs[0], refs[1], refs[2], refs[3:-6]
    total_ref, *index, index_sem, tile_sem = refs[-6:]
    copies = [
        pltpu.make_async_copy(source, target, index_sem.at[k])
        for k, (source, target) in enumerate(zip((row_vmem, col_vmem, used_vmem), index))
    ]
    for copy in copies:
        copy.start()
    count = tile_ref.shape[0]
    join = pltpu.make_async_copy(tile_ref, tiles_ref.at[pl.ds(count, count)], tile_sem.at[0])
    join.start()
    total_ref[...] = jnp.zeros_like(total_ref)
    for copy in copies:
        copy.wait()
    slots([ref.at[0] for ref in index], turn_step(tiles, tile_ref, turned_tile_ref, count, total_ref, plain_ref, turned_ref))
    give_columns(hyd_axis, order, own_total_ref, total_ref, own_ref, sends)
    join.wait()


def give_columns(hyd_axis, order, first_ref, second_ref, own_ref, sends):
    here = lax.axis_index(hyd_axis)
    part = own_ref.shape[0] // 2
    own_ref[:part, :] = first_ref[spans(part, here), :]
    own_ref[part:, :] = second_ref[spans(part, here), :]
    for send, offset in zip(sends, order):
        there = here ^ offset
        send[:part, :] = first_ref[spans(part, there), :].astype(BF16)
        send[part : 2 * part, :] = second_ref[spans(part, there), :].astype(BF16)


def list_kernel(plans, *refs):
    indices, lists = (refs[:3], refs[3:6]), refs[6:]
    slot_count = refs[0].shape[1]
    square = (slot_count, slot_count)
    down, along = (lax.broadcasted_iota(jnp.int32, square, k) for k in (0, 1))
    here = down == along

    def stand(row):
        return jnp.sum(jnp.where(here, jnp.broadcast_to(row, square), 0.0), axis=1, keepdims=True)

    def count(condition):
        return jnp.sum(jnp.where(condition, 1.0, 0.0), axis=1, keepdims=True)

    for list_ref, (way, groups) in zip(lists, plans):
        wide = lax.broadcasted_iota(jnp.int32, (slot_count, list_ref.shape[1]), 1).astype(F32)
        place = way.source_place()
        keys = []
        for index in indices:
            offset = (index[way.source][...] * way.size // way.part) ^ place
            bucket = jnp.zeros(offset.shape, F32)
            for at, group in enumerate(groups):
                for member in group:
                    bucket = jnp.where(offset == member, float(at), bucket)
            used = along[:1, :] < jnp.broadcast_to(index[2][...], (1, slot_count))
            bucket = jnp.where(used, bucket, float(len(groups)))
            keys.append((jnp.broadcast_to(bucket, square), stand(bucket)))
        rows = [jnp.zeros((1, list_ref.shape[1]), F32) for _ in range(4)]
        for k, index in enumerate(indices):
            (key, key_down), (other, _) = keys[k], keys[1 - k]
            place_down = count((key < key_down) | ((key == key_down) & (along < down)))
            place_down += count(other <= key_down) if k else count(other < key_down)
            source = index[way.source][...].astype(F32) + float(k * (way.halves - 1) * (way.length // way.size))
            target = index[1 - way.source][...].astype(F32) + float(k * way.target_shift)
            slot = (down[:, :1] + k * slot_count).astype(F32)
            found = place_down == wide
            for at, value in ((0, slot), (2, stand(source)), (3, stand(target))):
                rows[at] = rows[at] + jnp.sum(jnp.where(found, value, 0.0), axis=0, keepdims=True)
            rows[1] = rows[1] + jnp.sum(jnp.where(key_down < wide, 1.0, 0.0), axis=0, keepdims=True)
        for at, row in enumerate(rows):
            list_ref[at : at + 1, :] = row.astype(jnp.int32)


def step_kernel(way, pick, at_group, last, *refs):
    (tile_ref, list_ref), refs = refs[:2], refs[2:]
    chunks, refs = refs[: len(pick)], refs[len(pick) :]
    if at_group:
        folded, refs = refs[1][...], refs[2:]
    total_ref, refs = refs[0], refs[1:]
    here, there = way.source_place(), way.target_place()
    if not at_group:
        total_ref[...] = jnp.zeros_like(total_ref)
        folded = jnp.zeros((8, total_ref.shape[-1]), F32)
    plain_ref, turned_ref = refs[-2:]
    for chunk, offset in zip(chunks, pick):
        for half in range(way.halves):
            at = pl.ds(pl.multiple_of((here ^ offset) * way.part + half * way.length, way.part), way.part)
            folded += put_chunk(chunk[half * way.part : (half + 1) * way.part, :], plain_ref, turned_ref, at, way.sign)
    low, high = list_ref[1, at_group], list_ref[1, at_group + 1]
    width = LAST_WIDTH if last else WIDTH

    def turn_of(group, carry):
        for lane in range(width):
            at = low + group * width + lane
            target = jnp.where(at < high, list_ref[3, at], way.spare)
            span = spans(way.size, list_ref[2, at])
            right = jnp.concatenate([plain_ref[span, :], turned_ref[span, :]], axis=0)
            goal = spans(way.size, target)
            product = jnp.dot(way.weights(tile_ref, list_ref[0, at]), right, preferred_element_type=F32)
            total_ref[goal, :] = total_ref[goal, :] + product
        return carry

    lax.fori_loop(0, (high - low + width - 1) // width, turn_of, 0)
    if not last:
        refs[0][...] = folded
        return
    own_ref, norm_ref, sends = refs[0], refs[1], refs[2 : 2 + len(way.send_order)]
    norm = rows_of_norm(folded)
    norm_ref[...] = norm
    tail = norm_tail(norm)
    part = way.target_part
    for j, begin in enumerate(way.target_begins):
        def piece(position):
            return total_ref[pl.ds(pl.multiple_of(position * part + begin, part), part), :]

        own_ref[j * part : (j + 1) * part, :] = piece(there)
        for send, offset in zip(sends, way.send_order):
            send[j * part : (j + 1) * part, :] = piece(there ^ offset).astype(BF16)
    for send in sends:
        send[len(way.target_begins) * part :, :] = tail


def summed(own_ref, others):
    value = own_ref[...]
    for other in others:
        value = value + other[: own_ref.shape[0], :].astype(F32)
    return value


def norm_sum(own_norm, others, size):
    norm = own_norm
    for other in others:
        norm = norm + norm_from(other[size:, :])
    return norm


def start_kernel(others, own_ref, *refs):
    gradient = summed(own_ref, refs[:others])
    refs[-2][...] = gradient
    refs[-1][...] = gradient.astype(BF16)


def image_kernel(others, later, last, own_ref, norm_ref, *refs):
    ins, refs = refs[:others], refs[others:]
    image = summed(own_ref, ins)
    gamma = norm_sum(norm_ref[...], ins, own_ref.shape[0])
    if later:
        before_ref, gamma_ref = refs[:2]
        beta = gamma / (gamma_ref[...] + EPSILON)
        image = image + beta[:1] * before_ref[...]
        refs = refs[2:]
        refs[2][...] = beta
    refs[0][...] = image.astype(BF16)
    refs[1][...] = gamma
    if not last:
        refs[-1][...] = image


def gradient_kernel(others, own_ref, norm_ref, *refs):
    ins, (before_ref, gamma_ref, narrow_ref, alpha_ref, *wide) = refs[:others], refs[others:]
    change = summed(own_ref, ins)
    alpha = gamma_ref[...] / (norm_sum(norm_ref[...], ins, own_ref.shape[0]) + EPSILON)
    gradient = before_ref[...] - alpha[:1] * change
    narrow_ref[...] = gradient.astype(BF16)
    alpha_ref[...] = alpha
    for wide_ref in wide:
        wide_ref[...] = gradient


def norm_kernel(*refs):
    folded = sum(fold_squares(chunk[...].astype(F32)) for chunk in refs[:-1])
    refs[-1][...] = rows_of_norm(folded)


def answer_kernel(hyd_axis, core_axis, g_order, image_order, record_ref, gamma_ref, *refs):
    norms = len(g_order)
    norm = refs[0][...]
    for other in refs[1:norms]:
        norm = norm + other[...]
    refs = refs[norms:]
    alphas = [ref[...] for ref in refs[: ITERS - 1]] + [gamma_ref[...] / (norm + EPSILON)]
    refs = refs[ITERS - 1 :]
    betas = [ref[...] for ref in refs[: ITERS - 1]]
    refs = refs[ITERS - 1 :]
    g_count, image_count = ITERS * len(g_order), ITERS * len(image_order)
    g_chunks, images, (own_x, pair_x, wide_r, narrow_r) = refs[:g_count], refs[g_count : g_count + image_count], refs[g_count + image_count :]
    weights = [None] * ITERS
    weights[-1] = alphas[-1]
    for k in range(ITERS - 2, -1, -1):
        weights[k] = alphas[k] + betas[k] * weights[k + 1]
    core = lax.rem(lax.axis_index(core_axis), 2)
    here = lax.axis_index(hyd_axis)
    for at, offset in enumerate(g_order):
        mine = g_chunks[at :: len(g_order)]
        part = mine[0].shape[0] // 2
        span = spans(part, here ^ offset)
        own_x[span, :] = sum(w[:1] * g[:part, :].astype(F32) for w, g in zip(weights, mine))
        pair_x[span, :] = sum(w[:1] * g[part:, :].astype(F32) for w, g in zip(weights, mine)).astype(BF16)
    here = lax.axis_index(core_axis) // 2
    for at, offset in enumerate(image_order):
        mine = images[at :: len(image_order)]
        span = spans(mine[0].shape[0], here ^ offset)
        residual = packed_record(core, record_ref[0, span, :], record_ref[1, span, :])
        for alpha, image in zip(alphas, mine):
            residual = residual - alpha[:1] * image[...].astype(F32)
        wide_r[span, :] = residual
        narrow_r[span, :] = residual.astype(BF16)


def unpack_kernel(core_axis, own_x, own_r, pair_x, pair_r, x_hbm, r_hbm, x_ref, r_ref, sems):
    core = lax.rem(lax.axis_index(core_axis), 2)
    copies = []
    for k, (own, pair, out, target) in enumerate(((own_x, pair_x, x_ref, x_hbm), (own_r, pair_r, r_ref, r_hbm))):
        piece = own.shape[0] // sems.shape[1]
        for j in range(sems.shape[1]):
            span = pl.ds(j * piece, piece)
            mine, theirs = own[span, :], pair[span, :].astype(F32)
            first = jnp.where(core == 0, mine, theirs)
            second = jnp.where(core == 0, theirs, mine)
            low = low_half(mine.shape)
            out[0, span, :] = jnp.where(low, first, turn(second))
            out[1, span, :] = jnp.where(low, turn(first), second)
            copies.append(pltpu.make_async_copy(out.at[:, span, :], target.at[:, span, :], sems.at[k, j]))
            copies[-1].start()
    for copy in copies:
        copy.wait()


def solution(mesh):
    hyds, srcs = mesh.shape["hyd"], mesh.shape["src"]
    zs = srcs // 2

    def swap(value, axis, size, offset):
        return lax.ppermute(value, axis, [(i, i ^ offset) for i in range(size)])

    hyd_order = tuple(range(1, hyds))
    z_order = (zs - 1, *range(1, zs - 1))

    def over_hyd(values, order):
        return [swap(v, "hyd", hyds, o) for v, o in zip(values, order)]

    def over_z(values, order):
        return [swap(v, "src", srcs, 2 * o) for v, o in zip(values, order)]

    def groups_of(order, way):
        half = len(order) // 2
        return (order[:1], order[1:half], order[half:]) if way.part % way.size == 0 else (order,)

    def body(record, tile_data, tile_rows, tile_cols, tile_counts):
        own_tiles = tile_data[0, 0]
        slot_count, _, size, _ = own_tiles.shape
        rows, shots = record.shape[1:]
        cols = 2 * SRC_DEV
        row_tiles, col_tiles = rows // size, cols // size
        row_part, col_part = rows // zs, cols // hyds
        norm = ((8, shots), F32)
        row_sends = [((row_part + TAIL, shots), BF16)] * (zs - 1)
        col_sends = [((2 * col_part + TAIL, shots), BF16)] * (hyds - 1)
        col_total = ((cols + size, shots), F32)
        vector = lambda n, dtype: ((n, shots), dtype)

        pair_tiles = swap(own_tiles, "src", srcs, 1)
        index = (tile_rows[0], tile_cols[0], jnp.broadcast_to(tile_counts, tile_rows.shape[1:]))
        pair_index = tuple(swap(v, "src", srcs, 1) for v in index)
        pieces, groups = 4, slot_count // GROUP
        table = [(v.shape, jnp.int32) for v in index]
        joined = [((2 * slot_count, 2, size, size), BF16), ((2 * slot_count, size, 2 * size), BF16)]
        both_tiles, both_turned, total, plain, turned = call(
            functools.partial(pack_kernel, "src", col_tiles), "pack",
            [*joined, col_total, vector(rows, BF16), vector(rows, BF16)],
            [(record.shape, F32)] + table[:2] + [(n, pltpu.SemaphoreType.DMA) for n in (pieces, groups, 2)],
            record, own_tiles, *index, away=4,
        )
        both_tiles, both_turned, own, *sends = call(
            functools.partial(first_adjoint_kernel, "hyd", hyd_order, col_tiles), "first_adjoint",
            [*joined, vector(2 * col_part, F32)] + [vector(2 * col_part, BF16)] * (hyds - 1),
            [col_total] + table + [(len(table), pltpu.SemaphoreType.DMA), (1, pltpu.SemaphoreType.DMA)],
            pair_tiles, *(pltpu.with_memory_space_constraint(v, pltpu.VMEM) for v in pair_index),
            both_tiles, both_turned, total, plain, turned, vector=True, alias={4: 0, 5: 1},
        )
        gradient, narrow = call(
            functools.partial(start_kernel, hyds - 1), "start",
            [vector(2 * col_part, F32), vector(2 * col_part, BF16)], [],
            own, *over_hyd(sends, hyd_order),
        )

        hyd_place = lambda: lax.axis_index("hyd")
        z_place = lambda: lax.axis_index("src") // 2
        flat = lambda tile_ref, slot: jnp.concatenate([tile_ref[slot, 0], tile_ref[slot, 1]], axis=1)
        forward = Way(1, 1.0, size, col_part, 2, cols, row_part, (0,), 0, row_tiles, z_order, hyd_place, z_place, flat)
        adjoint = Way(
            0, -1.0, size, row_part, 1, rows, col_part, (0, cols), col_tiles, 2 * col_tiles, hyd_order,
            z_place, hyd_place, lambda tile_ref, slot: tile_ref[slot],
        )
        g_order, image_order = (0, *hyd_order), (0, *z_order)
        g_groups, image_groups = (groups_of(order, w) for order, w in ((g_order, forward), (image_order, adjoint)))
        lists = call(
            functools.partial(list_kernel, ((forward, g_groups), (adjoint, image_groups))),
            "lists", [((8, 128), jnp.int32)] * 2, [], *index, *pair_index, vector=True,
        )

        def apply(way, name, tiles, slot_list, chunks, groups, outs):
            total = (((len(way.target_begins) * (way.spare // len(way.target_begins)) + 1) * size, shots), F32)
            carry, at = [], 0
            for k, group in enumerate(groups):
                last = k + 1 == len(groups)
                carry = call(
                    functools.partial(step_kernel, way, group, k, last), name,
                    [total] + (outs if last else [norm]), [vector(way.halves * way.length, BF16)] * 2,
                    tiles, slot_list, *chunks[at : at + len(group)], *carry,
                    alias={2 + len(group): 0} if k else None,
                )
                at += len(group)
            return carry[1:]

        alphas, betas, g_chunks, images = [], [], [], []
        image = gamma = None
        for step in range(ITERS):
            last = step + 1 == ITERS
            chunks = [narrow, *over_hyd([narrow] * (hyds - 1), g_order[1:])]
            g_chunks += chunks
            own, own_norm, *sends = apply(
                forward, "forward", both_tiles, lists[0], chunks, g_groups, [vector(row_part, F32), norm] + row_sends
            )
            narrow, gamma, *more = call(
                functools.partial(image_kernel, zs - 1, step > 0, last), "image",
                [vector(row_part, BF16), norm] + [norm] * (step > 0) + [vector(row_part, F32)] * (not last), [],
                own, own_norm, *over_z(sends, z_order), *([image, gamma] if step else []),
            )
            image = None if last else more.pop()
            betas += more
            chunks = [narrow, *over_z([narrow] * (zs - 1), image_order[1:])]
            images += chunks
            if last:
                break
            own, own_norm, *sends = apply(
                adjoint, "adjoint", both_turned, lists[1], chunks, image_groups, [vector(2 * col_part, F32), norm] + col_sends
            )
            more_steps = step + 2 < ITERS
            narrow, alpha, *wide = call(
                functools.partial(gradient_kernel, hyds - 1), "gradient",
                [vector(2 * col_part, BF16), norm] + [vector(2 * col_part, F32)] * more_steps, [],
                own, own_norm, *over_hyd(sends, hyd_order), gradient, gamma,
            )
            gradient = wide[0] if more_steps else None
            alphas.append(alpha)

        (own_norm,) = call(norm_kernel, "norm", [norm], [], *chunks)
        norms = [own_norm] + over_hyd([own_norm] * (hyds - 1), hyd_order)
        own_x, pair_x, wide_r, narrow_r = call(
            functools.partial(answer_kernel, "hyd", "src", g_order, image_order), "answer",
            [vector(cols, F32), vector(cols, BF16), vector(rows, F32), vector(rows, BF16)], [],
            record, gamma, *norms, *alphas, *betas, *g_chunks, *images,
        )
        return call(
            functools.partial(unpack_kernel, "src"), "unpack",
            [((2, cols, shots), F32), ((2, rows, shots), F32)],
            [((2, cols, shots), F32), ((2, rows, shots), F32), ((2, 4), pltpu.SemaphoreType.DMA)],
            own_x, wide_r, swap(pair_x, "src", srcs, 1), swap(narrow_r, "src", srcs, 1), out_space=pltpu.HBM,
        )

    in_specs = (
        P(None, "hyd", None),
        P("hyd", "src", None, None, None, None),
        P("hyd", "src", None),
        P("hyd", "src", None),
        P("hyd", "src"),
    )
    out_specs = (P(None, "src", None), P(None, "hyd", None))
    return jax.shard_map(body, mesh=mesh, in_specs=in_specs, out_specs=out_specs, check_vma=False)
```

```python
import functools
from typing import NamedTuple

import jax
import jax.numpy as jnp
from jax import lax
from jax.experimental import pallas as pl
from jax.experimental.pallas import tpu as pltpu
from jax.sharding import PartitionSpec as P

SRC_DEV = 512
ITERS = 3
EPSILON = 1e-06
GROUP = 8
WIDTH = 8
LAST_WIDTH = 12
TAIL = 16
VMEM_BYTES = 16 << 20

F32 = jnp.float32
BF16 = jnp.bfloat16


class Way(NamedTuple):
    source: int
    sign: float
    size: int
    part: int
    halves: int
    length: int
    target_part: int
    target_begins: tuple
    target_shift: int
    spare: int
    send_order: tuple
    source_place: object
    target_place: object
    weights: object


def call(kernel, name, outs, scratch, *ins, vector=False, alias=None, away=0, out_space=pltpu.VMEM):
    def space(place, dtype):
        if place < away:
            return pltpu.HBM
        return pltpu.SMEM if dtype == jnp.int32 and not vector else pltpu.VMEM

    def room(shape, dtype):
        if dtype is pltpu.SemaphoreType.DMA:
            return dtype(shape if isinstance(shape, tuple) else (shape,))
        return (pltpu.SMEM if dtype == jnp.int32 else pltpu.VMEM)(shape, dtype)

    return pl.pallas_call(
        kernel,
        name=name,
        out_shape=[jax.ShapeDtypeStruct(s, d) for s, d in outs],
        in_specs=[pl.BlockSpec(memory_space=space(i, a.dtype)) for i, a in enumerate(ins)],
        out_specs=[pl.BlockSpec(memory_space=out_space) for _ in outs],
        scratch_shapes=[room(s, d) for s, d in scratch],
        input_output_aliases=alias or {},
        compiler_params=pltpu.CompilerParams(vmem_limit_bytes=VMEM_BYTES),
    )(*[pltpu.with_memory_space_constraint(a, pltpu.HBM) if i < away else a for i, a in enumerate(ins)])


def low_half(shape):
    return lax.broadcasted_iota(jnp.int32, shape, len(shape) - 1) < shape[-1] // 2


def turn(value):
    return pltpu.roll(value, value.shape[-1] // 2, value.ndim - 1)


def times_i(value, sign):
    rolled = turn(value)
    return jnp.where(low_half(value.shape), -sign * rolled, sign * rolled)


def both_parts(row):
    return row + turn(row)


def fold_squares(value):
    return jnp.sum((value * value).reshape(-1, 8, value.shape[-1]), axis=0)


def rows_of_norm(folded):
    row = both_parts(jnp.sum(folded, axis=0, keepdims=True))
    return jnp.broadcast_to(row, (8, folded.shape[-1]))


def norm_tail(norm):
    row = jnp.broadcast_to(norm[:1], (TAIL, norm.shape[-1]))
    high = row.astype(BF16).astype(F32)
    at = lax.broadcasted_iota(jnp.int32, row.shape, 0)
    return jnp.where(at == 0, high, jnp.where(at == 1, row - high, 0.0)).astype(BF16)


def norm_from(tail):
    tail = tail.astype(F32)
    return jnp.broadcast_to(tail[:1] + tail[1:2], (8, tail.shape[-1]))


def spans(size, count):
    return pl.ds(pl.multiple_of(count * size, size), size)


def group_of(index, group, step):
    for lane in range(GROUP):
        slot = group * GROUP + lane
        step(slot, slot < index[2][0], index[0][slot], index[1][slot])


def slots(index, step):
    def turn_of(group, carry):
        group_of(index, group, step)
        return carry

    lax.fori_loop(0, (index[2][0] + GROUP - 1) // GROUP, turn_of, 0)


def add_tile(acc_ref, weights, plain_ref, turned_ref, source, target):
    size = weights.shape[0]
    right = jnp.concatenate([plain_ref[spans(size, source), :], turned_ref[spans(size, source), :]], axis=0)
    at = spans(size, target)
    acc_ref[at, :] = acc_ref[at, :] + jnp.dot(weights, right, preferred_element_type=F32)


def put_chunk(chunk, plain_ref, turned_ref, at, sign):
    wide = chunk.astype(F32)
    plain_ref[at, :] = chunk
    turned_ref[at, :] = times_i(wide, sign).astype(BF16)
    return fold_squares(wide)


def packed_record(core, real, imag):
    first = jnp.where(core == 0, real, turn(real))
    second = jnp.where(core == 0, turn(imag), imag)
    return jnp.where(low_half(real.shape), first, second)


def pack_kernel(core_axis, tiles, record_hbm, tile_hbm, row_hbm, col_hbm, used_ref, *refs):
    tile_ref, turned_tile_ref, total_ref, plain_ref, turned_ref, record_ref, row_ref, col_ref, record_sem, tile_sem, index_sem = refs
    core = lax.rem(lax.axis_index(core_axis), 2)
    rows, slot_count = plain_ref.shape[0], tile_hbm.shape[0]
    pieces = record_sem.shape[0]
    piece, groups = rows // pieces, slot_count // GROUP

    def record_copy(k):
        span = pl.ds(k * piece, piece)
        return pltpu.make_async_copy(record_hbm.at[:, span, :], record_ref.at[:, span, :], record_sem.at[k])

    def tile_copy(k):
        span = pl.ds(k * GROUP, GROUP)
        return pltpu.make_async_copy(tile_hbm.at[span], tile_ref.at[span], tile_sem.at[k])

    index_copies = [
        pltpu.make_async_copy(source, target, index_sem.at[k])
        for k, (source, target) in enumerate(((row_hbm, row_ref), (col_hbm, col_ref)))
    ]
    for k in range(pieces):
        record_copy(k).start()
    for copy in index_copies:
        copy.start()
    for k in range(groups):
        tile_copy(k).start()
    total_ref[...] = jnp.zeros_like(total_ref)
    for k in range(pieces):
        record_copy(k).wait()
        span = pl.ds(k * piece, piece)
        packed = packed_record(core, record_ref[0, span, :], record_ref[1, span, :])
        put_chunk(packed.astype(BF16), plain_ref, turned_ref, span, -1.0)
    for copy in index_copies:
        copy.wait()
    step = turn_step(tiles, tile_ref, turned_tile_ref, 0, total_ref, plain_ref, turned_ref)
    for k in range(groups):
        tile_copy(k).wait()

        @pl.when(k * GROUP < used_ref[0, 0])
        def _():
            group_of((row_ref.at[0], col_ref.at[0], used_ref.at[0]), k, step)


def turn_step(tiles, tile_ref, turned_tile_ref, begin, total_ref, plain_ref, turned_ref):
    def step(slot, valid, row, col):
        weights = jnp.concatenate([tile_ref[slot, 0].T, tile_ref[slot, 1].T], axis=1)
        turned_tile_ref[begin + slot] = weights
        add_tile(total_ref, weights, plain_ref, turned_ref, row, jnp.where(valid, col, tiles))

    return step


def first_adjoint_kernel(hyd_axis, order, tiles, tile_ref, row_vmem, col_vmem, used_vmem, _, __, own_total_ref, plain_ref, turned_ref, *refs):
    tiles_ref, turned_tile_ref, own_ref, sends = refs[0], refs[1], refs[2], refs[3:-6]
    total_ref, *index, index_sem, tile_sem = refs[-6:]
    copies = [
        pltpu.make_async_copy(source, target, index_sem.at[k])
        for k, (source, target) in enumerate(zip((row_vmem, col_vmem, used_vmem), index))
    ]
    for copy in copies:
        copy.start()
    count = tile_ref.shape[0]
    join = pltpu.make_async_copy(tile_ref, tiles_ref.at[pl.ds(count, count)], tile_sem.at[0])
    join.start()
    total_ref[...] = jnp.zeros_like(total_ref)
    for copy in copies:
        copy.wait()
    slots([ref.at[0] for ref in index], turn_step(tiles, tile_ref, turned_tile_ref, count, total_ref, plain_ref, turned_ref))
    give_columns(hyd_axis, order, own_total_ref, total_ref, own_ref, sends)
    join.wait()


def give_columns(hyd_axis, order, first_ref, second_ref, own_ref, sends):
    here = lax.axis_index(hyd_axis)
    part = own_ref.shape[0] // 2
    own_ref[:part, :] = first_ref[spans(part, here), :]
    own_ref[part:, :] = second_ref[spans(part, here), :]
    for send, offset in zip(sends, order):
        there = here ^ offset
        send[:part, :] = first_ref[spans(part, there), :].astype(BF16)
        send[part : 2 * part, :] = second_ref[spans(part, there), :].astype(BF16)


def list_kernel(plans, *refs):
    indices, lists = (refs[:3], refs[3:6]), refs[6:]
    slot_count = refs[0].shape[1]
    square = (slot_count, slot_count)
    down, along = (lax.broadcasted_iota(jnp.int32, square, k) for k in (0, 1))
    here = down == along

    def stand(row):
        return jnp.sum(jnp.where(here, jnp.broadcast_to(row, square), 0.0), axis=1, keepdims=True)

    def count(condition):
        return jnp.sum(jnp.where(condition, 1.0, 0.0), axis=1, keepdims=True)

    for list_ref, (way, groups) in zip(lists, plans):
        wide = lax.broadcasted_iota(jnp.int32, (slot_count, list_ref.shape[1]), 1).astype(F32)
        place = way.source_place()
        keys = []
        for index in indices:
            offset = (index[way.source][...] * way.size // way.part) ^ place
            bucket = jnp.zeros(offset.shape, F32)
            for at, group in enumerate(groups):
                for member in group:
                    bucket = jnp.where(offset == member, float(at), bucket)
            used = along[:1, :] < jnp.broadcast_to(index[2][...], (1, slot_count))
            bucket = jnp.where(used, bucket, float(len(groups)))
            keys.append((jnp.broadcast_to(bucket, square), stand(bucket)))
        rows = [jnp.zeros((1, list_ref.shape[1]), F32) for _ in range(4)]
        for k, index in enumerate(indices):
            (key, key_down), (other, _) = keys[k], keys[1 - k]
            place_down = count((key < key_down) | ((key == key_down) & (along < down)))
            place_down += count(other <= key_down) if k else count(other < key_down)
            source = index[way.source][...].astype(F32) + float(k * (way.halves - 1) * (way.length // way.size))
            target = index[1 - way.source][...].astype(F32) + float(k * way.target_shift)
            slot = (down[:, :1] + k * slot_count).astype(F32)
            found = place_down == wide
            for at, value in ((0, slot), (2, stand(source)), (3, stand(target))):
                rows[at] = rows[at] + jnp.sum(jnp.where(found, value, 0.0), axis=0, keepdims=True)
            rows[1] = rows[1] + jnp.sum(jnp.where(key_down < wide, 1.0, 0.0), axis=0, keepdims=True)
        for at, row in enumerate(rows):
            list_ref[at : at + 1, :] = row.astype(jnp.int32)


def step_kernel(way, pick, at_group, last, *refs):
    (tile_ref, list_ref), refs = refs[:2], refs[2:]
    chunks, refs = refs[: len(pick)], refs[len(pick) :]
    if at_group:
        folded, refs = refs[1][...], refs[2:]
    total_ref, refs = refs[0], refs[1:]
    here, there = way.source_place(), way.target_place()
    if not at_group:
        total_ref[...] = jnp.zeros_like(total_ref)
        folded = jnp.zeros((8, total_ref.shape[-1]), F32)
    plain_ref, turned_ref = refs[-2:]
    for chunk, offset in zip(chunks, pick):
        for half in range(way.halves):
            at = pl.ds(pl.multiple_of((here ^ offset) * way.part + half * way.length, way.part), way.part)
            folded += put_chunk(chunk[half * way.part : (half + 1) * way.part, :], plain_ref, turned_ref, at, way.sign)
    low, high = list_ref[1, at_group], list_ref[1, at_group + 1]
    width = min(LAST_WIDTH * len(pick), 2 * LAST_WIDTH) if last else WIDTH

    def turn_of(group, carry):
        for lane in range(width):
            at = low + group * width + lane
            target = jnp.where(at < high, list_ref[3, at], way.spare)
            span = spans(way.size, list_ref[2, at])
            right = jnp.concatenate([plain_ref[span, :], turned_ref[span, :]], axis=0)
            goal = spans(way.size, target)
            product = jnp.dot(way.weights(tile_ref, list_ref[0, at]), right, preferred_element_type=F32)
            total_ref[goal, :] = total_ref[goal, :] + product
        return carry

    lax.fori_loop(0, (high - low + width - 1) // width, turn_of, 0)
    if not last:
        refs[0][...] = folded
        return
    own_ref, norm_ref, sends = refs[0], refs[1], refs[2 : 2 + len(way.send_order)]
    norm = rows_of_norm(folded)
    norm_ref[...] = norm
    tail = norm_tail(norm)
    part = way.target_part
    for j, begin in enumerate(way.target_begins):
        def piece(position):
            return total_ref[pl.ds(pl.multiple_of(position * part + begin, part), part), :]

        own_ref[j * part : (j + 1) * part, :] = piece(there)
        for send, offset in zip(sends, way.send_order):
            send[j * part : (j + 1) * part, :] = piece(there ^ offset).astype(BF16)
    for send in sends:
        send[len(way.target_begins) * part :, :] = tail


def summed(own_ref, others):
    value = own_ref[...]
    for other in others:
        value = value + other[: own_ref.shape[0], :].astype(F32)
    return value


def norm_sum(own_norm, others, size):
    norm = own_norm
    for other in others:
        norm = norm + norm_from(other[size:, :])
    return norm


def start_kernel(others, own_ref, *refs):
    gradient = summed(own_ref, refs[:others])
    refs[-2][...] = gradient
    refs[-1][...] = gradient.astype(BF16)


def image_kernel(others, later, last, own_ref, norm_ref, *refs):
    ins, refs = refs[:others], refs[others:]
    image = summed(own_ref, ins)
    gamma = norm_sum(norm_ref[...], ins, own_ref.shape[0])
    if later:
        before_ref, gamma_ref = refs[:2]
        beta = gamma / (gamma_ref[...] + EPSILON)
        image = image + beta[:1] * before_ref[...]
        refs = refs[2:]
        refs[2][...] = beta
    refs[0][...] = image.astype(BF16)
    refs[1][...] = gamma
    if not last:
        refs[-1][...] = image


def gradient_kernel(others, own_ref, norm_ref, *refs):
    ins, (before_ref, gamma_ref, narrow_ref, alpha_ref, *wide) = refs[:others], refs[others:]
    change = summed(own_ref, ins)
    alpha = gamma_ref[...] / (norm_sum(norm_ref[...], ins, own_ref.shape[0]) + EPSILON)
    gradient = before_ref[...] - alpha[:1] * change
    narrow_ref[...] = gradient.astype(BF16)
    alpha_ref[...] = alpha
    for wide_ref in wide:
        wide_ref[...] = gradient


def norm_kernel(*refs):
    folded = sum(fold_squares(chunk[...].astype(F32)) for chunk in refs[:-1])
    refs[-1][...] = rows_of_norm(folded)


def answer_kernel(hyd_axis, core_axis, g_order, image_order, record_ref, gamma_ref, *refs):
    norms = len(g_order)
    norm = refs[0][...]
    for other in refs[1:norms]:
        norm = norm + other[...]
    refs = refs[norms:]
    alphas = [ref[...] for ref in refs[: ITERS - 1]] + [gamma_ref[...] / (norm + EPSILON)]
    refs = refs[ITERS - 1 :]
    betas = [ref[...] for ref in refs[: ITERS - 1]]
    refs = refs[ITERS - 1 :]
    g_count, image_count = ITERS * len(g_order), ITERS * len(image_order)
    g_chunks, images, (own_x, pair_x, wide_r, narrow_r) = refs[:g_count], refs[g_count : g_count + image_count], refs[g_count + image_count :]
    weights = [None] * ITERS
    weights[-1] = alphas[-1]
    for k in range(ITERS - 2, -1, -1):
        weights[k] = alphas[k] + betas[k] * weights[k + 1]
    core = lax.rem(lax.axis_index(core_axis), 2)
    here = lax.axis_index(hyd_axis)
    for at, offset in enumerate(g_order):
        mine = g_chunks[at :: len(g_order)]
        part = mine[0].shape[0] // 2
        span = spans(part, here ^ offset)
        own_x[span, :] = sum(w[:1] * g[:part, :].astype(F32) for w, g in zip(weights, mine))
        pair_x[span, :] = sum(w[:1] * g[part:, :].astype(F32) for w, g in zip(weights, mine)).astype(BF16)
    here = lax.axis_index(core_axis) // 2
    for at, offset in enumerate(image_order):
        mine = images[at :: len(image_order)]
        span = spans(mine[0].shape[0], here ^ offset)
        residual = packed_record(core, record_ref[0, span, :], record_ref[1, span, :])
        for alpha, image in zip(alphas, mine):
            residual = residual - alpha[:1] * image[...].astype(F32)
        wide_r[span, :] = residual
        narrow_r[span, :] = residual.astype(BF16)


def unpack_kernel(core_axis, own_x, own_r, pair_x, pair_r, x_hbm, r_hbm, x_ref, r_ref, sems):
    core = lax.rem(lax.axis_index(core_axis), 2)
    copies = []
    for k, (own, pair, out, target) in enumerate(((own_x, pair_x, x_ref, x_hbm), (own_r, pair_r, r_ref, r_hbm))):
        piece = own.shape[0] // sems.shape[1]
        for j in range(sems.shape[1]):
            span = pl.ds(j * piece, piece)
            mine, theirs = own[span, :], pair[span, :].astype(F32)
            first = jnp.where(core == 0, mine, theirs)
            second = jnp.where(core == 0, theirs, mine)
            low = low_half(mine.shape)
            out[0, span, :] = jnp.where(low, first, turn(second))
            out[1, span, :] = jnp.where(low, turn(first), second)
            copies.append(pltpu.make_async_copy(out.at[:, span, :], target.at[:, span, :], sems.at[k, j]))
            copies[-1].start()
    for copy in copies:
        copy.wait()


def solution(mesh):
    hyds, srcs = mesh.shape["hyd"], mesh.shape["src"]
    zs = srcs // 2

    def swap(value, axis, size, offset):
        return lax.ppermute(value, axis, [(i, i ^ offset) for i in range(size)])

    hyd_order = tuple(range(1, hyds))
    z_order = (zs - 1, *range(1, zs - 1))

    def over_hyd(values, order):
        return [swap(v, "hyd", hyds, o) for v, o in zip(values, order)]

    def over_z(values, order):
        return [swap(v, "src", srcs, 2 * o) for v, o in zip(values, order)]

    def groups_of(order, way):
        half = len(order) // 2
        if way.part % way.size:
            return (order,)
        return (order[:1], order[1:half], order[half:-1], order[-1:]) if way.halves == 2 else (order[:1], order[1:half], order[half:])

    def body(record, tile_data, tile_rows, tile_cols, tile_counts):
        own_tiles = tile_data[0, 0]
        slot_count, _, size, _ = own_tiles.shape
        rows, shots = record.shape[1:]
        cols = 2 * SRC_DEV
        row_tiles, col_tiles = rows // size, cols // size
        row_part, col_part = rows // zs, cols // hyds
        norm = ((8, shots), F32)
        row_sends = [((row_part + TAIL, shots), BF16)] * (zs - 1)
        col_sends = [((2 * col_part + TAIL, shots), BF16)] * (hyds - 1)
        col_total = ((cols + size, shots), F32)
        vector = lambda n, dtype: ((n, shots), dtype)

        pair_tiles = swap(own_tiles, "src", srcs, 1)
        index = (tile_rows[0], tile_cols[0], jnp.broadcast_to(tile_counts, tile_rows.shape[1:]))
        pair_index = tuple(swap(v, "src", srcs, 1) for v in index)
        pieces, groups = 4, slot_count // GROUP
        table = [(v.shape, jnp.int32) for v in index]
        joined = [((2 * slot_count, 2, size, size), BF16), ((2 * slot_count, size, 2 * size), BF16)]
        both_tiles, both_turned, total, plain, turned = call(
            functools.partial(pack_kernel, "src", col_tiles), "pack",
            [*joined, col_total, vector(rows, BF16), vector(rows, BF16)],
            [(record.shape, F32)] + table[:2] + [(n, pltpu.SemaphoreType.DMA) for n in (pieces, groups, 2)],
            record, own_tiles, *index, away=4,
        )
        both_tiles, both_turned, own, *sends = call(
            functools.partial(first_adjoint_kernel, "hyd", hyd_order, col_tiles), "first_adjoint",
            [*joined, vector(2 * col_part, F32)] + [vector(2 * col_part, BF16)] * (hyds - 1),
            [col_total] + table + [(len(table), pltpu.SemaphoreType.DMA), (1, pltpu.SemaphoreType.DMA)],
            pair_tiles, *(pltpu.with_memory_space_constraint(v, pltpu.VMEM) for v in pair_index),
            both_tiles, both_turned, total, plain, turned, vector=True, alias={4: 0, 5: 1},
        )
        gradient, narrow = call(
            functools.partial(start_kernel, hyds - 1), "start",
            [vector(2 * col_part, F32), vector(2 * col_part, BF16)], [],
            own, *over_hyd(sends, hyd_order),
        )

        hyd_place = lambda: lax.axis_index("hyd")
        z_place = lambda: lax.axis_index("src") // 2
        flat = lambda tile_ref, slot: jnp.concatenate([tile_ref[slot, 0], tile_ref[slot, 1]], axis=1)
        forward = Way(1, 1.0, size, col_part, 2, cols, row_part, (0,), 0, row_tiles, z_order, hyd_place, z_place, flat)
        adjoint = Way(
            0, -1.0, size, row_part, 1, rows, col_part, (0, cols), col_tiles, 2 * col_tiles, hyd_order,
            z_place, hyd_place, lambda tile_ref, slot: tile_ref[slot],
        )
        g_order, image_order = (0, *hyd_order), (0, *z_order)
        g_groups, image_groups = (groups_of(order, w) for order, w in ((g_order, forward), (image_order, adjoint)))
        lists = call(
            functools.partial(list_kernel, ((forward, g_groups), (adjoint, image_groups))),
            "lists", [((8, 128), jnp.int32)] * 2, [], *index, *pair_index, vector=True,
        )

        def apply(way, name, tiles, slot_list, chunks, groups, outs):
            total = (((len(way.target_begins) * (way.spare // len(way.target_begins)) + 1) * size, shots), F32)
            carry, at = [], 0
            for k, group in enumerate(groups):
                last = k + 1 == len(groups)
                carry = call(
                    functools.partial(step_kernel, way, group, k, last), name,
                    [total] + (outs if last else [norm]), [vector(way.halves * way.length, BF16)] * 2,
                    tiles, slot_list, *chunks[at : at + len(group)], *carry,
                    alias={2 + len(group): 0} if k else None,
                )
                at += len(group)
            return carry[1:]

        alphas, betas, g_chunks, images = [], [], [], []
        image = gamma = None
        for step in range(ITERS):
            last = step + 1 == ITERS
            chunks = [narrow, *over_hyd([narrow] * (hyds - 1), g_order[1:])]
            g_chunks += chunks
            own, own_norm, *sends = apply(
                forward, "forward", both_tiles, lists[0], chunks, g_groups, [vector(row_part, F32), norm] + row_sends
            )
            narrow, gamma, *more = call(
                functools.partial(image_kernel, zs - 1, step > 0, last), "image",
                [vector(row_part, BF16), norm] + [norm] * (step > 0) + [vector(row_part, F32)] * (not last), [],
                own, own_norm, *over_z(sends, z_order), *([image, gamma] if step else []),
            )
            image = None if last else more.pop()
            betas += more
            chunks = [narrow, *over_z([narrow] * (zs - 1), image_order[1:])]
            images += chunks
            if last:
                break
            own, own_norm, *sends = apply(
                adjoint, "adjoint", both_turned, lists[1], chunks, image_groups, [vector(2 * col_part, F32), norm] + col_sends
            )
            more_steps = step + 2 < ITERS
            narrow, alpha, *wide = call(
                functools.partial(gradient_kernel, hyds - 1), "gradient",
                [vector(2 * col_part, BF16), norm] + [vector(2 * col_part, F32)] * more_steps, [],
                own, own_norm, *over_hyd(sends, hyd_order), gradient, gamma,
            )
            gradient = wide[0] if more_steps else None
            alphas.append(alpha)

        (own_norm,) = call(norm_kernel, "norm", [norm], [], *chunks)
        norms = [own_norm] + over_hyd([own_norm] * (hyds - 1), hyd_order)
        own_x, pair_x, wide_r, narrow_r = call(
            functools.partial(answer_kernel, "hyd", "src", g_order, image_order), "answer",
            [vector(cols, F32), vector(cols, BF16), vector(rows, F32), vector(rows, BF16)], [],
            record, gamma, *norms, *alphas, *betas, *g_chunks, *images,
        )
        return call(
            functools.partial(unpack_kernel, "src"), "unpack",
            [((2, cols, shots), F32), ((2, rows, shots), F32)],
            [((2, cols, shots), F32), ((2, rows, shots), F32), ((2, 4), pltpu.SemaphoreType.DMA)],
            own_x, wide_r, swap(pair_x, "src", srcs, 1), swap(narrow_r, "src", srcs, 1), out_space=pltpu.HBM,
        )

    in_specs = (
        P(None, "hyd", None),
        P("hyd", "src", None, None, None, None),
        P("hyd", "src", None),
        P("hyd", "src", None),
        P("hyd", "src"),
    )
    out_specs = (P(None, "src", None), P(None, "hyd", None))
    return jax.shard_map(body, mesh=mesh, in_specs=in_specs, out_specs=out_specs, check_vma=False)
```

```python
import functools
from typing import NamedTuple

import jax
import jax.numpy as jnp
from jax import lax
from jax.experimental import pallas as pl
from jax.experimental.pallas import tpu as pltpu
from jax.sharding import PartitionSpec as P

SRC_DEV = 512
ITERS = 3
EPSILON = 1e-06
GROUP = 8
WIDTH = 8
LAST_WIDTH = 12
TAIL = 16
VMEM_BYTES = 16 << 20

F32 = jnp.float32
BF16 = jnp.bfloat16


class Way(NamedTuple):
    source: int
    sign: float
    size: int
    part: int
    halves: int
    length: int
    target_part: int
    target_begins: tuple
    target_shift: int
    spare: int
    send_order: tuple
    source_place: object
    target_place: object
    weights: object


def call(kernel, name, outs, scratch, *ins, vector=False, alias=None, away=0, out_space=pltpu.VMEM):
    def space(place, dtype):
        if place < away:
            return pltpu.HBM
        return pltpu.SMEM if dtype == jnp.int32 and not vector else pltpu.VMEM

    def room(shape, dtype):
        if dtype is pltpu.SemaphoreType.DMA:
            return dtype(shape if isinstance(shape, tuple) else (shape,))
        return (pltpu.SMEM if dtype == jnp.int32 else pltpu.VMEM)(shape, dtype)

    return pl.pallas_call(
        kernel,
        name=name,
        out_shape=[jax.ShapeDtypeStruct(s, d) for s, d in outs],
        in_specs=[pl.BlockSpec(memory_space=space(i, a.dtype)) for i, a in enumerate(ins)],
        out_specs=[pl.BlockSpec(memory_space=out_space) for _ in outs],
        scratch_shapes=[room(s, d) for s, d in scratch],
        input_output_aliases=alias or {},
        compiler_params=pltpu.CompilerParams(vmem_limit_bytes=VMEM_BYTES),
    )(*[pltpu.with_memory_space_constraint(a, pltpu.HBM) if i < away else a for i, a in enumerate(ins)])


def low_half(shape):
    return lax.broadcasted_iota(jnp.int32, shape, len(shape) - 1) < shape[-1] // 2


def turn(value):
    return pltpu.roll(value, value.shape[-1] // 2, value.ndim - 1)


def times_i(value, sign):
    rolled = turn(value)
    return jnp.where(low_half(value.shape), -sign * rolled, sign * rolled)


def both_parts(row):
    return row + turn(row)


def fold_squares(value):
    return jnp.sum((value * value).reshape(-1, 8, value.shape[-1]), axis=0)


def rows_of_norm(folded):
    row = both_parts(jnp.sum(folded, axis=0, keepdims=True))
    return jnp.broadcast_to(row, (8, folded.shape[-1]))


def norm_tail(norm):
    row = jnp.broadcast_to(norm[:1], (TAIL, norm.shape[-1]))
    high = row.astype(BF16).astype(F32)
    at = lax.broadcasted_iota(jnp.int32, row.shape, 0)
    return jnp.where(at == 0, high, jnp.where(at == 1, row - high, 0.0)).astype(BF16)


def norm_from(tail):
    tail = tail.astype(F32)
    return jnp.broadcast_to(tail[:1] + tail[1:2], (8, tail.shape[-1]))


def spans(size, count):
    return pl.ds(pl.multiple_of(count * size, size), size)


def group_of(index, group, step):
    for lane in range(GROUP):
        slot = group * GROUP + lane
        step(slot, slot < index[2][0], index[0][slot], index[1][slot])


def slots(index, step):
    def turn_of(group, carry):
        group_of(index, group, step)
        return carry

    lax.fori_loop(0, (index[2][0] + GROUP - 1) // GROUP, turn_of, 0)


def add_tile(acc_ref, weights, plain_ref, turned_ref, source, target):
    size = weights.shape[0]
    right = jnp.concatenate([plain_ref[spans(size, source), :], turned_ref[spans(size, source), :]], axis=0)
    at = spans(size, target)
    acc_ref[at, :] = acc_ref[at, :] + jnp.dot(weights, right, preferred_element_type=F32)


def put_chunk(chunk, plain_ref, turned_ref, at, sign):
    wide = chunk.astype(F32)
    plain_ref[at, :] = chunk
    turned_ref[at, :] = times_i(wide, sign).astype(BF16)
    return fold_squares(wide)


def packed_record(core, real, imag):
    first = jnp.where(core == 0, real, turn(real))
    second = jnp.where(core == 0, turn(imag), imag)
    return jnp.where(low_half(real.shape), first, second)


def pack_kernel(core_axis, tiles, record_hbm, tile_hbm, row_hbm, col_hbm, used_ref, *refs):
    tile_ref, turned_tile_ref, total_ref, plain_ref, turned_ref, record_ref, row_ref, col_ref, record_sem, tile_sem, index_sem = refs
    core = lax.rem(lax.axis_index(core_axis), 2)
    rows, slot_count = plain_ref.shape[0], tile_hbm.shape[0]
    pieces = record_sem.shape[0]
    piece, groups = rows // pieces, slot_count // GROUP

    def record_copy(k):
        span = pl.ds(k * piece, piece)
        return pltpu.make_async_copy(record_hbm.at[:, span, :], record_ref.at[:, span, :], record_sem.at[k])

    def tile_copy(k):
        span = pl.ds(k * GROUP, GROUP)
        return pltpu.make_async_copy(tile_hbm.at[span], tile_ref.at[span], tile_sem.at[k])

    index_copies = [
        pltpu.make_async_copy(source, target, index_sem.at[k])
        for k, (source, target) in enumerate(((row_hbm, row_ref), (col_hbm, col_ref)))
    ]
    for k in range(pieces):
        record_copy(k).start()
    for copy in index_copies:
        copy.start()
    for k in range(groups):
        tile_copy(k).start()
    total_ref[...] = jnp.zeros_like(total_ref)
    for k in range(pieces):
        record_copy(k).wait()
        span = pl.ds(k * piece, piece)
        packed = packed_record(core, record_ref[0, span, :], record_ref[1, span, :])
        put_chunk(packed.astype(BF16), plain_ref, turned_ref, span, -1.0)
    for copy in index_copies:
        copy.wait()
    step = turn_step(tiles, tile_ref, turned_tile_ref, 0, total_ref, plain_ref, turned_ref)
    for k in range(groups):
        tile_copy(k).wait()

        @pl.when(k * GROUP < used_ref[0, 0])
        def _():
            group_of((row_ref.at[0], col_ref.at[0], used_ref.at[0]), k, step)


def turn_step(tiles, tile_ref, turned_tile_ref, begin, total_ref, plain_ref, turned_ref):
    def step(slot, valid, row, col):
        weights = jnp.concatenate([tile_ref[slot, 0].T, tile_ref[slot, 1].T], axis=1)
        turned_tile_ref[begin + slot] = weights
        add_tile(total_ref, weights, plain_ref, turned_ref, row, jnp.where(valid, col, tiles))

    return step


def first_adjoint_kernel(hyd_axis, order, tiles, tile_ref, row_vmem, col_vmem, used_vmem, _, __, own_total_ref, plain_ref, turned_ref, *refs):
    tiles_ref, turned_tile_ref, own_ref, sends = refs[0], refs[1], refs[2], refs[3:-6]
    total_ref, *index, index_sem, tile_sem = refs[-6:]
    copies = [
        pltpu.make_async_copy(source, target, index_sem.at[k])
        for k, (source, target) in enumerate(zip((row_vmem, col_vmem, used_vmem), index))
    ]
    for copy in copies:
        copy.start()
    count = tile_ref.shape[0]
    join = pltpu.make_async_copy(tile_ref, tiles_ref.at[pl.ds(count, count)], tile_sem.at[0])
    join.start()
    total_ref[...] = jnp.zeros_like(total_ref)
    for copy in copies:
        copy.wait()
    slots([ref.at[0] for ref in index], turn_step(tiles, tile_ref, turned_tile_ref, count, total_ref, plain_ref, turned_ref))
    give_columns(hyd_axis, order, own_total_ref, total_ref, own_ref, sends)
    join.wait()


def give_columns(hyd_axis, order, first_ref, second_ref, own_ref, sends):
    here = lax.axis_index(hyd_axis)
    part = own_ref.shape[0] // 2
    own_ref[:part, :] = first_ref[spans(part, here), :]
    own_ref[part:, :] = second_ref[spans(part, here), :]
    for send, offset in zip(sends, order):
        there = here ^ offset
        send[:part, :] = first_ref[spans(part, there), :].astype(BF16)
        send[part : 2 * part, :] = second_ref[spans(part, there), :].astype(BF16)


def list_kernel(plans, *refs):
    indices, lists = (refs[:3], refs[3:6]), refs[6:]
    slot_count = refs[0].shape[1]
    square = (slot_count, slot_count)
    down, along = (lax.broadcasted_iota(jnp.int32, square, k) for k in (0, 1))
    here = down == along

    def stand(row):
        return jnp.sum(jnp.where(here, jnp.broadcast_to(row, square), 0.0), axis=1, keepdims=True)

    def count(condition):
        return jnp.sum(jnp.where(condition, 1.0, 0.0), axis=1, keepdims=True)

    for list_ref, (way, groups) in zip(lists, plans):
        wide = lax.broadcasted_iota(jnp.int32, (slot_count, list_ref.shape[1]), 1).astype(F32)
        place = way.source_place()
        keys = []
        for index in indices:
            offset = (index[way.source][...] * way.size // way.part) ^ place
            bucket = jnp.zeros(offset.shape, F32)
            for at, group in enumerate(groups):
                for member in group:
                    bucket = jnp.where(offset == member, float(at), bucket)
            used = along[:1, :] < jnp.broadcast_to(index[2][...], (1, slot_count))
            bucket = jnp.where(used, bucket, float(len(groups)))
            keys.append((jnp.broadcast_to(bucket, square), stand(bucket)))
        rows = [jnp.zeros((1, list_ref.shape[1]), F32) for _ in range(4)]
        for k, index in enumerate(indices):
            (key, key_down), (other, _) = keys[k], keys[1 - k]
            place_down = count((key < key_down) | ((key == key_down) & (along < down)))
            place_down += count(other <= key_down) if k else count(other < key_down)
            source = index[way.source][...].astype(F32) + float(k * (way.halves - 1) * (way.length // way.size))
            target = index[1 - way.source][...].astype(F32) + float(k * way.target_shift)
            slot = (down[:, :1] + k * slot_count).astype(F32)
            found = place_down == wide
            for at, value in ((0, slot), (2, stand(source)), (3, stand(target))):
                rows[at] = rows[at] + jnp.sum(jnp.where(found, value, 0.0), axis=0, keepdims=True)
            rows[1] = rows[1] + jnp.sum(jnp.where(key_down < wide, 1.0, 0.0), axis=0, keepdims=True)
        for at, row in enumerate(rows):
            list_ref[at : at + 1, :] = row.astype(jnp.int32)


def step_kernel(way, pick, at_group, last, *refs):
    (tile_ref, list_vmem), refs, (list_ref, list_sem) = refs[:2], refs[2:-2], refs[-2:]
    fetch = pltpu.make_async_copy(list_vmem, list_ref, list_sem.at[0])
    fetch.start()
    chunks, refs = refs[: len(pick)], refs[len(pick) :]
    if at_group:
        folded, refs = refs[1][...], refs[2:]
    total_ref, refs = refs[0], refs[1:]
    here, there = way.source_place(), way.target_place()
    if not at_group:
        total_ref[...] = jnp.zeros_like(total_ref)
        folded = jnp.zeros((8, total_ref.shape[-1]), F32)
    plain_ref, turned_ref = refs[-2:]
    for chunk, offset in zip(chunks, pick):
        for half in range(way.halves):
            at = pl.ds(pl.multiple_of((here ^ offset) * way.part + half * way.length, way.part), way.part)
            folded += put_chunk(chunk[half * way.part : (half + 1) * way.part, :], plain_ref, turned_ref, at, way.sign)
    fetch.wait()
    low, high = list_ref[1, at_group], list_ref[1, at_group + 1]
    width = LAST_WIDTH if last else WIDTH

    def turn_of(group, carry):
        for lane in range(width):
            at = low + group * width + lane
            target = jnp.where(at < high, list_ref[3, at], way.spare)
            span = spans(way.size, list_ref[2, at])
            right = jnp.concatenate([plain_ref[span, :], turned_ref[span, :]], axis=0)
            goal = spans(way.size, target)
            product = jnp.dot(way.weights(tile_ref, list_ref[0, at]), right, preferred_element_type=F32)
            total_ref[goal, :] = total_ref[goal, :] + product
        return carry

    lax.fori_loop(0, (high - low + width - 1) // width, turn_of, 0)
    if not last:
        refs[0][...] = folded
        return
    own_ref, norm_ref, sends = refs[0], refs[1], refs[2 : 2 + len(way.send_order)]
    norm = rows_of_norm(folded)
    norm_ref[...] = norm
    tail = norm_tail(norm)
    part = way.target_part
    for j, begin in enumerate(way.target_begins):
        def piece(position):
            return total_ref[pl.ds(pl.multiple_of(position * part + begin, part), part), :]

        own_ref[j * part : (j + 1) * part, :] = piece(there)
        for send, offset in zip(sends, way.send_order):
            send[j * part : (j + 1) * part, :] = piece(there ^ offset).astype(BF16)
    for send in sends:
        send[len(way.target_begins) * part :, :] = tail


def summed(own_ref, others):
    value = own_ref[...]
    for other in others:
        value = value + other[: own_ref.shape[0], :].astype(F32)
    return value


def norm_sum(own_norm, others, size):
    norm = own_norm
    for other in others:
        norm = norm + norm_from(other[size:, :])
    return norm


def start_kernel(others, own_ref, *refs):
    gradient = summed(own_ref, refs[:others])
    refs[-2][...] = gradient
    refs[-1][...] = gradient.astype(BF16)


def image_kernel(others, later, last, own_ref, norm_ref, *refs):
    ins, refs = refs[:others], refs[others:]
    image = summed(own_ref, ins)
    gamma = norm_sum(norm_ref[...], ins, own_ref.shape[0])
    if later:
        before_ref, gamma_ref = refs[:2]
        beta = gamma / (gamma_ref[...] + EPSILON)
        image = image + beta[:1] * before_ref[...]
        refs = refs[2:]
        refs[2][...] = beta
    refs[0][...] = image.astype(BF16)
    refs[1][...] = gamma
    if not last:
        refs[-1][...] = image


def gradient_kernel(others, own_ref, norm_ref, *refs):
    ins, (before_ref, gamma_ref, narrow_ref, alpha_ref, *wide) = refs[:others], refs[others:]
    change = summed(own_ref, ins)
    alpha = gamma_ref[...] / (norm_sum(norm_ref[...], ins, own_ref.shape[0]) + EPSILON)
    gradient = before_ref[...] - alpha[:1] * change
    narrow_ref[...] = gradient.astype(BF16)
    alpha_ref[...] = alpha
    for wide_ref in wide:
        wide_ref[...] = gradient


def norm_kernel(*refs):
    folded = sum(fold_squares(chunk[...].astype(F32)) for chunk in refs[:-1])
    refs[-1][...] = rows_of_norm(folded)


def answer_kernel(hyd_axis, core_axis, g_order, image_order, record_ref, gamma_ref, *refs):
    norms = len(g_order)
    norm = refs[0][...]
    for other in refs[1:norms]:
        norm = norm + other[...]
    refs = refs[norms:]
    alphas = [ref[...] for ref in refs[: ITERS - 1]] + [gamma_ref[...] / (norm + EPSILON)]
    refs = refs[ITERS - 1 :]
    betas = [ref[...] for ref in refs[: ITERS - 1]]
    refs = refs[ITERS - 1 :]
    g_count, image_count = ITERS * len(g_order), ITERS * len(image_order)
    g_chunks, images, (own_x, pair_x, wide_r, narrow_r) = refs[:g_count], refs[g_count : g_count + image_count], refs[g_count + image_count :]
    weights = [None] * ITERS
    weights[-1] = alphas[-1]
    for k in range(ITERS - 2, -1, -1):
        weights[k] = alphas[k] + betas[k] * weights[k + 1]
    core = lax.rem(lax.axis_index(core_axis), 2)
    here = lax.axis_index(hyd_axis)
    for at, offset in enumerate(g_order):
        mine = g_chunks[at :: len(g_order)]
        part = mine[0].shape[0] // 2
        span = spans(part, here ^ offset)
        own_x[span, :] = sum(w[:1] * g[:part, :].astype(F32) for w, g in zip(weights, mine))
        pair_x[span, :] = sum(w[:1] * g[part:, :].astype(F32) for w, g in zip(weights, mine)).astype(BF16)
    here = lax.axis_index(core_axis) // 2
    for at, offset in enumerate(image_order):
        mine = images[at :: len(image_order)]
        span = spans(mine[0].shape[0], here ^ offset)
        residual = packed_record(core, record_ref[0, span, :], record_ref[1, span, :])
        for alpha, image in zip(alphas, mine):
            residual = residual - alpha[:1] * image[...].astype(F32)
        wide_r[span, :] = residual
        narrow_r[span, :] = residual.astype(BF16)


def unpack_kernel(core_axis, own_x, own_r, pair_x, pair_r, x_hbm, r_hbm, x_ref, r_ref, sems):
    core = lax.rem(lax.axis_index(core_axis), 2)
    copies = []
    for k, (own, pair, out, target) in enumerate(((own_x, pair_x, x_ref, x_hbm), (own_r, pair_r, r_ref, r_hbm))):
        piece = own.shape[0] // sems.shape[1]
        for j in range(sems.shape[1]):
            span = pl.ds(j * piece, piece)
            mine, theirs = own[span, :], pair[span, :].astype(F32)
            first = jnp.where(core == 0, mine, theirs)
            second = jnp.where(core == 0, theirs, mine)
            low = low_half(mine.shape)
            out[0, span, :] = jnp.where(low, first, turn(second))
            out[1, span, :] = jnp.where(low, turn(first), second)
            copies.append(pltpu.make_async_copy(out.at[:, span, :], target.at[:, span, :], sems.at[k, j]))
            copies[-1].start()
    for copy in copies:
        copy.wait()


def solution(mesh):
    hyds, srcs = mesh.shape["hyd"], mesh.shape["src"]
    zs = srcs // 2

    def swap(value, axis, size, offset):
        return lax.ppermute(value, axis, [(i, i ^ offset) for i in range(size)])

    hyd_order = tuple(range(1, hyds))
    z_order = (zs - 1, *range(1, zs - 1))

    def over_hyd(values, order):
        return [swap(v, "hyd", hyds, o) for v, o in zip(values, order)]

    def over_z(values, order):
        return [swap(v, "src", srcs, 2 * o) for v, o in zip(values, order)]

    def groups_of(order, way):
        half = len(order) // 2
        return (order[:1], order[1:half], order[half:]) if way.part % way.size == 0 else (order,)

    def body(record, tile_data, tile_rows, tile_cols, tile_counts):
        own_tiles = tile_data[0, 0]
        slot_count, _, size, _ = own_tiles.shape
        rows, shots = record.shape[1:]
        cols = 2 * SRC_DEV
        row_tiles, col_tiles = rows // size, cols // size
        row_part, col_part = rows // zs, cols // hyds
        norm = ((8, shots), F32)
        row_sends = [((row_part + TAIL, shots), BF16)] * (zs - 1)
        col_sends = [((2 * col_part + TAIL, shots), BF16)] * (hyds - 1)
        col_total = ((cols + size, shots), F32)
        vector = lambda n, dtype: ((n, shots), dtype)

        pair_tiles = swap(own_tiles, "src", srcs, 1)
        index = (tile_rows[0], tile_cols[0], jnp.broadcast_to(tile_counts, tile_rows.shape[1:]))
        pair_index = tuple(swap(v, "src", srcs, 1) for v in index)
        pieces, groups = 4, slot_count // GROUP
        table = [(v.shape, jnp.int32) for v in index]
        joined = [((2 * slot_count, 2, size, size), BF16), ((2 * slot_count, size, 2 * size), BF16)]
        both_tiles, both_turned, total, plain, turned = call(
            functools.partial(pack_kernel, "src", col_tiles), "pack",
            [*joined, col_total, vector(rows, BF16), vector(rows, BF16)],
            [(record.shape, F32)] + table[:2] + [(n, pltpu.SemaphoreType.DMA) for n in (pieces, groups, 2)],
            record, own_tiles, *index, away=4,
        )
        both_tiles, both_turned, own, *sends = call(
            functools.partial(first_adjoint_kernel, "hyd", hyd_order, col_tiles), "first_adjoint",
            [*joined, vector(2 * col_part, F32)] + [vector(2 * col_part, BF16)] * (hyds - 1),
            [col_total] + table + [(len(table), pltpu.SemaphoreType.DMA), (1, pltpu.SemaphoreType.DMA)],
            pair_tiles, *(pltpu.with_memory_space_constraint(v, pltpu.VMEM) for v in pair_index),
            both_tiles, both_turned, total, plain, turned, vector=True, alias={4: 0, 5: 1},
        )
        gradient, narrow = call(
            functools.partial(start_kernel, hyds - 1), "start",
            [vector(2 * col_part, F32), vector(2 * col_part, BF16)], [],
            own, *over_hyd(sends, hyd_order),
        )

        hyd_place = lambda: lax.axis_index("hyd")
        z_place = lambda: lax.axis_index("src") // 2
        flat = lambda tile_ref, slot: jnp.concatenate([tile_ref[slot, 0], tile_ref[slot, 1]], axis=1)
        forward = Way(1, 1.0, size, col_part, 2, cols, row_part, (0,), 0, row_tiles, z_order, hyd_place, z_place, flat)
        adjoint = Way(
            0, -1.0, size, row_part, 1, rows, col_part, (0, cols), col_tiles, 2 * col_tiles, hyd_order,
            z_place, hyd_place, lambda tile_ref, slot: tile_ref[slot],
        )
        g_order, image_order = (0, *hyd_order), (0, *z_order)
        g_groups, image_groups = (groups_of(order, w) for order, w in ((g_order, forward), (image_order, adjoint)))
        lists = call(
            functools.partial(list_kernel, ((forward, g_groups), (adjoint, image_groups))),
            "lists", [((8, 128), jnp.int32)] * 2, [], *index, *pair_index, vector=True,
        )

        def apply(way, name, tiles, slot_list, chunks, groups, outs):
            total = (((len(way.target_begins) * (way.spare // len(way.target_begins)) + 1) * size, shots), F32)
            carry, at = [], 0
            for k, group in enumerate(groups):
                last = k + 1 == len(groups)
                carry = call(
                    functools.partial(step_kernel, way, group, k, last), name,
                    [total] + (outs if last else [norm]),
                    [vector(way.halves * way.length, BF16)] * 2 + [((8, 128), jnp.int32), (1, pltpu.SemaphoreType.DMA)],
                    tiles, slot_list, *chunks[at : at + len(group)], *carry,
                    alias={2 + len(group): 0} if k else None, vector=True,
                )
                at += len(group)
            return carry[1:]

        alphas, betas, g_chunks, images = [], [], [], []
        image = gamma = None
        for step in range(ITERS):
            last = step + 1 == ITERS
            chunks = [narrow, *over_hyd([narrow] * (hyds - 1), g_order[1:])]
            g_chunks += chunks
            own, own_norm, *sends = apply(
                forward, "forward", both_tiles, lists[0], chunks, g_groups, [vector(row_part, F32), norm] + row_sends
            )
            narrow, gamma, *more = call(
                functools.partial(image_kernel, zs - 1, step > 0, last), "image",
                [vector(row_part, BF16), norm] + [norm] * (step > 0) + [vector(row_part, F32)] * (not last), [],
                own, own_norm, *over_z(sends, z_order), *([image, gamma] if step else []),
            )
            image = None if last else more.pop()
            betas += more
            chunks = [narrow, *over_z([narrow] * (zs - 1), image_order[1:])]
            images += chunks
            if last:
                break
            own, own_norm, *sends = apply(
                adjoint, "adjoint", both_turned, lists[1], chunks, image_groups, [vector(2 * col_part, F32), norm] + col_sends
            )
            more_steps = step + 2 < ITERS
            narrow, alpha, *wide = call(
                functools.partial(gradient_kernel, hyds - 1), "gradient",
                [vector(2 * col_part, BF16), norm] + [vector(2 * col_part, F32)] * more_steps, [],
                own, own_norm, *over_hyd(sends, hyd_order), gradient, gamma,
            )
            gradient = wide[0] if more_steps else None
            alphas.append(alpha)

        (own_norm,) = call(norm_kernel, "norm", [norm], [], *chunks)
        norms = [own_norm] + over_hyd([own_norm] * (hyds - 1), hyd_order)
        own_x, pair_x, wide_r, narrow_r = call(
            functools.partial(answer_kernel, "hyd", "src", g_order, image_order), "answer",
            [vector(cols, F32), vector(cols, BF16), vector(rows, F32), vector(rows, BF16)], [],
            record, gamma, *norms, *alphas, *betas, *g_chunks, *images,
        )
        return call(
            functools.partial(unpack_kernel, "src"), "unpack",
            [((2, cols, shots), F32), ((2, rows, shots), F32)],
            [((2, cols, shots), F32), ((2, rows, shots), F32), ((2, 4), pltpu.SemaphoreType.DMA)],
            own_x, wide_r, swap(pair_x, "src", srcs, 1), swap(narrow_r, "src", srcs, 1), out_space=pltpu.HBM,
        )

    in_specs = (
        P(None, "hyd", None),
        P("hyd", "src", None, None, None, None),
        P("hyd", "src", None),
        P("hyd", "src", None),
        P("hyd", "src"),
    )
    out_specs = (P(None, "src", None), P(None, "hyd", None))
    return jax.shard_map(body, mesh=mesh, in_specs=in_specs, out_specs=out_specs, check_vma=False)
```

```python
import functools
from typing import NamedTuple

import jax
import jax.numpy as jnp
from jax import lax
from jax.experimental import pallas as pl
from jax.experimental.pallas import tpu as pltpu
from jax.sharding import PartitionSpec as P

SRC_DEV = 512
ITERS = 3
EPSILON = 1e-06
GROUP = 8
WIDTH = 8
LAST_WIDTH = 24
TAIL = 16
VMEM_BYTES = 16 << 20

F32 = jnp.float32
BF16 = jnp.bfloat16


class Way(NamedTuple):
    source: int
    sign: float
    size: int
    part: int
    halves: int
    length: int
    target_part: int
    target_begins: tuple
    target_shift: int
    spare: int
    send_order: tuple
    source_place: object
    target_place: object
    weights: object


def call(kernel, name, outs, scratch, *ins, vector=False, alias=None, away=0, out_space=pltpu.VMEM):
    def space(place, dtype):
        if place < away:
            return pltpu.HBM
        return pltpu.SMEM if dtype == jnp.int32 and not vector else pltpu.VMEM

    def room(shape, dtype):
        if dtype is pltpu.SemaphoreType.DMA:
            return dtype(shape if isinstance(shape, tuple) else (shape,))
        return (pltpu.SMEM if dtype == jnp.int32 else pltpu.VMEM)(shape, dtype)

    return pl.pallas_call(
        kernel,
        name=name,
        out_shape=[jax.ShapeDtypeStruct(s, d) for s, d in outs],
        in_specs=[pl.BlockSpec(memory_space=space(i, a.dtype)) for i, a in enumerate(ins)],
        out_specs=[pl.BlockSpec(memory_space=out_space) for _ in outs],
        scratch_shapes=[room(s, d) for s, d in scratch],
        input_output_aliases=alias or {},
        compiler_params=pltpu.CompilerParams(vmem_limit_bytes=VMEM_BYTES),
    )(*[pltpu.with_memory_space_constraint(a, pltpu.HBM) if i < away else a for i, a in enumerate(ins)])


def low_half(shape):
    return lax.broadcasted_iota(jnp.int32, shape, len(shape) - 1) < shape[-1] // 2


def turn(value):
    return pltpu.roll(value, value.shape[-1] // 2, value.ndim - 1)


def times_i(value, sign):
    rolled = turn(value)
    return jnp.where(low_half(value.shape), -sign * rolled, sign * rolled)


def both_parts(row):
    return row + turn(row)


def fold_squares(value):
    return jnp.sum((value * value).reshape(-1, 8, value.shape[-1]), axis=0)


def rows_of_norm(folded):
    row = both_parts(jnp.sum(folded, axis=0, keepdims=True))
    return jnp.broadcast_to(row, (8, folded.shape[-1]))


def norm_tail(norm):
    row = jnp.broadcast_to(norm[:1], (TAIL, norm.shape[-1]))
    high = row.astype(BF16).astype(F32)
    at = lax.broadcasted_iota(jnp.int32, row.shape, 0)
    return jnp.where(at == 0, high, jnp.where(at == 1, row - high, 0.0)).astype(BF16)


def norm_from(tail):
    tail = tail.astype(F32)
    return jnp.broadcast_to(tail[:1] + tail[1:2], (8, tail.shape[-1]))


def spans(size, count):
    return pl.ds(pl.multiple_of(count * size, size), size)


def group_of(index, group, step):
    for lane in range(GROUP):
        slot = group * GROUP + lane
        step(slot, slot < index[2][0], index[0][slot], index[1][slot])


def slots(index, step):
    def turn_of(group, carry):
        group_of(index, group, step)
        return carry

    lax.fori_loop(0, (index[2][0] + GROUP - 1) // GROUP, turn_of, 0)


def add_tile(acc_ref, weights, plain_ref, turned_ref, source, target):
    size = weights.shape[0]
    right = jnp.concatenate([plain_ref[spans(size, source), :], turned_ref[spans(size, source), :]], axis=0)
    at = spans(size, target)
    acc_ref[at, :] = acc_ref[at, :] + jnp.dot(weights, right, preferred_element_type=F32)


def put_chunk(chunk, plain_ref, turned_ref, at, sign):
    wide = chunk.astype(F32)
    plain_ref[at, :] = chunk
    turned_ref[at, :] = times_i(wide, sign).astype(BF16)
    return fold_squares(wide)


def packed_record(core, real, imag):
    first = jnp.where(core == 0, real, turn(real))
    second = jnp.where(core == 0, turn(imag), imag)
    return jnp.where(low_half(real.shape), first, second)


def pack_kernel(core_axis, tiles, record_hbm, tile_hbm, row_hbm, col_hbm, used_ref, *refs):
    tile_ref, turned_tile_ref, total_ref, plain_ref, turned_ref, record_ref, row_ref, col_ref, record_sem, tile_sem, index_sem = refs
    core = lax.rem(lax.axis_index(core_axis), 2)
    rows, slot_count = plain_ref.shape[0], tile_hbm.shape[0]
    pieces = record_sem.shape[0]
    piece, groups = rows // pieces, slot_count // GROUP

    def record_copy(k):
        span = pl.ds(k * piece, piece)
        return pltpu.make_async_copy(record_hbm.at[:, span, :], record_ref.at[:, span, :], record_sem.at[k])

    def tile_copy(k):
        span = pl.ds(k * GROUP, GROUP)
        return pltpu.make_async_copy(tile_hbm.at[span], tile_ref.at[span], tile_sem.at[k])

    index_copies = [
        pltpu.make_async_copy(source, target, index_sem.at[k])
        for k, (source, target) in enumerate(((row_hbm, row_ref), (col_hbm, col_ref)))
    ]
    for k in range(pieces):
        record_copy(k).start()
    for copy in index_copies:
        copy.start()
    for k in range(groups):
        tile_copy(k).start()
    total_ref[...] = jnp.zeros_like(total_ref)
    for k in range(pieces):
        record_copy(k).wait()
        span = pl.ds(k * piece, piece)
        packed = packed_record(core, record_ref[0, span, :], record_ref[1, span, :])
        put_chunk(packed.astype(BF16), plain_ref, turned_ref, span, -1.0)
    for copy in index_copies:
        copy.wait()
    step = turn_step(tiles, tile_ref, turned_tile_ref, 0, total_ref, plain_ref, turned_ref)
    for k in range(groups):
        tile_copy(k).wait()

        @pl.when(k * GROUP < used_ref[0, 0])
        def _():
            group_of((row_ref.at[0], col_ref.at[0], used_ref.at[0]), k, step)


def turn_step(tiles, tile_ref, turned_tile_ref, begin, total_ref, plain_ref, turned_ref):
    def step(slot, valid, row, col):
        weights = jnp.concatenate([tile_ref[slot, 0].T, tile_ref[slot, 1].T], axis=1)
        turned_tile_ref[begin + slot] = weights
        add_tile(total_ref, weights, plain_ref, turned_ref, row, jnp.where(valid, col, tiles))

    return step


def first_adjoint_kernel(hyd_axis, order, tiles, tile_ref, row_vmem, col_vmem, used_vmem, _, __, own_total_ref, plain_ref, turned_ref, *refs):
    tiles_ref, turned_tile_ref, own_ref, sends = refs[0], refs[1], refs[2], refs[3:-6]
    total_ref, *index, index_sem, tile_sem = refs[-6:]
    copies = [
        pltpu.make_async_copy(source, target, index_sem.at[k])
        for k, (source, target) in enumerate(zip((row_vmem, col_vmem, used_vmem), index))
    ]
    for copy in copies:
        copy.start()
    count = tile_ref.shape[0]
    join = pltpu.make_async_copy(tile_ref, tiles_ref.at[pl.ds(count, count)], tile_sem.at[0])
    join.start()
    total_ref[...] = jnp.zeros_like(total_ref)
    for copy in copies:
        copy.wait()
    slots([ref.at[0] for ref in index], turn_step(tiles, tile_ref, turned_tile_ref, count, total_ref, plain_ref, turned_ref))
    give_columns(hyd_axis, order, own_total_ref, total_ref, own_ref, sends)
    join.wait()


def give_columns(hyd_axis, order, first_ref, second_ref, own_ref, sends):
    here = lax.axis_index(hyd_axis)
    part = own_ref.shape[0] // 2
    own_ref[:part, :] = first_ref[spans(part, here), :]
    own_ref[part:, :] = second_ref[spans(part, here), :]
    for send, offset in zip(sends, order):
        there = here ^ offset
        send[:part, :] = first_ref[spans(part, there), :].astype(BF16)
        send[part : 2 * part, :] = second_ref[spans(part, there), :].astype(BF16)


def list_kernel(plans, *refs):
    indices, lists = (refs[:3], refs[3:6]), refs[6:]
    slot_count = refs[0].shape[1]
    square = (slot_count, slot_count)
    down, along = (lax.broadcasted_iota(jnp.int32, square, k) for k in (0, 1))
    here = down == along

    def stand(row):
        return jnp.sum(jnp.where(here, jnp.broadcast_to(row, square), 0.0), axis=1, keepdims=True)

    def count(condition):
        return jnp.sum(jnp.where(condition, 1.0, 0.0), axis=1, keepdims=True)

    for list_ref, (way, groups) in zip(lists, plans):
        wide = lax.broadcasted_iota(jnp.int32, (slot_count, list_ref.shape[1]), 1).astype(F32)
        place = way.source_place()
        keys = []
        for index in indices:
            offset = (index[way.source][...] * way.size // way.part) ^ place
            bucket = jnp.zeros(offset.shape, F32)
            for at, group in enumerate(groups):
                for member in group:
                    bucket = jnp.where(offset == member, float(at), bucket)
            used = along[:1, :] < jnp.broadcast_to(index[2][...], (1, slot_count))
            bucket = jnp.where(used, bucket, float(len(groups)))
            keys.append((jnp.broadcast_to(bucket, square), stand(bucket)))
        rows = [jnp.zeros((1, list_ref.shape[1]), F32) for _ in range(4)]
        for k, index in enumerate(indices):
            (key, key_down), (other, _) = keys[k], keys[1 - k]
            place_down = count((key < key_down) | ((key == key_down) & (along < down)))
            place_down += count(other <= key_down) if k else count(other < key_down)
            source = index[way.source][...].astype(F32) + float(k * (way.halves - 1) * (way.length // way.size))
            target = index[1 - way.source][...].astype(F32) + float(k * way.target_shift)
            slot = (down[:, :1] + k * slot_count).astype(F32)
            found = place_down == wide
            for at, value in ((0, slot), (2, stand(source)), (3, stand(target))):
                rows[at] = rows[at] + jnp.sum(jnp.where(found, value, 0.0), axis=0, keepdims=True)
            rows[1] = rows[1] + jnp.sum(jnp.where(key_down < wide, 1.0, 0.0), axis=0, keepdims=True)
        for at, row in enumerate(rows):
            list_ref[at : at + 1, :] = row.astype(jnp.int32)


def step_kernel(way, pick, at_group, last, *refs):
    (tile_ref, list_ref), refs = refs[:2], refs[2:]
    chunks, refs = refs[: len(pick)], refs[len(pick) :]
    if at_group:
        folded, refs = refs[1][...], refs[2:]
    total_ref, refs = refs[0], refs[1:]
    here, there = way.source_place(), way.target_place()
    if not at_group:
        total_ref[...] = jnp.zeros_like(total_ref)
        folded = jnp.zeros((8, total_ref.shape[-1]), F32)
    plain_ref, turned_ref = refs[-2:]
    for chunk, offset in zip(chunks, pick):
        for half in range(way.halves):
            at = pl.ds(pl.multiple_of((here ^ offset) * way.part + half * way.length, way.part), way.part)
            folded += put_chunk(chunk[half * way.part : (half + 1) * way.part, :], plain_ref, turned_ref, at, way.sign)
    low, high = list_ref[1, at_group], list_ref[1, at_group + 1]
    width = LAST_WIDTH if last else WIDTH

    def turn_of(group, carry):
        for lane in range(width):
            at = low + group * width + lane
            target = jnp.where(at < high, list_ref[3, at], way.spare)
            span = spans(way.size, list_ref[2, at])
            right = jnp.concatenate([plain_ref[span, :], turned_ref[span, :]], axis=0)
            goal = spans(way.size, target)
            product = jnp.dot(way.weights(tile_ref, list_ref[0, at]), right, preferred_element_type=F32)
            total_ref[goal, :] = total_ref[goal, :] + product
        return carry

    lax.fori_loop(0, (high - low + width - 1) // width, turn_of, 0)
    if not last:
        refs[0][...] = folded
        return
    own_ref, norm_ref, sends = refs[0], refs[1], refs[2 : 2 + len(way.send_order)]
    norm = rows_of_norm(folded)
    norm_ref[...] = norm
    tail = norm_tail(norm)
    part = way.target_part
    for j, begin in enumerate(way.target_begins):
        def piece(position):
            return total_ref[pl.ds(pl.multiple_of(position * part + begin, part), part), :]

        own_ref[j * part : (j + 1) * part, :] = piece(there)
        for send, offset in zip(sends, way.send_order):
            send[j * part : (j + 1) * part, :] = piece(there ^ offset).astype(BF16)
    for send in sends:
        send[len(way.target_begins) * part :, :] = tail


def summed(own_ref, others):
    value = own_ref[...]
    for other in others:
        value = value + other[: own_ref.shape[0], :].astype(F32)
    return value


def norm_sum(own_norm, others, size):
    norm = own_norm
    for other in others:
        norm = norm + norm_from(other[size:, :])
    return norm


def start_kernel(others, own_ref, *refs):
    gradient = summed(own_ref, refs[:others])
    refs[-2][...] = gradient
    refs[-1][...] = gradient.astype(BF16)


def image_kernel(others, later, last, own_ref, norm_ref, *refs):
    ins, refs = refs[:others], refs[others:]
    image = summed(own_ref, ins)
    gamma = norm_sum(norm_ref[...], ins, own_ref.shape[0])
    if later:
        before_ref, gamma_ref = refs[:2]
        beta = gamma / (gamma_ref[...] + EPSILON)
        image = image + beta[:1] * before_ref[...]
        refs = refs[2:]
        refs[2][...] = beta
    refs[0][...] = image.astype(BF16)
    refs[1][...] = gamma
    if not last:
        refs[-1][...] = image


def gradient_kernel(others, own_ref, norm_ref, *refs):
    ins, (before_ref, gamma_ref, narrow_ref, alpha_ref, *wide) = refs[:others], refs[others:]
    change = summed(own_ref, ins)
    alpha = gamma_ref[...] / (norm_sum(norm_ref[...], ins, own_ref.shape[0]) + EPSILON)
    gradient = before_ref[...] - alpha[:1] * change
    narrow_ref[...] = gradient.astype(BF16)
    alpha_ref[...] = alpha
    for wide_ref in wide:
        wide_ref[...] = gradient


def norm_kernel(*refs):
    folded = sum(fold_squares(chunk[...].astype(F32)) for chunk in refs[:-1])
    refs[-1][...] = rows_of_norm(folded)


def answer_kernel(hyd_axis, core_axis, g_order, image_order, record_ref, gamma_ref, *refs):
    norms = len(g_order)
    norm = refs[0][...]
    for other in refs[1:norms]:
        norm = norm + other[...]
    refs = refs[norms:]
    alphas = [ref[...] for ref in refs[: ITERS - 1]] + [gamma_ref[...] / (norm + EPSILON)]
    refs = refs[ITERS - 1 :]
    betas = [ref[...] for ref in refs[: ITERS - 1]]
    refs = refs[ITERS - 1 :]
    g_count, image_count = ITERS * len(g_order), ITERS * len(image_order)
    g_chunks, images, (own_x, pair_x, wide_r, narrow_r) = refs[:g_count], refs[g_count : g_count + image_count], refs[g_count + image_count :]
    weights = [None] * ITERS
    weights[-1] = alphas[-1]
    for k in range(ITERS - 2, -1, -1):
        weights[k] = alphas[k] + betas[k] * weights[k + 1]
    core = lax.rem(lax.axis_index(core_axis), 2)
    here = lax.axis_index(hyd_axis)
    for at, offset in enumerate(g_order):
        mine = g_chunks[at :: len(g_order)]
        part = mine[0].shape[0] // 2
        span = spans(part, here ^ offset)
        own_x[span, :] = sum(w[:1] * g[:part, :].astype(F32) for w, g in zip(weights, mine))
        pair_x[span, :] = sum(w[:1] * g[part:, :].astype(F32) for w, g in zip(weights, mine)).astype(BF16)
    here = lax.axis_index(core_axis) // 2
    for at, offset in enumerate(image_order):
        mine = images[at :: len(image_order)]
        span = spans(mine[0].shape[0], here ^ offset)
        residual = packed_record(core, record_ref[0, span, :], record_ref[1, span, :])
        for alpha, image in zip(alphas, mine):
            residual = residual - alpha[:1] * image[...].astype(F32)
        wide_r[span, :] = residual
        narrow_r[span, :] = residual.astype(BF16)


def unpack_kernel(core_axis, own_x, own_r, pair_x, pair_r, x_hbm, r_hbm, x_ref, r_ref, sems):
    core = lax.rem(lax.axis_index(core_axis), 2)
    copies = []
    for k, (own, pair, out, target) in enumerate(((own_x, pair_x, x_ref, x_hbm), (own_r, pair_r, r_ref, r_hbm))):
        piece = own.shape[0] // sems.shape[1]
        for j in range(sems.shape[1]):
            span = pl.ds(j * piece, piece)
            mine, theirs = own[span, :], pair[span, :].astype(F32)
            first = jnp.where(core == 0, mine, theirs)
            second = jnp.where(core == 0, theirs, mine)
            low = low_half(mine.shape)
            out[0, span, :] = jnp.where(low, first, turn(second))
            out[1, span, :] = jnp.where(low, turn(first), second)
            copies.append(pltpu.make_async_copy(out.at[:, span, :], target.at[:, span, :], sems.at[k, j]))
            copies[-1].start()
    for copy in copies:
        copy.wait()


def solution(mesh):
    hyds, srcs = mesh.shape["hyd"], mesh.shape["src"]
    zs = srcs // 2

    def swap(value, axis, size, offset):
        return lax.ppermute(value, axis, [(i, i ^ offset) for i in range(size)])

    hyd_order = tuple(range(1, hyds))
    z_order = (zs - 1, *range(1, zs - 1))

    def over_hyd(values, order):
        return [swap(v, "hyd", hyds, o) for v, o in zip(values, order)]

    def over_z(values, order):
        return [swap(v, "src", srcs, 2 * o) for v, o in zip(values, order)]

    def groups_of(order, way):
        half = len(order) // 2
        return (order[:1], order[1:half], order[half:]) if way.part % way.size == 0 else (order,)

    def body(record, tile_data, tile_rows, tile_cols, tile_counts):
        own_tiles = tile_data[0, 0]
        slot_count, _, size, _ = own_tiles.shape
        rows, shots = record.shape[1:]
        cols = 2 * SRC_DEV
        row_tiles, col_tiles = rows // size, cols // size
        row_part, col_part = rows // zs, cols // hyds
        norm = ((8, shots), F32)
        row_sends = [((row_part + TAIL, shots), BF16)] * (zs - 1)
        col_sends = [((2 * col_part + TAIL, shots), BF16)] * (hyds - 1)
        col_total = ((cols + size, shots), F32)
        vector = lambda n, dtype: ((n, shots), dtype)

        pair_tiles = swap(own_tiles, "src", srcs, 1)
        index = (tile_rows[0], tile_cols[0], jnp.broadcast_to(tile_counts, tile_rows.shape[1:]))
        pair_index = tuple(swap(v, "src", srcs, 1) for v in index)
        pieces, groups = 4, slot_count // GROUP
        table = [(v.shape, jnp.int32) for v in index]
        joined = [((2 * slot_count, 2, size, size), BF16), ((2 * slot_count, size, 2 * size), BF16)]
        both_tiles, both_turned, total, plain, turned = call(
            functools.partial(pack_kernel, "src", col_tiles), "pack",
            [*joined, col_total, vector(rows, BF16), vector(rows, BF16)],
            [(record.shape, F32)] + table[:2] + [(n, pltpu.SemaphoreType.DMA) for n in (pieces, groups, 2)],
            record, own_tiles, *index, away=4,
        )
        both_tiles, both_turned, own, *sends = call(
            functools.partial(first_adjoint_kernel, "hyd", hyd_order, col_tiles), "first_adjoint",
            [*joined, vector(2 * col_part, F32)] + [vector(2 * col_part, BF16)] * (hyds - 1),
            [col_total] + table + [(len(table), pltpu.SemaphoreType.DMA), (1, pltpu.SemaphoreType.DMA)],
            pair_tiles, *(pltpu.with_memory_space_constraint(v, pltpu.VMEM) for v in pair_index),
            both_tiles, both_turned, total, plain, turned, vector=True, alias={4: 0, 5: 1},
        )
        gradient, narrow = call(
            functools.partial(start_kernel, hyds - 1), "start",
            [vector(2 * col_part, F32), vector(2 * col_part, BF16)], [],
            own, *over_hyd(sends, hyd_order),
        )

        hyd_place = lambda: lax.axis_index("hyd")
        z_place = lambda: lax.axis_index("src") // 2
        flat = lambda tile_ref, slot: jnp.concatenate([tile_ref[slot, 0], tile_ref[slot, 1]], axis=1)
        forward = Way(1, 1.0, size, col_part, 2, cols, row_part, (0,), 0, row_tiles, z_order, hyd_place, z_place, flat)
        adjoint = Way(
            0, -1.0, size, row_part, 1, rows, col_part, (0, cols), col_tiles, 2 * col_tiles, hyd_order,
            z_place, hyd_place, lambda tile_ref, slot: tile_ref[slot],
        )
        g_order, image_order = (0, *hyd_order), (0, *z_order)
        g_groups, image_groups = (groups_of(order, w) for order, w in ((g_order, forward), (image_order, adjoint)))
        lists = call(
            functools.partial(list_kernel, ((forward, g_groups), (adjoint, image_groups))),
            "lists", [((8, 128), jnp.int32)] * 2, [], *index, *pair_index, vector=True,
        )

        def apply(way, name, tiles, slot_list, chunks, groups, outs):
            total = (((len(way.target_begins) * (way.spare // len(way.target_begins)) + 1) * size, shots), F32)
            carry, at = [], 0
            for k, group in enumerate(groups):
                last = k + 1 == len(groups)
                carry = call(
                    functools.partial(step_kernel, way, group, k, last), name,
                    [total] + (outs if last else [norm]), [vector(way.halves * way.length, BF16)] * 2,
                    tiles, slot_list, *chunks[at : at + len(group)], *carry,
                    alias={2 + len(group): 0} if k else None,
                )
                at += len(group)
            return carry[1:]

        alphas, betas, g_chunks, images = [], [], [], []
        image = gamma = None
        for step in range(ITERS):
            last = step + 1 == ITERS
            chunks = [narrow, *over_hyd([narrow] * (hyds - 1), g_order[1:])]
            g_chunks += chunks
            own, own_norm, *sends = apply(
                forward, "forward", both_tiles, lists[0], chunks, g_groups, [vector(row_part, F32), norm] + row_sends
            )
            narrow, gamma, *more = call(
                functools.partial(image_kernel, zs - 1, step > 0, last), "image",
                [vector(row_part, BF16), norm] + [norm] * (step > 0) + [vector(row_part, F32)] * (not last), [],
                own, own_norm, *over_z(sends, z_order), *([image, gamma] if step else []),
            )
            image = None if last else more.pop()
            betas += more
            chunks = [narrow, *over_z([narrow] * (zs - 1), image_order[1:])]
            images += chunks
            if last:
                break
            own, own_norm, *sends = apply(
                adjoint, "adjoint", both_turned, lists[1], chunks, image_groups, [vector(2 * col_part, F32), norm] + col_sends
            )
            more_steps = step + 2 < ITERS
            narrow, alpha, *wide = call(
                functools.partial(gradient_kernel, hyds - 1), "gradient",
                [vector(2 * col_part, BF16), norm] + [vector(2 * col_part, F32)] * more_steps, [],
                own, own_norm, *over_hyd(sends, hyd_order), gradient, gamma,
            )
            gradient = wide[0] if more_steps else None
            alphas.append(alpha)

        (own_norm,) = call(norm_kernel, "norm", [norm], [], *chunks)
        norms = [own_norm] + over_hyd([own_norm] * (hyds - 1), hyd_order)
        own_x, pair_x, wide_r, narrow_r = call(
            functools.partial(answer_kernel, "hyd", "src", g_order, image_order), "answer",
            [vector(cols, F32), vector(cols, BF16), vector(rows, F32), vector(rows, BF16)], [],
            record, gamma, *norms, *alphas, *betas, *g_chunks, *images,
        )
        return call(
            functools.partial(unpack_kernel, "src"), "unpack",
            [((2, cols, shots), F32), ((2, rows, shots), F32)],
            [((2, cols, shots), F32), ((2, rows, shots), F32), ((2, 4), pltpu.SemaphoreType.DMA)],
            own_x, wide_r, swap(pair_x, "src", srcs, 1), swap(narrow_r, "src", srcs, 1), out_space=pltpu.HBM,
        )

    in_specs = (
        P(None, "hyd", None),
        P("hyd", "src", None, None, None, None),
        P("hyd", "src", None),
        P("hyd", "src", None),
        P("hyd", "src"),
    )
    out_specs = (P(None, "src", None), P(None, "hyd", None))
    return jax.shard_map(body, mesh=mesh, in_specs=in_specs, out_specs=out_specs, check_vma=False)
```

```python
import functools
from typing import NamedTuple

import jax
import jax.numpy as jnp
from jax import lax
from jax.experimental import pallas as pl
from jax.experimental.pallas import tpu as pltpu
from jax.sharding import PartitionSpec as P

SRC_DEV = 512
ITERS = 3
EPSILON = 1e-06
GROUP = 8
WIDTH = 12
LAST_WIDTH = 12
TAIL = 16
VMEM_BYTES = 16 << 20

F32 = jnp.float32
BF16 = jnp.bfloat16


class Way(NamedTuple):
    source: int
    sign: float
    size: int
    part: int
    halves: int
    length: int
    target_part: int
    target_begins: tuple
    target_shift: int
    spare: int
    send_order: tuple
    source_place: object
    target_place: object
    weights: object


def call(kernel, name, outs, scratch, *ins, vector=False, alias=None, away=0, out_space=pltpu.VMEM):
    def space(place, dtype):
        if place < away:
            return pltpu.HBM
        return pltpu.SMEM if dtype == jnp.int32 and not vector else pltpu.VMEM

    def room(shape, dtype):
        if dtype is pltpu.SemaphoreType.DMA:
            return dtype(shape if isinstance(shape, tuple) else (shape,))
        return (pltpu.SMEM if dtype == jnp.int32 else pltpu.VMEM)(shape, dtype)

    return pl.pallas_call(
        kernel,
        name=name,
        out_shape=[jax.ShapeDtypeStruct(s, d) for s, d in outs],
        in_specs=[pl.BlockSpec(memory_space=space(i, a.dtype)) for i, a in enumerate(ins)],
        out_specs=[pl.BlockSpec(memory_space=out_space) for _ in outs],
        scratch_shapes=[room(s, d) for s, d in scratch],
        input_output_aliases=alias or {},
        compiler_params=pltpu.CompilerParams(vmem_limit_bytes=VMEM_BYTES),
    )(*[pltpu.with_memory_space_constraint(a, pltpu.HBM) if i < away else a for i, a in enumerate(ins)])


def low_half(shape):
    return lax.broadcasted_iota(jnp.int32, shape, len(shape) - 1) < shape[-1] // 2


def turn(value):
    return pltpu.roll(value, value.shape[-1] // 2, value.ndim - 1)


def times_i(value, sign):
    rolled = turn(value)
    return jnp.where(low_half(value.shape), -sign * rolled, sign * rolled)


def both_parts(row):
    return row + turn(row)


def fold_squares(value):
    return jnp.sum((value * value).reshape(-1, 8, value.shape[-1]), axis=0)


def rows_of_norm(folded):
    row = both_parts(jnp.sum(folded, axis=0, keepdims=True))
    return jnp.broadcast_to(row, (8, folded.shape[-1]))


def norm_tail(norm):
    row = jnp.broadcast_to(norm[:1], (TAIL, norm.shape[-1]))
    high = row.astype(BF16).astype(F32)
    at = lax.broadcasted_iota(jnp.int32, row.shape, 0)
    return jnp.where(at == 0, high, jnp.where(at == 1, row - high, 0.0)).astype(BF16)


def norm_from(tail):
    tail = tail.astype(F32)
    return jnp.broadcast_to(tail[:1] + tail[1:2], (8, tail.shape[-1]))


def spans(size, count):
    return pl.ds(pl.multiple_of(count * size, size), size)


def group_of(index, group, step):
    for lane in range(GROUP):
        slot = group * GROUP + lane
        step(slot, slot < index[2][0], index[0][slot], index[1][slot])


def slots(index, step):
    def turn_of(group, carry):
        group_of(index, group, step)
        return carry

    lax.fori_loop(0, (index[2][0] + GROUP - 1) // GROUP, turn_of, 0)


def add_tile(acc_ref, weights, plain_ref, turned_ref, source, target):
    size = weights.shape[0]
    right = jnp.concatenate([plain_ref[spans(size, source), :], turned_ref[spans(size, source), :]], axis=0)
    at = spans(size, target)
    acc_ref[at, :] = acc_ref[at, :] + jnp.dot(weights, right, preferred_element_type=F32)


def put_chunk(chunk, plain_ref, turned_ref, at, sign):
    wide = chunk.astype(F32)
    plain_ref[at, :] = chunk
    turned_ref[at, :] = times_i(wide, sign).astype(BF16)
    return fold_squares(wide)


def packed_record(core, real, imag):
    first = jnp.where(core == 0, real, turn(real))
    second = jnp.where(core == 0, turn(imag), imag)
    return jnp.where(low_half(real.shape), first, second)


def pack_kernel(core_axis, tiles, record_hbm, tile_hbm, row_hbm, col_hbm, used_ref, *refs):
    tile_ref, turned_tile_ref, total_ref, plain_ref, turned_ref, record_ref, row_ref, col_ref, record_sem, tile_sem, index_sem = refs
    core = lax.rem(lax.axis_index(core_axis), 2)
    rows, slot_count = plain_ref.shape[0], tile_hbm.shape[0]
    pieces = record_sem.shape[0]
    piece, groups = rows // pieces, slot_count // GROUP

    def record_copy(k):
        span = pl.ds(k * piece, piece)
        return pltpu.make_async_copy(record_hbm.at[:, span, :], record_ref.at[:, span, :], record_sem.at[k])

    def tile_copy(k):
        span = pl.ds(k * GROUP, GROUP)
        return pltpu.make_async_copy(tile_hbm.at[span], tile_ref.at[span], tile_sem.at[k])

    index_copies = [
        pltpu.make_async_copy(source, target, index_sem.at[k])
        for k, (source, target) in enumerate(((row_hbm, row_ref), (col_hbm, col_ref)))
    ]
    for k in range(pieces):
        record_copy(k).start()
    for copy in index_copies:
        copy.start()
    for k in range(groups):
        tile_copy(k).start()
    total_ref[...] = jnp.zeros_like(total_ref)
    for k in range(pieces):
        record_copy(k).wait()
        span = pl.ds(k * piece, piece)
        packed = packed_record(core, record_ref[0, span, :], record_ref[1, span, :])
        put_chunk(packed.astype(BF16), plain_ref, turned_ref, span, -1.0)
    for copy in index_copies:
        copy.wait()
    step = turn_step(tiles, tile_ref, turned_tile_ref, 0, total_ref, plain_ref, turned_ref)
    for k in range(groups):
        tile_copy(k).wait()

        @pl.when(k * GROUP < used_ref[0, 0])
        def _():
            group_of((row_ref.at[0], col_ref.at[0], used_ref.at[0]), k, step)


def turn_step(tiles, tile_ref, turned_tile_ref, begin, total_ref, plain_ref, turned_ref):
    def step(slot, valid, row, col):
        weights = jnp.concatenate([tile_ref[slot, 0].T, tile_ref[slot, 1].T], axis=1)
        turned_tile_ref[begin + slot] = weights
        add_tile(total_ref, weights, plain_ref, turned_ref, row, jnp.where(valid, col, tiles))

    return step


def first_adjoint_kernel(hyd_axis, order, tiles, tile_ref, row_vmem, col_vmem, used_vmem, _, __, own_total_ref, plain_ref, turned_ref, *refs):
    tiles_ref, turned_tile_ref, own_ref, sends = refs[0], refs[1], refs[2], refs[3:-6]
    total_ref, *index, index_sem, tile_sem = refs[-6:]
    copies = [
        pltpu.make_async_copy(source, target, index_sem.at[k])
        for k, (source, target) in enumerate(zip((row_vmem, col_vmem, used_vmem), index))
    ]
    for copy in copies:
        copy.start()
    count = tile_ref.shape[0]
    join = pltpu.make_async_copy(tile_ref, tiles_ref.at[pl.ds(count, count)], tile_sem.at[0])
    join.start()
    total_ref[...] = jnp.zeros_like(total_ref)
    for copy in copies:
        copy.wait()
    slots([ref.at[0] for ref in index], turn_step(tiles, tile_ref, turned_tile_ref, count, total_ref, plain_ref, turned_ref))
    give_columns(hyd_axis, order, own_total_ref, total_ref, own_ref, sends)
    join.wait()


def give_columns(hyd_axis, order, first_ref, second_ref, own_ref, sends):
    here = lax.axis_index(hyd_axis)
    part = own_ref.shape[0] // 2
    own_ref[:part, :] = first_ref[spans(part, here), :]
    own_ref[part:, :] = second_ref[spans(part, here), :]
    for send, offset in zip(sends, order):
        there = here ^ offset
        send[:part, :] = first_ref[spans(part, there), :].astype(BF16)
        send[part : 2 * part, :] = second_ref[spans(part, there), :].astype(BF16)


def list_kernel(plans, *refs):
    indices, lists = (refs[:3], refs[3:6]), refs[6:]
    slot_count = refs[0].shape[1]
    square = (slot_count, slot_count)
    down, along = (lax.broadcasted_iota(jnp.int32, square, k) for k in (0, 1))
    here = down == along

    def stand(row):
        return jnp.sum(jnp.where(here, jnp.broadcast_to(row, square), 0.0), axis=1, keepdims=True)

    def count(condition):
        return jnp.sum(jnp.where(condition, 1.0, 0.0), axis=1, keepdims=True)

    for list_ref, (way, groups) in zip(lists, plans):
        wide = lax.broadcasted_iota(jnp.int32, (slot_count, list_ref.shape[1]), 1).astype(F32)
        place = way.source_place()
        keys = []
        for index in indices:
            offset = (index[way.source][...] * way.size // way.part) ^ place
            bucket = jnp.zeros(offset.shape, F32)
            for at, group in enumerate(groups):
                for member in group:
                    bucket = jnp.where(offset == member, float(at), bucket)
            used = along[:1, :] < jnp.broadcast_to(index[2][...], (1, slot_count))
            bucket = jnp.where(used, bucket, float(len(groups)))
            keys.append((jnp.broadcast_to(bucket, square), stand(bucket)))
        rows = [jnp.zeros((1, list_ref.shape[1]), F32) for _ in range(4)]
        for k, index in enumerate(indices):
            (key, key_down), (other, _) = keys[k], keys[1 - k]
            place_down = count((key < key_down) | ((key == key_down) & (along < down)))
            place_down += count(other <= key_down) if k else count(other < key_down)
            source = index[way.source][...].astype(F32) + float(k * (way.halves - 1) * (way.length // way.size))
            target = index[1 - way.source][...].astype(F32) + float(k * way.target_shift)
            slot = (down[:, :1] + k * slot_count).astype(F32)
            found = place_down == wide
            for at, value in ((0, slot), (2, stand(source)), (3, stand(target))):
                rows[at] = rows[at] + jnp.sum(jnp.where(found, value, 0.0), axis=0, keepdims=True)
            rows[1] = rows[1] + jnp.sum(jnp.where(key_down < wide, 1.0, 0.0), axis=0, keepdims=True)
        for at, row in enumerate(rows):
            list_ref[at : at + 1, :] = row.astype(jnp.int32)


def step_kernel(way, pick, at_group, last, *refs):
    (tile_ref, list_ref), refs = refs[:2], refs[2:]
    chunks, refs = refs[: len(pick)], refs[len(pick) :]
    if at_group:
        folded, refs = refs[1][...], refs[2:]
    total_ref, refs = refs[0], refs[1:]
    here, there = way.source_place(), way.target_place()
    if not at_group:
        total_ref[...] = jnp.zeros_like(total_ref)
        folded = jnp.zeros((8, total_ref.shape[-1]), F32)
    plain_ref, turned_ref = refs[-2:]
    for chunk, offset in zip(chunks, pick):
        for half in range(way.halves):
            at = pl.ds(pl.multiple_of((here ^ offset) * way.part + half * way.length, way.part), way.part)
            folded += put_chunk(chunk[half * way.part : (half + 1) * way.part, :], plain_ref, turned_ref, at, way.sign)
    low, high = list_ref[1, at_group], list_ref[1, at_group + 1]
    width = LAST_WIDTH if last else WIDTH

    def turn_of(group, carry):
        for lane in range(width):
            at = low + group * width + lane
            target = jnp.where(at < high, list_ref[3, at], way.spare)
            span = spans(way.size, list_ref[2, at])
            right = jnp.concatenate([plain_ref[span, :], turned_ref[span, :]], axis=0)
            goal = spans(way.size, target)
            product = jnp.dot(way.weights(tile_ref, list_ref[0, at]), right, preferred_element_type=F32)
            total_ref[goal, :] = total_ref[goal, :] + product
        return carry

    lax.fori_loop(0, (high - low + width - 1) // width, turn_of, 0)
    if not last:
        refs[0][...] = folded
        return
    own_ref, norm_ref, sends = refs[0], refs[1], refs[2 : 2 + len(way.send_order)]
    norm = rows_of_norm(folded)
    norm_ref[...] = norm
    tail = norm_tail(norm)
    part = way.target_part
    for j, begin in enumerate(way.target_begins):
        def piece(position):
            return total_ref[pl.ds(pl.multiple_of(position * part + begin, part), part), :]

        own_ref[j * part : (j + 1) * part, :] = piece(there)
        for send, offset in zip(sends, way.send_order):
            send[j * part : (j + 1) * part, :] = piece(there ^ offset).astype(BF16)
    for send in sends:
        send[len(way.target_begins) * part :, :] = tail


def summed(own_ref, others):
    value = own_ref[...]
    for other in others:
        value = value + other[: own_ref.shape[0], :].astype(F32)
    return value


def norm_sum(own_norm, others, size):
    norm = own_norm
    for other in others:
        norm = norm + norm_from(other[size:, :])
    return norm


def start_kernel(others, own_ref, *refs):
    gradient = summed(own_ref, refs[:others])
    refs[-2][...] = gradient
    refs[-1][...] = gradient.astype(BF16)


def image_kernel(others, later, last, own_ref, norm_ref, *refs):
    ins, refs = refs[:others], refs[others:]
    image = summed(own_ref, ins)
    gamma = norm_sum(norm_ref[...], ins, own_ref.shape[0])
    if later:
        before_ref, gamma_ref = refs[:2]
        beta = gamma / (gamma_ref[...] + EPSILON)
        image = image + beta[:1] * before_ref[...]
        refs = refs[2:]
        refs[2][...] = beta
    refs[0][...] = image.astype(BF16)
    refs[1][...] = gamma
    if not last:
        refs[-1][...] = image


def gradient_kernel(others, own_ref, norm_ref, *refs):
    ins, (before_ref, gamma_ref, narrow_ref, alpha_ref, *wide) = refs[:others], refs[others:]
    change = summed(own_ref, ins)
    alpha = gamma_ref[...] / (norm_sum(norm_ref[...], ins, own_ref.shape[0]) + EPSILON)
    gradient = before_ref[...] - alpha[:1] * change
    narrow_ref[...] = gradient.astype(BF16)
    alpha_ref[...] = alpha
    for wide_ref in wide:
        wide_ref[...] = gradient


def norm_kernel(*refs):
    folded = sum(fold_squares(chunk[...].astype(F32)) for chunk in refs[:-1])
    refs[-1][...] = rows_of_norm(folded)


def answer_kernel(hyd_axis, core_axis, g_order, image_order, record_ref, gamma_ref, *refs):
    norms = len(g_order)
    norm = refs[0][...]
    for other in refs[1:norms]:
        norm = norm + other[...]
    refs = refs[norms:]
    alphas = [ref[...] for ref in refs[: ITERS - 1]] + [gamma_ref[...] / (norm + EPSILON)]
    refs = refs[ITERS - 1 :]
    betas = [ref[...] for ref in refs[: ITERS - 1]]
    refs = refs[ITERS - 1 :]
    g_count, image_count = ITERS * len(g_order), ITERS * len(image_order)
    g_chunks, images, (own_x, pair_x, wide_r, narrow_r) = refs[:g_count], refs[g_count : g_count + image_count], refs[g_count + image_count :]
    weights = [None] * ITERS
    weights[-1] = alphas[-1]
    for k in range(ITERS - 2, -1, -1):
        weights[k] = alphas[k] + betas[k] * weights[k + 1]
    core = lax.rem(lax.axis_index(core_axis), 2)
    here = lax.axis_index(hyd_axis)
    for at, offset in enumerate(g_order):
        mine = g_chunks[at :: len(g_order)]
        part = mine[0].shape[0] // 2
        span = spans(part, here ^ offset)
        own_x[span, :] = sum(w[:1] * g[:part, :].astype(F32) for w, g in zip(weights, mine))
        pair_x[span, :] = sum(w[:1] * g[part:, :].astype(F32) for w, g in zip(weights, mine)).astype(BF16)
    here = lax.axis_index(core_axis) // 2
    for at, offset in enumerate(image_order):
        mine = images[at :: len(image_order)]
        span = spans(mine[0].shape[0], here ^ offset)
        residual = packed_record(core, record_ref[0, span, :], record_ref[1, span, :])
        for alpha, image in zip(alphas, mine):
            residual = residual - alpha[:1] * image[...].astype(F32)
        wide_r[span, :] = residual
        narrow_r[span, :] = residual.astype(BF16)


def unpack_kernel(core_axis, own_x, own_r, pair_x, pair_r, x_hbm, r_hbm, x_ref, r_ref, sems):
    core = lax.rem(lax.axis_index(core_axis), 2)
    copies = []
    for k, (own, pair, out, target) in enumerate(((own_x, pair_x, x_ref, x_hbm), (own_r, pair_r, r_ref, r_hbm))):
        piece = own.shape[0] // sems.shape[1]
        for j in range(sems.shape[1]):
            span = pl.ds(j * piece, piece)
            mine, theirs = own[span, :], pair[span, :].astype(F32)
            first = jnp.where(core == 0, mine, theirs)
            second = jnp.where(core == 0, theirs, mine)
            low = low_half(mine.shape)
            out[0, span, :] = jnp.where(low, first, turn(second))
            out[1, span, :] = jnp.where(low, turn(first), second)
            copies.append(pltpu.make_async_copy(out.at[:, span, :], target.at[:, span, :], sems.at[k, j]))
            copies[-1].start()
    for copy in copies:
        copy.wait()


def solution(mesh):
    hyds, srcs = mesh.shape["hyd"], mesh.shape["src"]
    zs = srcs // 2

    def swap(value, axis, size, offset):
        return lax.ppermute(value, axis, [(i, i ^ offset) for i in range(size)])

    hyd_order = tuple(range(1, hyds))
    z_order = (zs - 1, *range(1, zs - 1))

    def over_hyd(values, order):
        return [swap(v, "hyd", hyds, o) for v, o in zip(values, order)]

    def over_z(values, order):
        return [swap(v, "src", srcs, 2 * o) for v, o in zip(values, order)]

    def groups_of(order, way):
        half = len(order) // 2
        return (order[:1], order[1:half], order[half:]) if way.part % way.size == 0 else (order,)

    def body(record, tile_data, tile_rows, tile_cols, tile_counts):
        own_tiles = tile_data[0, 0]
        slot_count, _, size, _ = own_tiles.shape
        rows, shots = record.shape[1:]
        cols = 2 * SRC_DEV
        row_tiles, col_tiles = rows // size, cols // size
        row_part, col_part = rows // zs, cols // hyds
        norm = ((8, shots), F32)
        row_sends = [((row_part + TAIL, shots), BF16)] * (zs - 1)
        col_sends = [((2 * col_part + TAIL, shots), BF16)] * (hyds - 1)
        col_total = ((cols + size, shots), F32)
        vector = lambda n, dtype: ((n, shots), dtype)

        pair_tiles = swap(own_tiles, "src", srcs, 1)
        index = (tile_rows[0], tile_cols[0], jnp.broadcast_to(tile_counts, tile_rows.shape[1:]))
        pair_index = tuple(swap(v, "src", srcs, 1) for v in index)
        pieces, groups = 4, slot_count // GROUP
        table = [(v.shape, jnp.int32) for v in index]
        joined = [((2 * slot_count, 2, size, size), BF16), ((2 * slot_count, size, 2 * size), BF16)]
        both_tiles, both_turned, total, plain, turned = call(
            functools.partial(pack_kernel, "src", col_tiles), "pack",
            [*joined, col_total, vector(rows, BF16), vector(rows, BF16)],
            [(record.shape, F32)] + table[:2] + [(n, pltpu.SemaphoreType.DMA) for n in (pieces, groups, 2)],
            record, own_tiles, *index, away=4,
        )
        both_tiles, both_turned, own, *sends = call(
            functools.partial(first_adjoint_kernel, "hyd", hyd_order, col_tiles), "first_adjoint",
            [*joined, vector(2 * col_part, F32)] + [vector(2 * col_part, BF16)] * (hyds - 1),
            [col_total] + table + [(len(table), pltpu.SemaphoreType.DMA), (1, pltpu.SemaphoreType.DMA)],
            pair_tiles, *(pltpu.with_memory_space_constraint(v, pltpu.VMEM) for v in pair_index),
            both_tiles, both_turned, total, plain, turned, vector=True, alias={4: 0, 5: 1},
        )
        gradient, narrow = call(
            functools.partial(start_kernel, hyds - 1), "start",
            [vector(2 * col_part, F32), vector(2 * col_part, BF16)], [],
            own, *over_hyd(sends, hyd_order),
        )

        hyd_place = lambda: lax.axis_index("hyd")
        z_place = lambda: lax.axis_index("src") // 2
        flat = lambda tile_ref, slot: jnp.concatenate([tile_ref[slot, 0], tile_ref[slot, 1]], axis=1)
        forward = Way(1, 1.0, size, col_part, 2, cols, row_part, (0,), 0, row_tiles, z_order, hyd_place, z_place, flat)
        adjoint = Way(
            0, -1.0, size, row_part, 1, rows, col_part, (0, cols), col_tiles, 2 * col_tiles, hyd_order,
            z_place, hyd_place, lambda tile_ref, slot: tile_ref[slot],
        )
        g_order, image_order = (0, *hyd_order), (0, *z_order)
        g_groups, image_groups = (groups_of(order, w) for order, w in ((g_order, forward), (image_order, adjoint)))
        lists = call(
            functools.partial(list_kernel, ((forward, g_groups), (adjoint, image_groups))),
            "lists", [((8, 128), jnp.int32)] * 2, [], *index, *pair_index, vector=True,
        )

        def apply(way, name, tiles, slot_list, chunks, groups, outs):
            total = (((len(way.target_begins) * (way.spare // len(way.target_begins)) + 1) * size, shots), F32)
            carry, at = [], 0
            for k, group in enumerate(groups):
                last = k + 1 == len(groups)
                carry = call(
                    functools.partial(step_kernel, way, group, k, last), name,
                    [total] + (outs if last else [norm]), [vector(way.halves * way.length, BF16)] * 2,
                    tiles, slot_list, *chunks[at : at + len(group)], *carry,
                    alias={2 + len(group): 0} if k else None,
                )
                at += len(group)
            return carry[1:]

        alphas, betas, g_chunks, images = [], [], [], []
        image = gamma = None
        for step in range(ITERS):
            last = step + 1 == ITERS
            chunks = [narrow, *over_hyd([narrow] * (hyds - 1), g_order[1:])]
            g_chunks += chunks
            own, own_norm, *sends = apply(
                forward, "forward", both_tiles, lists[0], chunks, g_groups, [vector(row_part, F32), norm] + row_sends
            )
            narrow, gamma, *more = call(
                functools.partial(image_kernel, zs - 1, step > 0, last), "image",
                [vector(row_part, BF16), norm] + [norm] * (step > 0) + [vector(row_part, F32)] * (not last), [],
                own, own_norm, *over_z(sends, z_order), *([image, gamma] if step else []),
            )
            image = None if last else more.pop()
            betas += more
            chunks = [narrow, *over_z([narrow] * (zs - 1), image_order[1:])]
            images += chunks
            if last:
                break
            own, own_norm, *sends = apply(
                adjoint, "adjoint", both_turned, lists[1], chunks, image_groups, [vector(2 * col_part, F32), norm] + col_sends
            )
            more_steps = step + 2 < ITERS
            narrow, alpha, *wide = call(
                functools.partial(gradient_kernel, hyds - 1), "gradient",
                [vector(2 * col_part, BF16), norm] + [vector(2 * col_part, F32)] * more_steps, [],
                own, own_norm, *over_hyd(sends, hyd_order), gradient, gamma,
            )
            gradient = wide[0] if more_steps else None
            alphas.append(alpha)

        (own_norm,) = call(norm_kernel, "norm", [norm], [], *chunks)
        norms = [own_norm] + over_hyd([own_norm] * (hyds - 1), hyd_order)
        own_x, pair_x, wide_r, narrow_r = call(
            functools.partial(answer_kernel, "hyd", "src", g_order, image_order), "answer",
            [vector(cols, F32), vector(cols, BF16), vector(rows, F32), vector(rows, BF16)], [],
            record, gamma, *norms, *alphas, *betas, *g_chunks, *images,
        )
        return call(
            functools.partial(unpack_kernel, "src"), "unpack",
            [((2, cols, shots), F32), ((2, rows, shots), F32)],
            [((2, cols, shots), F32), ((2, rows, shots), F32), ((2, 4), pltpu.SemaphoreType.DMA)],
            own_x, wide_r, swap(pair_x, "src", srcs, 1), swap(narrow_r, "src", srcs, 1), out_space=pltpu.HBM,
        )

    in_specs = (
        P(None, "hyd", None),
        P("hyd", "src", None, None, None, None),
        P("hyd", "src", None),
        P("hyd", "src", None),
        P("hyd", "src"),
    )
    out_specs = (P(None, "src", None), P(None, "hyd", None))
    return jax.shard_map(body, mesh=mesh, in_specs=in_specs, out_specs=out_specs, check_vma=False)
```
